128 devices in a mesh: gx: 16 (over y, z), gy: 8 (over x, core).
Axes of the slice: x: 4, y: 4, z: 4, core: 2. Of those that a mesh axis runs over, the one named last changes fastest.
Arguments:
- block_list: int32 [256], P(('gx', 'gy')), may hold values from -1 to 255, as said below
- wet_levels: int32 [256, 1800], P(('gx', 'gy')), may hold values from 0 to 62, as said below
- mixing: float32 [256, 1800], P(('gx', 'gy')), may hold values from 0.5 to 2
- velocity: float32 [256, 2, 62, 1800], P(('gx', 'gy')), may hold values from -3 to 3
- tracers: float32 [256, 2, 62, 1800], P(('gx', 'gy')), may hold values from -6 to 6
- damping: float32 [320, 1440], P('gy', 'gx'), may hold values from 0.05 to 0.5
Outputs:
- new_tracers: float32 [256, 2, 62, 1800], P(('gx', 'gy'))
- surface_height: float32 [320, 1440], P('gy', 'gx')
The draws below stay inside these ranges and needn't reach their ends.
Inputs may be any that keep to these rules, and one draw needn't show every extreme that they name: `block_list`: slots form runs of 2 (run j holds slots j * 2 to j * 2 + 1). With q = j // 8 and r = j % 8, run j names distinct blocks r * 32 + q * 2 + s with 0 <= s < 2, in any order, and -1 in its remaining slots. Every run names one block or more, and the last run names all 2. Blocks that no run names are land. `wet_levels`: 0 in every slot whose block_list entry is -1; some column has 62 wet levels.
All inputs are finite; a program needn't handle non-finite values.
Results may differ from the reference program's by a relative error of at most 0.0003.
Values sent between devices are 32-bit elements; how exact they have to be, the bound alone decides.
No kernel may reach another device: no remote copies, remote signals or barrier semaphores. Data moves between devices by JAX's collectives and lax.ppermute only.
A program may use at most 128 MiB of HBM per device.

```python
import math
import jax
import jax.numpy as jnp
from jax import lax

BX = 45
BY = 40
WATER_COLUMNS = 1800
VERTICAL_LEVELS = 62
TRACER_COUNT = 2
DEVICE_SLOTS = 2
PASSES = 2
ITERS = 3
GBX = 32
NY = 320
NX = 1440
SLOT_TOTAL = 256


def layout(key):
    base_key = jax.random.fold_in(key, 4051)
    key_list = jax.random.split(base_key, 9)
    device_count = SLOT_TOTAL // DEVICE_SLOTS
    block_rows = NY // BY
    device_ids = jnp.arange(device_count, dtype=jnp.int32)
    live_counts = jax.random.randint(key_list[0], (device_count,), 1, DEVICE_SLOTS + 1)
    fullest = device_count - 1
    live_counts = jnp.where(device_ids == fullest, DEVICE_SLOTS, live_counts)
    scores = jax.random.randint(key_list[2], (device_count, DEVICE_SLOTS), 0, 1 << 20) * DEVICE_SLOTS + jnp.arange(DEVICE_SLOTS, dtype=jnp.int32)[None, :]
    ordering = jnp.argsort(scores, axis=1, stable=True).astype(jnp.int32)
    slot_ids = jnp.arange(DEVICE_SLOTS, dtype=jnp.int32)[None, :]
    present = slot_ids < live_counts[:, None]
    column_group = device_ids // block_rows
    row_group = device_ids % block_rows
    blocks = row_group[:, None] * GBX + column_group[:, None] * DEVICE_SLOTS + ordering
    block_listing = jnp.where(present, blocks, -1)
    depth_caps = jax.random.randint(key_list[3], (device_count,), VERTICAL_LEVELS // 4, VERTICAL_LEVELS + 1)
    deepest = jax.random.randint(key_list[4], (), 0, device_count)
    depth_caps = jnp.where(device_ids == deepest, VERTICAL_LEVELS, depth_caps)
    block_caps = 1 + jax.random.randint(key_list[5], (device_count, DEVICE_SLOTS), 0, 1 << 20) % depth_caps[:, None]
    block_caps = jnp.where(slot_ids == 0, depth_caps[:, None], block_caps)
    cell_ids = jnp.arange(WATER_COLUMNS, dtype=jnp.int32)[None, None, :]
    water_column_depth = 1 + jax.random.randint(key_list[6], (device_count, DEVICE_SLOTS, WATER_COLUMNS), 0, 1 << 20) % block_caps[:, :, None]
    deep_cell = jax.random.randint(key_list[7], (device_count, DEVICE_SLOTS, 1), 0, WATER_COLUMNS)
    dry_column = jax.random.randint(key_list[8], (device_count, DEVICE_SLOTS, WATER_COLUMNS), 0, 5) == 0
    water_column_depth = jnp.where(cell_ids == deep_cell, block_caps[:, :, None], jnp.where(dry_column, 0, water_column_depth))
    water_column_depth = jnp.where(present[:, :, None], water_column_depth, 0)
    return (block_listing.reshape(SLOT_TOTAL).astype(jnp.int32), water_column_depth.reshape(SLOT_TOTAL, WATER_COLUMNS).astype(jnp.int32))


def draw_block_list(key, part):
    return layout(key)[0]


def draw_wet_levels(key, part):
    return layout(key)[1]


def block_levels(rng, dims, cuts, low, high):
    def one(position, blocks):
        heights = jax.random.uniform(jax.random.fold_in(jax.random.fold_in(rng, 6), position), (blocks,), jnp.float32, low / len(cuts), high / len(cuts))
        return jnp.repeat(jnp.exp(heights), dims[position] // blocks).reshape((-1,) + (1,) * (len(dims) - position - 1))

    level = one(*cuts[0])
    for cut in cuts[1:]:
        level = level * one(*cut)
    return level


def scatter_about(rng, extent, deviation, reach, shards=(), kind=jnp.bfloat16):
    values = deviation * jax.random.normal(rng, extent, jnp.float32)
    if shards:
        values = values * block_levels(rng, extent, shards, -0.22, 0.18)
    return jnp.clip(values, -reach, reach).astype(kind)


def setup_inputs(seed: int = 0) -> dict:
    seeds = jax.random.split(jax.random.key(seed), 7)
    return {
        "block_list": draw_block_list(jax.random.fold_in(seeds[6], 71), 0),
        "wet_levels": draw_wet_levels(jax.random.fold_in(seeds[6], 71), 0),
        "mixing": jnp.clip(jnp.exp(math.log(2.0) - 1.3862944 * jax.random.uniform(seeds[2], (SLOT_TOTAL, WATER_COLUMNS), jnp.float32) ** block_levels(seeds[2], (SLOT_TOTAL, WATER_COLUMNS), ((0, 128),), -0.2, 0.2)), 0.5, 2.0),
        "velocity": scatter_about(seeds[3], (SLOT_TOTAL, 2, VERTICAL_LEVELS, WATER_COLUMNS), 0.5, 3.0, ((0, 128),), jnp.float32),
        "tracers": scatter_about(seeds[4], (SLOT_TOTAL, TRACER_COUNT, VERTICAL_LEVELS, WATER_COLUMNS), 1.0, 6.0, ((0, 128),), jnp.float32),
        "damping": jnp.clip(jnp.exp(math.log(0.5) - 2.3025851 * jax.random.uniform(seeds[5], (NY, NX), jnp.float32) ** block_levels(seeds[5], (NY, NX), ((0, 8), (1, 16)), -0.2, 0.2)), 0.05, 0.5),
    }


advect_rate = 0.25
mixing_rate = 0.015
salt_weight = 0.8
directions = ((0, 1), (0, -1), (1, 0), (-1, 0))

def window(values, shrink, step_y, step_x):
    height = values.shape[-2]
    breadth = values.shape[-1]
    return values[..., shrink + step_y:height - shrink + step_y, shrink + step_x:breadth - shrink + step_x]

def laplace(values, wetness, shrink):
    centre = window(values, shrink, 0, 0)
    wet_centre = window(wetness, shrink, 0, 0)
    pieces = [wet_centre * window(wetness, shrink, step_y, step_x) * (window(values, shrink, step_y, step_x) - centre) for step_y, step_x in directions]
    return pieces[0] + pieces[1] + pieces[2] + pieces[3]

def advect(values, wetness, eastward, northward):
    centre = window(values, 2, 0, 0)
    wet_centre = window(wetness, 2, 0, 0)

    def face_flux(speeds, step_y, step_x):
        face_speed = 0.5 * (window(speeds, 2, 0, 0) + window(speeds, 2, step_y, step_x))
        face_wet = wet_centre * window(wetness, 2, step_y, step_x)
        return face_wet * face_speed * (0.5 * (centre + window(values, 2, step_y, step_x)))
    return -(face_flux(eastward, 0, 1) - face_flux(eastward, 0, -1) + face_flux(northward, 1, 0) - face_flux(northward, -1, 0))

def tracer_pass(padded, wetness, eastward, northward, mixing):
    first_lap = laplace(padded, wetness, 1)
    scaled = window(mixing, 1, 0, 0) * first_lap
    biharmonic = -laplace(scaled, window(wetness, 1, 0, 0), 1)
    return window(padded, 2, 0, 0) + advect_rate * advect(padded, wetness, eastward, northward) + mixing_rate * biharmonic

def to_grid(slot_values, block_list):
    block_rows = NY // BY
    blocks = block_rows * GBX
    target = jnp.where(block_list >= 0, block_list, blocks).astype(jnp.int32)
    middle = slot_values.shape[1:-1]
    leading = len(middle)
    placed = jnp.zeros((blocks,) + middle + (WATER_COLUMNS,), slot_values.dtype).at[target].set(slot_values, mode='drop')
    placed = placed.reshape((block_rows, GBX) + middle + (BY, BX))
    axes_order = tuple(range(2, leading + 2)) + (0, leading + 2, 1, leading + 3)
    return placed.transpose(axes_order).reshape(middle + (NY, NX))

def from_grid(grid_values, block_list):
    block_rows = NY // BY
    middle = grid_values.shape[:-2]
    leading = len(middle)
    blocks = grid_values.reshape(middle + (block_rows, BY, GBX, BX))
    axes_order = (leading, leading + 2) + tuple(range(leading)) + (leading + 1, leading + 3)
    blocks = blocks.transpose(axes_order).reshape((block_rows * GBX,) + middle + (WATER_COLUMNS,))
    return blocks[jnp.maximum(block_list, 0).astype(jnp.int32)]

def pad_grid(values, margin):
    spacing = [(0, 0)] * (values.ndim - 2) + [(margin, margin), (0, 0)]
    padded_rows = jnp.pad(values, spacing)
    return jnp.concatenate([padded_rows[..., -margin:], padded_rows, padded_rows[..., :margin]], axis=-1)

def reference(block_list, wet_levels, mixing, velocity, tracers, damping):
    present = block_list >= 0
    depth_grid = to_grid(wet_levels.astype(jnp.float32), block_list)
    depth_pad = pad_grid(depth_grid, 2)
    mixing_pad = pad_grid(to_grid(mixing, block_list), 2)

    def level_step(forcing, level_index):
        level_tracers = lax.dynamic_index_in_dim(tracers, level_index, 2, keepdims=False)
        level_flow = lax.dynamic_index_in_dim(velocity, level_index, 2, keepdims=False)
        current = to_grid(level_tracers, block_list)
        flow_pad = pad_grid(to_grid(level_flow, block_list), 2)
        wetness = (level_index.astype(jnp.float32) < depth_pad).astype(jnp.float32)
        for pass_index in range(PASSES):
            current = tracer_pass(pad_grid(current, 2), wetness, flow_pad[0], flow_pad[1], mixing_pad)
        wet_inner = window(wetness, 2, 0, 0)
        forcing = forcing + wet_inner * (current[0] - salt_weight * current[1])
        return (forcing, from_grid(current, block_list))
    forcing, slot_levels = lax.scan(level_step, jnp.zeros((NY, NX), jnp.float32), jnp.arange(VERTICAL_LEVELS, dtype=jnp.int32))
    forcing = forcing / math.sqrt(VERTICAL_LEVELS)
    restored = jnp.transpose(slot_levels, (1, 2, 0, 3))
    new_tracers = jnp.where(present[:, None, None, None], restored, tracers)
    height_pad = pad_grid(depth_grid, 1)
    centre_depth = window(height_pad, 1, 0, 0)
    couplings = [jnp.minimum(centre_depth, window(height_pad, 1, step_y, step_x)) / VERTICAL_LEVELS for step_y, step_x in directions]
    diagonal = damping + (couplings[0] + couplings[1] + couplings[2] + couplings[3])

    def operate(values):
        padded = pad_grid(values, 1)
        beside = [couplings[number] * window(padded, 1, step_y, step_x) for number, (step_y, step_x) in enumerate(directions)]
        return diagonal * values - (beside[0] + beside[1] + beside[2] + beside[3])
    solution = jnp.zeros_like(forcing)
    residual = forcing
    direction = forcing
    norm_now = jnp.sum(residual * residual)
    for iteration in range(ITERS):
        applied = operate(direction)
        step_size = norm_now / jnp.sum(direction * applied)
        solution = solution + step_size * direction
        residual = residual - step_size * applied
        norm_next = jnp.sum(residual * residual)
        direction = residual + norm_next / norm_now * direction
        norm_now = norm_next
    return (new_tracers, solution)
```

```python
import math

import jax
import jax.numpy as jnp
from jax import lax
from jax.sharding import PartitionSpec as P

BX = 45
BY = 40
PASSES = 2
ITERS = 3


advect_rate = 0.25
mixing_rate = 0.015
salt_weight = 0.8
directions = ((0, 1), (0, -1), (1, 0), (-1, 0))


def with_halo(cells, sides, width):
    for axis, dim in sides:
        count = lax.axis_size(axis)
        head = lax.slice_in_dim(cells, 0, width, axis=dim)
        tail = lax.slice_in_dim(cells, cells.shape[dim] - width, cells.shape[dim], axis=dim)
        cells = jnp.concatenate(
            [
                lax.ppermute(tail, axis, [(i, (i + 1) % count) for i in range(count)]),
                cells,
                lax.ppermute(head, axis, [((i + 1) % count, i) for i in range(count)]),
            ],
            axis=dim,
        )
    return cells


def window(values, shrink, step_y, step_x):
    height = values.shape[-2]
    breadth = values.shape[-1]
    return values[
        ..., shrink + step_y : height - shrink + step_y, shrink + step_x : breadth - shrink + step_x
    ]


def laplace(values, wetness, shrink):
    centre = window(values, shrink, 0, 0)
    wet_centre = window(wetness, shrink, 0, 0)
    pieces = [
        wet_centre
        * window(wetness, shrink, step_y, step_x)
        * (window(values, shrink, step_y, step_x) - centre)
        for step_y, step_x in directions
    ]
    return pieces[0] + pieces[1] + pieces[2] + pieces[3]


def advect(values, wetness, eastward, northward):
    centre = window(values, 2, 0, 0)
    wet_centre = window(wetness, 2, 0, 0)

    def face_flux(speeds, step_y, step_x):
        face_speed = 0.5 * (window(speeds, 2, 0, 0) + window(speeds, 2, step_y, step_x))
        face_wet = wet_centre * window(wetness, 2, step_y, step_x)
        return face_wet * face_speed * (0.5 * (centre + window(values, 2, step_y, step_x)))

    return -(
        face_flux(eastward, 0, 1)
        - face_flux(eastward, 0, -1)
        + face_flux(northward, 1, 0)
        - face_flux(northward, -1, 0)
    )


def tracer_pass(padded, wetness, eastward, northward, mixing):
    first_lap = laplace(padded, wetness, 1)
    scaled = window(mixing, 1, 0, 0) * first_lap
    biharmonic = -laplace(scaled, window(wetness, 1, 0, 0), 1)
    return (
        window(padded, 2, 0, 0)
        + advect_rate * advect(padded, wetness, eastward, northward)
        + mixing_rate * biharmonic
    )


def to_strip(slot_values, selector):
    placed = jnp.einsum("ps,s...->p...", selector, slot_values, precision=lax.Precision.HIGHEST)
    slot_count = placed.shape[0]
    middle = placed.shape[1:-1]
    leading = len(middle)
    placed = placed.reshape((slot_count,) + middle + (BY, BX))
    axes_order = tuple(range(1, leading + 1)) + (leading + 1, 0, leading + 2)
    return placed.transpose(axes_order).reshape(middle + (BY, slot_count * BX))


def from_strip(strip_values, selector):
    slot_count = selector.shape[0]
    middle = strip_values.shape[:-2]
    leading = len(middle)
    blocks = strip_values.reshape(middle + (BY, slot_count, BX))
    axes_order = (leading + 1,) + tuple(range(leading)) + (leading, leading + 2)
    blocks = blocks.transpose(axes_order).reshape((slot_count,) + middle + (BY * BX,))
    return jnp.einsum("ps,p...->s...", selector, blocks, precision=lax.Precision.HIGHEST)


def quad_sum(values, axis, partner):
    count = lax.axis_size(axis)
    others = [
        lax.ppermute(values, axis, [(i, partner(i, turn)) for i in range(count)])
        for turn in range(1, 4)
    ]
    return (values + others[0]) + (others[1] + others[2])


def total_over_devices(values):
    values = values + lax.ppermute(values, "gy", [(i, i ^ 1) for i in range(lax.axis_size("gy"))])
    values = quad_sum(values, "gy", lambda i, turn: i ^ (2 * turn))
    values = quad_sum(values, "gx", lambda i, turn: i ^ turn)
    return quad_sum(values, "gx", lambda i, turn: i ^ (4 * turn))


def krylov_weights(moments):
    m = [moments[k] for k in range(6)]
    low10 = m[2] / m[1]
    low20 = m[3] / m[1]
    pivot1 = m[3] - low10 * m[2]
    part21 = m[4] - low20 * m[2]
    low21 = part21 / pivot1
    pivot2 = m[5] - low20 * m[3] - low21 * part21
    y1 = m[1] - low10 * m[0]
    y2 = m[2] - low20 * m[0] - low21 * y1
    z2 = y2 / pivot2
    z1 = y1 / pivot1 - low21 * z2
    z0 = m[0] / m[1] - low10 * z1 - low20 * z2
    return z0, z1, z2


def per_device(block_list, wet_levels, mixing, velocity, tracers, damping):
    slot_count = block_list.shape[0]
    level_numbers = tracers.shape[2]
    present = block_list >= 0
    position = jnp.where(present, block_list % slot_count, -1)
    selector = (position[None, :] == jnp.arange(slot_count, dtype=jnp.int32)[:, None]).astype(
        jnp.float32
    )
    margin = 2
    flow_strip = to_strip(velocity, selector)
    flow_strip = flow_strip.reshape((2 * level_numbers,) + flow_strip.shape[2:])
    depth_strip = to_strip(wet_levels.astype(jnp.float32), selector)
    mixing_strip = to_strip(mixing, selector)
    static = jnp.concatenate([flow_strip, depth_strip[None], mixing_strip[None]], axis=0)
    padded_static = with_halo(static, (("gx", 2), ("gy", 1)), margin)
    row_index = lax.broadcasted_iota(jnp.int32, padded_static.shape[1:], 0)
    row_total = padded_static.shape[1]
    row_owner = lax.axis_index("gy")
    outside = (row_owner == 0) & (row_index < margin) | (row_owner == lax.axis_size("gy") - 1) & (
        row_index >= row_total - margin
    )
    depth_pad = jnp.where(outside, 0.0, padded_static[-2])
    mixing_pad = padded_static[-1]
    east_pad = padded_static[:level_numbers]
    north_pad = padded_static[level_numbers : 2 * level_numbers]
    current = to_strip(tracers, selector)
    for pass_index in range(PASSES):
        padded = with_halo(current, (("gx", 3), ("gy", 2)), margin)
        eastward = window(east_pad, 0, 0, 0)
        northward = window(north_pad, 0, 0, 0)
        depth_now = window(depth_pad, 0, 0, 0)
        mixing_now = window(mixing_pad, 0, 0, 0)
        advance_level_ids = lax.broadcasted_iota(jnp.int32, (level_numbers, 1, 1), 0)
        wetness = (advance_level_ids.astype(jnp.float32) < depth_now[None]).astype(jnp.float32)
        current = tracer_pass(padded, wetness, eastward, northward, mixing_now)
    inner_depth = window(depth_pad, margin, 0, 0)
    level_ids = lax.broadcasted_iota(jnp.int32, (level_numbers, 1, 1), 0)
    wet_inner = (level_ids.astype(jnp.float32) < inner_depth[None]).astype(jnp.float32)
    forcing = jnp.sum(wet_inner * (current[0] - salt_weight * current[1]), axis=0) / math.sqrt(
        level_numbers
    )
    reach = 3
    surface = with_halo(
        jnp.stack([forcing, inner_depth, damping]), (("gx", 2), ("gy", 1)), reach
    )
    surface_row = lax.broadcasted_iota(jnp.int32, surface.shape[1:], 0)
    beyond = (row_owner == 0) & (surface_row < reach) | (row_owner == lax.axis_size("gy") - 1) & (
        surface_row >= surface.shape[1] - reach
    )
    depth_wide = jnp.where(beyond, 0.0, surface[1])

    def operate(values, cut):
        depth_cut = window(depth_wide, cut, 0, 0)
        damping_inner = window(surface[2], cut + 1, 0, 0)
        centre = window(values, 1, 0, 0)
        centre_depth = window(depth_cut, 1, 0, 0)
        total = damping_inner * centre
        for step_y, step_x in directions:
            coupling = jnp.minimum(centre_depth, window(depth_cut, 1, step_y, step_x)) / level_numbers
            total = total + coupling * (centre - window(values, 1, step_y, step_x))
        return total

    first = operate(surface[0], 0)
    second = operate(first, 1)
    third = operate(second, 2)
    basis = [forcing, window(first, 2, 0, 0), window(second, 1, 0, 0), third]
    moments = jnp.stack(
        [jnp.sum(basis[k // 2] * basis[(k + 1) // 2]) for k in range(6)]
    )
    moments = total_over_devices(moments)
    weights = krylov_weights(moments)
    solution = weights[0] * basis[0] + weights[1] * basis[1] + weights[2] * basis[2]
    restored = from_strip(current, selector)
    new_tracers = jnp.where(present[:, None, None, None], restored, tracers)
    return (new_tracers, solution)


def solution(mesh):
    return jax.shard_map(
        per_device,
        mesh=mesh,
        in_specs=(
            P(("gx", "gy")),
            P(("gx", "gy"), None),
            P(("gx", "gy"), None),
            P(("gx", "gy"), None, None, None),
            P(("gx", "gy"), None, None, None),
            P("gy", "gx"),
        ),
        out_specs=(P(("gx", "gy"), None, None, None), P("gy", "gx")),
        check_vma=False,
    )
```

```python
import functools
import math

import jax
import jax.numpy as jnp
from jax import lax
from jax.experimental import pallas as pl
from jax.experimental.pallas import tpu as pltpu
from jax.sharding import PartitionSpec as P

BX = 45
BY = 40
CELLS = BX * BY
LEVELS = 62
LANES = 128
TILES = 8
REACH = 7
ROWS = BY + 2 * REACH
BASE = 8
WIDE = 2 * BX
NS = 21
EW = 13
SURFACE = 56

advect_rate = 0.25
mixing_rate = 0.015
salt_weight = 0.8


def lane_ids():
    return lax.broadcasted_iota(jnp.int32, (8, LANES), 1)


def merge(parts, lane):
    flat = []
    for low, width, value in parts:
        low %= LANES
        if low + width > LANES:
            flat.append((low, value))
            flat.append((0, value))
        else:
            flat.append((low, value))
    flat.sort(key=lambda part: part[0])
    result = flat[0][1]
    last = result
    for low, value in flat[1:]:
        if value is last:
            continue
        result = jnp.where(lane >= low, value, result)
        last = value
    return result


def turn(value, shift):
    shift %= LANES
    return pltpu.roll(value, shift, 1) if shift else value


class Source:
    def __init__(self, own, up=None, down=None, west=None, east=None):
        self.load = {"own": own, "up": up, "down": down, "west": west, "east": east}
        self.kept = {}

    def tile(self, kind, position, number):
        key = (kind, position, number)
        if kind in ("west", "east"):
            key = (kind, 0, number)
        elif kind == "up" and number == 14:
            key = (kind, position, 11)
        if key not in self.kept:
            self.kept[key] = self.fetch(*key)
        return self.kept[key]

    def fetch(self, kind, position, number):
        load = self.load[kind]
        if kind == "own":
            return load(position, number)
        if kind in ("west", "east"):
            return load(number)
        shift = 120 if kind == "up" else 8
        first = 12 if kind == "up" else 0
        if first <= number <= first + 1:
            return turn(load(1 + 2 * position + number - first), shift)
        return turn(load(0), shift + 64 * position)

    def cells(self, position, start, width):
        parts = []
        at = start
        while at < start + width:
            if at < 0:
                number = (at + CELLS) // LANES
                end = min(start + width, 0, (number + 1) * LANES - CELLS)
                value = self.tile("up", position, number)
            elif at < CELLS:
                number = at // LANES
                end = min(start + width, CELLS, (number + 1) * LANES)
                value = self.tile("own", position, number)
            else:
                number = (at - CELLS) // LANES
                end = min(start + width, (number + 1) * LANES + CELLS)
                value = self.tile("down", position, number)
            parts.append((at, end - at, value))
            at = end
        return parts


def west_edge(row):
    if row == 45:
        return 2, 0, 1
    if -6 <= row <= 44:
        return (row + 6) // 17, 0, REACH
    return None


def east_edge(row):
    if row == -6:
        return 0, 6, 1
    if -5 <= row <= 45:
        return (row + 5) // 17, 0, REACH
    return None


def pack_columns(source, lane):
    east, west = [], []
    for group in range(3):
        parts = []
        for row in range(-6, 46):
            number, first, count = east_edge(row)
            if number == group:
                parts += source.cells(1, BX * row + BX - REACH + first, count)
        east.append(merge(parts, lane))
        parts = []
        for row in range(-6, 46):
            number, first, count = west_edge(row)
            if number == group:
                parts += source.cells(0, BX * row + first, count)
        west.append(merge(parts, lane))
    return east, west


def strip_rows(source, lane):
    turned = {}

    def combined(r):
        if r in turned:
            return turned[r]
        parts = []
        if east_edge(r - 1):
            number, first, count = east_edge(r - 1)
            value = source.tile("west", 0, number)
            parts.append((BX * r - REACH + first, count, value))
        if -REACH <= r < BY + REACH:
            parts += source.cells(0, BX * r, BX)
        if -REACH <= r + 1 < BY + REACH:
            parts += source.cells(1, BX * (r + 1), BX)
        if west_edge(r + 2):
            number, first, count = west_edge(r + 2)
            value = source.tile("east", 0, number)
            parts.append((BX * (r + 2) + first, count, value))
        turned[r] = turn(merge(parts, lane), BASE - BX * r)
        return turned[r]

    for row in range(-REACH, BY + REACH):
        value = combined(row)
        if east_edge(row):
            value = jnp.where(lane < BASE, combined(row + 1), value)
        value = jnp.where(lane < BASE + BX, value, combined(row - 1))
        if west_edge(row):
            value = jnp.where(lane < BASE + WIDE, value, combined(row - 2))
        yield row, value


def slot_swap(block_list):
    first = block_list[0]
    return jnp.where(first >= 0, first & 1, 1 - (block_list[1] & 1))


def field_loader(ref, which, swap):
    def load(position, number):
        slot = swap if position == 0 else 1 - swap
        if number < 14:
            return ref[slot, which, :, number * LANES : (number + 1) * LANES]
        return turn(ref[slot, which, :, CELLS - LANES : CELLS], CELLS % LANES)

    return load


def column_loader(wet_levels, mixing, swap):
    def load(position, number):
        slot = swap if position == 0 else 1 - swap
        low = number * LANES if number < 14 else CELLS - LANES
        both = wet_levels[:, low : low + LANES].astype(jnp.float32)
        depth = jnp.where(slot == 0, both[0:1, :], both[1:2, :])
        both = mixing[:, low : low + LANES]
        mix = jnp.where(slot == 0, both[0:1, :], both[1:2, :])
        sublane = lax.broadcasted_iota(jnp.int32, (8, LANES), 0)
        value = jnp.where(
            sublane == 0, jnp.broadcast_to(depth, (8, LANES)), jnp.broadcast_to(mix, (8, LANES))
        )
        return value if number < 14 else turn(value, CELLS % LANES)

    return load


def pack_rows(load, lane):
    ends = [jnp.where(lane < 8, load(p, 14), load(p, 11)) for p in range(2)]
    mixed = jnp.where((lane >= 13) & (lane < 72), turn(ends[1], 64), ends[0])
    up = [mixed, load(0, 12), load(0, 13), load(1, 12), load(1, 13)]
    mixed = jnp.where(lane < 64, load(0, 2), turn(load(1, 2), 64))
    down = [mixed, load(0, 0), load(0, 1), load(1, 0), load(1, 1)]
    return up, down


def rows_kernel(block_list, wet_levels, mixing, damping, velocity, tracers, up, down, padded):
    lane = lane_ids()
    swap = slot_swap(block_list)
    step = pl.program_id(0)
    for field in range(4):
        load = field_loader(tracers if field < 2 else velocity, field % 2, swap)
        ups, downs = pack_rows(load, lane)
        for number in range(5):
            up[0, 5 * field + number] = ups[number]
            down[0, 5 * field + number] = downs[number]

    @pl.when(step == 0)
    def _():
        padded[...] = jnp.zeros_like(padded)
        padded[:, 0:WIDE] = damping[...]

    load = column_loader(wet_levels, mixing, swap)
    for number in range(5):

        @pl.when(step == number)
        def _():
            ups, downs = pack_rows(load, lane)
            up[0, NS - 1] = ups[number]
            down[0, NS - 1] = downs[number]

    @pl.when(step >= 5)
    def _():
        up[0, NS - 1] = padded[BY - 8 : BY, :]
        down[0, NS - 1] = padded[0:8, :]


def columns_kernel(
    block_list, wet_levels, mixing, damping, velocity, tracers, up, down, up_extra, down_extra,
    east, west, padded,
):
    lane = lane_ids()
    swap = slot_swap(block_list)
    step = pl.program_id(0)
    for field in range(4):
        source = Source(
            field_loader(tracers if field < 2 else velocity, field % 2, swap),
            lambda number, field=field: up[0, 5 * field + number],
            lambda number, field=field: down[0, 5 * field + number],
        )
        easts, wests = pack_columns(source, lane)
        for number in range(3):
            east[0, 3 * field + number] = easts[number]
            west[0, 3 * field + number] = wests[number]

    @pl.when(step == 0)
    def _():
        padded[...] = jnp.zeros_like(padded)
        padded[:, 0:WIDE] = damping[...]

    for number in range(3):

        @pl.when(step == number)
        def _():
            source = Source(
                column_loader(wet_levels, mixing, swap),
                lambda tile: up_extra[tile, 0],
                lambda tile: down_extra[tile, 0],
            )
            easts, wests = pack_columns(source, lane)
            east[0, EW - 1] = easts[number]
            west[0, EW - 1] = wests[number]

    @pl.when(step >= 3)
    def _():
        tiles = [up_extra[5, 0]]
        tiles += [padded[8 * j : 8 * j + 8, :] for j in range(5)]
        tiles += [down_extra[5, 0]]
        east[0, EW - 1] = merge([(2 * j, 2, turn(t, 2 * j - WIDE + 2)) for j, t in enumerate(tiles)], lane)
        west[0, EW - 1] = merge([(2 * j, 2, turn(t, 2 * j)) for j, t in enumerate(tiles)], lane)


def advance(fields, read, write, low, high, levels, shared, lane):
    depth_east, depth_north, mix = shared
    zero = jnp.zeros((8, LANES), jnp.float32)
    row0 = low - 1
    now = [read(n, row0) for n in range(2)]
    below = [read(n, row0 - 1) for n in range(2)]
    wet_north = levels < depth_north[row0 - 1 + REACH]
    drop = [jnp.where(wet_north, now[n] - below[n], zero) for n in range(2)]
    scaled = [None, None]
    flow = [None, None]
    held = [None, None]
    gone = None
    for row in range(row0, high + 2):
        at = row + REACH
        wet_east = levels < depth_east[at]
        wet_north = levels < depth_north[at]
        mixing = mix[at]
        above = [read(n, row + 1) for n in range(2)]
        fresh = []
        kept = []
        for n in range(2):
            beside = turn(now[n], LANES - 1)
            step_east = jnp.where(wet_east, beside - now[n], zero)
            rise = jnp.where(wet_north, above[n] - now[n], zero)
            lap = (step_east - turn(step_east, 1)) + (rise - drop[n])
            fresh.append(mixing * lap)
            drop[n] = rise
            kept.append(beside + now[n])
        if row > row0:
            old_east, old_north, old_row = gone
            flow_east = fields[2, old_row + REACH]
            flow_east = flow_east + turn(flow_east, LANES - 1)
            flow_north = fields[3, old_row + REACH] + fields[3, at]
            for n in range(2):
                beside = turn(scaled[n], LANES - 1)
                east = jnp.where(old_east, flow_east * held[n] + (beside - scaled[n]), zero)
                north = jnp.where(
                    old_north, flow_north * (below[n] + now[n]) + (fresh[n] - scaled[n]), zero
                )
                if old_row >= low:
                    out = below[n] - ((east - turn(east, 1)) + (north - flow[n]))
                    write(n, old_row, out)
                flow[n] = north
        gone = (wet_east, wet_north, row)
        scaled = fresh
        held = kept
        below = now
        now = above


def surface_operator(values, couple_east, couple_north, damping):
    east = couple_east * (values - turn(values, LANES - 1))
    north = couple_north * (values - pltpu.roll(values, SURFACE - 1, 0))
    return damping * values + ((east - turn(east, 1)) + (north - pltpu.roll(north, 1, 0)))


def main_kernel(
    block_list, wet_levels, mixing, damping, velocity, tracers,
    up, down, from_west, from_east, up_extra, down_extra, west_extra, east_extra,
    new_tracers, basis, moments,
    fields, halfway, depth, depth_east, depth_north, mix, forcing, surface, depths, dampings,
):
    lane = lane_ids()
    swap = slot_swap(block_list)
    step = pl.program_id(0)

    @pl.when(step == 0)
    def _():
        source = Source(
            column_loader(wet_levels, mixing, swap),
            lambda tile: up_extra[tile, 0],
            lambda tile: down_extra[tile, 0],
            lambda tile: west_extra[tile, 0],
            lambda tile: east_extra[tile, 0],
        )
        depths[...] = jnp.zeros_like(depths)
        last = None
        for row, value in strip_rows(source, lane):
            here = jnp.broadcast_to(value[0:1, :], (8, LANES))
            depth[row + REACH] = here
            depth_east[row + REACH] = jnp.minimum(here, turn(here, LANES - 1))
            mix[row + REACH] = mixing_rate * jnp.broadcast_to(value[1:2, :], (8, LANES))
            depths[row + 8 : row + 9, :] = value[0:1, :]
            if last is not None:
                depth_north[row + REACH - 1] = jnp.minimum(here, last)
            last = here
        forcing[...] = jnp.zeros_like(forcing)

    for field in range(4):
        source = Source(
            field_loader(tracers if field < 2 else velocity, field % 2, swap),
            lambda number, field=field: up[0, 5 * field + number],
            lambda number, field=field: down[0, 5 * field + number],
            lambda number, field=field: from_west[0, 3 * field + number],
            lambda number, field=field: from_east[0, 3 * field + number],
        )
        for row, value in strip_rows(source, lane):
            fields[field, row + REACH] = value if field < 2 else (0.25 * advect_rate) * value

    levels = (lax.broadcasted_iota(jnp.int32, (8, LANES), 0) + 8 * step).astype(jnp.float32)
    shared = (depth_east, depth_north, mix)

    def read_first(n, row):
        return fields[n, row + REACH]

    def write_first(n, row, value):
        halfway[n, row + REACH] = value

    advance(fields, read_first, write_first, -5, 44, levels, shared, lane)

    def read_second(n, row):
        return halfway[n, row + REACH]

    def write_second(n, row, value):
        fields[n, row + REACH] = value

    advance(fields, read_second, write_second, -3, 42, levels, shared, lane)

    for row in range(-3, 43):
        at = row + REACH
        part = fields[0, at] - salt_weight * fields[1, at]
        forcing[at] += jnp.where(levels < depth[at], part, 0.0)

    for n in range(2):
        turned = {}

        def back(r, n=n, turned=turned):
            if r not in turned:
                value = jnp.where(lane < BASE + BX, fields[n, r + REACH], fields[n, r + 1 + REACH])
                turned[r] = turn(value, BX * r - BASE)
            return turned[r]

        for number in range(15):
            for position in range(2):
                slot = swap if position == 0 else 1 - swap
                first, end = number * LANES, min((number + 1) * LANES, CELLS)
                parts = []
                for row in range(first // BX, (end - 1) // BX + 1):
                    low = max(row * BX, first)
                    parts.append((low, min((row + 1) * BX, end) - low, back(row - position)))
                value = merge(parts, lane)
                new_tracers[slot, n, :, first:end] = value[:, 0 : end - first]

    @pl.when(step == TILES - 1)
    def _():
        surface[...] = jnp.zeros_like(surface)
        for row in range(-3, 43):
            total = jnp.sum(forcing[row + REACH], axis=0, keepdims=True)
            surface[row + 8 : row + 9, :] = total * (1.0 / math.sqrt(LEVELS))
        dampings[...] = jnp.zeros_like(dampings)
        dampings[8 : 8 + BY, 0:WIDE] = damping[...]
        dampings[0:8, :] = up_extra[5, 0]
        dampings[8 + BY : 16 + BY, :] = down_extra[5, 0]
        for j in range(7):
            value = turn(dampings[8 * j : 8 * j + 8, :], BASE)
            value = jnp.where(lane < BASE, turn(west_extra[3, 0], BASE - 2 - 2 * j), value)
            value = jnp.where(lane < BASE + WIDE, value, turn(east_extra[3, 0], BASE + WIDE - 2 * j))
            dampings[8 * j : 8 * j + 8, :] = value
        here = depths[...]
        couple_east = jnp.minimum(here, turn(here, LANES - 1)) * (1.0 / LEVELS)
        couple_north = jnp.minimum(here, pltpu.roll(here, SURFACE - 1, 0)) * (1.0 / LEVELS)
        diagonal = dampings[...]
        powers = [surface[...]]
        for _ in range(3):
            powers.append(surface_operator(powers[-1], couple_east, couple_north, diagonal))
        row_id = lax.broadcasted_iota(jnp.int32, (SURFACE, LANES), 0)
        lane_id = lax.broadcasted_iota(jnp.int32, (SURFACE, LANES), 1)
        own = (row_id >= 8) & (row_id < 8 + BY) & (lane_id >= BASE) & (lane_id < BASE + WIDE)
        moments[...] = jnp.zeros_like(moments)
        for k in range(6):
            product = jnp.where(own, powers[k // 2] * powers[(k + 1) // 2], 0.0)
            moments[k : k + 1, :] = jnp.sum(product, axis=0, keepdims=True)
        for k in range(3):
            basis[k] = turn(powers[k], LANES - BASE)[8 : 8 + BY, :]


def finish_kernel(moments, basis, out):
    totals = jnp.sum(moments[...], axis=1, keepdims=True)
    m = [totals[k : k + 1, :] for k in range(6)]
    low10 = m[2] / m[1]
    low20 = m[3] / m[1]
    pivot1 = m[3] - low10 * m[2]
    part21 = m[4] - low20 * m[2]
    low21 = part21 / pivot1
    pivot2 = m[5] - low20 * m[3] - low21 * part21
    y1 = m[1] - low10 * m[0]
    y2 = m[2] - low20 * m[0] - low21 * y1
    z2 = y2 / pivot2
    z1 = y1 / pivot1 - low21 * z2
    z0 = m[0] / m[1] - low10 * z1 - low20 * z2
    value = z0 * basis[0] + z1 * basis[1] + z2 * basis[2]
    out[...] = value[:, 0:WIDE]


def quad_sum(values, axis, partner):
    count = lax.axis_size(axis)
    others = [
        lax.ppermute(values, axis, [(i, partner(i, turn)) for i in range(count)])
        for turn in range(1, 4)
    ]
    return (values + others[0]) + (others[1] + others[2])


def total_over_devices(values):
    values = values + lax.ppermute(values, "gy", [(i, i ^ 1) for i in range(lax.axis_size("gy"))])
    values = quad_sum(values, "gy", lambda i, turn: i ^ (2 * turn))
    values = quad_sum(values, "gx", lambda i, turn: i ^ turn)
    return quad_sum(values, "gx", lambda i, turn: i ^ (4 * turn))


def whole(shape):
    return pl.BlockSpec(shape, lambda k: (0,) * len(shape))


def per_device(block_list, wet_levels, mixing, velocity, tracers, damping):
    f32 = jnp.float32
    slots, fields_each, levels, cells = tracers.shape
    params = pltpu.CompilerParams(
        dimension_semantics=("arbitrary",), vmem_limit_bytes=40 * 1024 * 1024
    )
    level_block = pl.BlockSpec((slots, fields_each, 8, cells), lambda k: (0, 0, k, 0))
    rows_block = pl.BlockSpec((1, NS, 8, LANES), lambda k: (k, 0, 0, 0))
    columns_block = pl.BlockSpec((1, EW, 8, LANES), lambda k: (k, 0, 0, 0))
    rows_extra = pl.BlockSpec((TILES, 1, 8, LANES), lambda k: (0, NS - 1, 0, 0))
    columns_extra = pl.BlockSpec((TILES, 1, 8, LANES), lambda k: (0, EW - 1, 0, 0))
    own_specs = [
        pl.BlockSpec(memory_space=pltpu.SMEM),
        whole(wet_levels.shape),
        whole(mixing.shape),
        whole(damping.shape),
        level_block,
        level_block,
    ]
    own = (block_list, wet_levels, mixing, damping, velocity, tracers)
    rows_type = jax.ShapeDtypeStruct((TILES, NS, 8, LANES), f32)
    columns_type = jax.ShapeDtypeStruct((TILES, EW, 8, LANES), f32)

    up, down = pl.pallas_call(
        rows_kernel,
        grid=(TILES,),
        in_specs=own_specs,
        out_specs=[rows_block, rows_block],
        out_shape=[rows_type, rows_type],
        scratch_shapes=[pltpu.VMEM((BY, LANES), f32)],
        compiler_params=params,
        name="pack_rows",
    )(*own)
    rows_total = lax.axis_size("gy")
    up = lax.ppermute(up, "gy", [(i, i + 1) for i in range(rows_total - 1)])
    down = lax.ppermute(down, "gy", [(i + 1, i) for i in range(rows_total - 1)])

    east, west = pl.pallas_call(
        columns_kernel,
        grid=(TILES,),
        in_specs=own_specs + [rows_block, rows_block, rows_extra, rows_extra],
        out_specs=[columns_block, columns_block],
        out_shape=[columns_type, columns_type],
        scratch_shapes=[pltpu.VMEM((BY, LANES), f32)],
        compiler_params=params,
        name="pack_columns",
    )(*own, up, down, up, down)
    columns_total = lax.axis_size("gx")
    from_west = lax.ppermute(east, "gx", [(i, (i + 1) % columns_total) for i in range(columns_total)])
    from_east = lax.ppermute(west, "gx", [((i + 1) % columns_total, i) for i in range(columns_total)])

    row_store = pltpu.VMEM((ROWS, 8, LANES), f32)
    new_tracers, basis, moments = pl.pallas_call(
        main_kernel,
        grid=(TILES,),
        in_specs=own_specs
        + [rows_block, rows_block, columns_block, columns_block]
        + [rows_extra, rows_extra, columns_extra, columns_extra],
        out_specs=[level_block, whole((3, BY, LANES)), whole((8, LANES))],
        out_shape=[
            jax.ShapeDtypeStruct(tracers.shape, f32),
            jax.ShapeDtypeStruct((3, BY, LANES), f32),
            jax.ShapeDtypeStruct((8, LANES), f32),
        ],
        scratch_shapes=[
            pltpu.VMEM((4, ROWS, 8, LANES), f32),
            pltpu.VMEM((2, ROWS, 8, LANES), f32),
            row_store,
            row_store,
            row_store,
            row_store,
            row_store,
            pltpu.VMEM((SURFACE, LANES), f32),
            pltpu.VMEM((SURFACE, LANES), f32),
            pltpu.VMEM((SURFACE, LANES), f32),
        ],
        compiler_params=params,
        name="advance",
    )(*own, up, down, from_west, from_east, up, down, from_west, from_east)

    moments = total_over_devices(moments)
    height = pl.pallas_call(
        finish_kernel,
        out_shape=jax.ShapeDtypeStruct((BY, WIDE), f32),
        name="finish",
    )(moments, basis)
    return (new_tracers, height)


def solution(mesh):
    return jax.shard_map(
        per_device,
        mesh=mesh,
        in_specs=(
            P(("gx", "gy")),
            P(("gx", "gy"), None),
            P(("gx", "gy"), None),
            P(("gx", "gy"), None, None, None),
            P(("gx", "gy"), None, None, None),
            P("gy", "gx"),
        ),
        out_specs=(P(("gx", "gy"), None, None, None), P("gy", "gx")),
        check_vma=False,
    )
```

```python
import functools
import math

import jax
import jax.numpy as jnp
from jax import lax
from jax.experimental import pallas as pl
from jax.experimental.pallas import tpu as pltpu
from jax.sharding import PartitionSpec as P

BX = 45
BY = 40
CELLS = BX * BY
LEVELS = 62
LANES = 128
TILES = 8
REACH = 7
ROWS = BY + 2 * REACH
AHEAD = 26
BASE = 8
WIDE = 2 * BX
NS = 21
EW = 13
SURFACE = 56

advect_rate = 0.25
mixing_rate = 0.015
salt_weight = 0.8


def lane_ids():
    return lax.broadcasted_iota(jnp.int32, (8, LANES), 1)


def merge(parts, lane):
    flat = []
    for low, width, value in parts:
        low %= LANES
        if low + width > LANES:
            flat.append((low, value))
            flat.append((0, value))
        else:
            flat.append((low, value))
    flat.sort(key=lambda part: part[0])
    result = flat[0][1]
    last = result
    for low, value in flat[1:]:
        if value is last:
            continue
        result = jnp.where(lane >= low, value, result)
        last = value
    return result


def turn(value, shift):
    shift %= LANES
    return pltpu.roll(value, shift, 1) if shift else value


class Source:
    def __init__(self, own, up=None, down=None, west=None, east=None):
        self.load = {"own": own, "up": up, "down": down, "west": west, "east": east}
        self.kept = {}

    def tile(self, kind, position, number):
        key = (kind, position, number)
        if kind in ("west", "east"):
            key = (kind, 0, number)
        elif kind == "up" and number == 14:
            key = (kind, position, 11)
        if key not in self.kept:
            self.kept[key] = self.fetch(*key)
        return self.kept[key]

    def fetch(self, kind, position, number):
        load = self.load[kind]
        if kind == "own":
            return load(position, number)
        if kind in ("west", "east"):
            return load(number)
        shift = 120 if kind == "up" else 8
        first = 12 if kind == "up" else 0
        if first <= number <= first + 1:
            return turn(load(1 + 2 * position + number - first), shift)
        return turn(load(0), shift + 64 * position)

    def cells(self, position, start, width):
        parts = []
        at = start
        while at < start + width:
            if at < 0:
                number = (at + CELLS) // LANES
                end = min(start + width, 0, (number + 1) * LANES - CELLS)
                value = self.tile("up", position, number)
            elif at < CELLS:
                number = at // LANES
                end = min(start + width, CELLS, (number + 1) * LANES)
                value = self.tile("own", position, number)
            else:
                number = (at - CELLS) // LANES
                end = min(start + width, (number + 1) * LANES + CELLS)
                value = self.tile("down", position, number)
            parts.append((at, end - at, value))
            at = end
        return parts


def west_edge(row):
    if row == 45:
        return 2, 0, 1
    if -6 <= row <= 44:
        return (row + 6) // 17, 0, REACH
    return None


def east_edge(row):
    if row == -6:
        return 0, 6, 1
    if -5 <= row <= 45:
        return (row + 5) // 17, 0, REACH
    return None


def pack_columns(source, lane):
    east, west = [], []
    for group in range(3):
        parts = []
        for row in range(-6, 46):
            number, first, count = east_edge(row)
            if number == group:
                parts += source.cells(1, BX * row + BX - REACH + first, count)
        east.append(merge(parts, lane))
        parts = []
        for row in range(-6, 46):
            number, first, count = west_edge(row)
            if number == group:
                parts += source.cells(0, BX * row + first, count)
        west.append(merge(parts, lane))
    return east, west


def strip_rows(source, lane):
    turned = {}

    def combined(r):
        if r in turned:
            return turned[r]
        parts = []
        if east_edge(r - 1):
            number, first, count = east_edge(r - 1)
            value = source.tile("west", 0, number)
            parts.append((BX * r - REACH + first, count, value))
        if -REACH <= r < BY + REACH:
            parts += source.cells(0, BX * r, BX)
        if -REACH <= r + 1 < BY + REACH:
            parts += source.cells(1, BX * (r + 1), BX)
        if west_edge(r + 2):
            number, first, count = west_edge(r + 2)
            value = source.tile("east", 0, number)
            parts.append((BX * (r + 2) + first, count, value))
        turned[r] = turn(merge(parts, lane), BASE - BX * r)
        return turned[r]

    for row in range(-REACH, BY + REACH):
        value = combined(row)
        if east_edge(row):
            value = jnp.where(lane < BASE, combined(row + 1), value)
        value = jnp.where(lane < BASE + BX, value, combined(row - 1))
        if west_edge(row):
            value = jnp.where(lane < BASE + WIDE, value, combined(row - 2))
        yield row, value


def slot_swap(block_list):
    first = block_list[0]
    return jnp.where(first >= 0, first & 1, 1 - (block_list[1] & 1))


def field_loader(ref, which, swap):
    def load(position, number):
        slot = swap if position == 0 else 1 - swap
        if number < 14:
            return ref[slot, which, :, number * LANES : (number + 1) * LANES]
        return turn(ref[slot, which, :, CELLS - LANES : CELLS], CELLS % LANES)

    return load


def column_loader(wet_levels, mixing, swap):
    def load(position, number):
        slot = swap if position == 0 else 1 - swap
        low = number * LANES if number < 14 else CELLS - LANES
        both = wet_levels[:, low : low + LANES].astype(jnp.float32)
        depth = jnp.where(slot == 0, both[0:1, :], both[1:2, :])
        both = mixing[:, low : low + LANES]
        mix = jnp.where(slot == 0, both[0:1, :], both[1:2, :])
        sublane = lax.broadcasted_iota(jnp.int32, (8, LANES), 0)
        value = jnp.where(
            sublane == 0, jnp.broadcast_to(depth, (8, LANES)), jnp.broadcast_to(mix, (8, LANES))
        )
        return value if number < 14 else turn(value, CELLS % LANES)

    return load


def pack_rows(load, lane):
    ends = [jnp.where(lane < 8, load(p, 14), load(p, 11)) for p in range(2)]
    mixed = jnp.where((lane >= 13) & (lane < 72), turn(ends[1], 64), ends[0])
    up = [mixed, load(0, 12), load(0, 13), load(1, 12), load(1, 13)]
    mixed = jnp.where(lane < 64, load(0, 2), turn(load(1, 2), 64))
    down = [mixed, load(0, 0), load(0, 1), load(1, 0), load(1, 1)]
    return up, down


def rows_kernel(block_list, wet_levels, mixing, damping, velocity, tracers, up, down, padded):
    lane = lane_ids()
    swap = slot_swap(block_list)
    step = pl.program_id(0)
    for field in range(4):
        load = field_loader(tracers if field < 2 else velocity, field % 2, swap)
        ups, downs = pack_rows(load, lane)
        for number in range(5):
            up[0, 5 * field + number] = ups[number]
            down[0, 5 * field + number] = downs[number]

    @pl.when(step == 0)
    def _():
        padded[...] = jnp.zeros_like(padded)
        padded[:, 0:WIDE] = damping[...]

    load = column_loader(wet_levels, mixing, swap)
    for number in range(5):

        @pl.when(step == number)
        def _():
            ups, downs = pack_rows(load, lane)
            up[0, NS - 1] = ups[number]
            down[0, NS - 1] = downs[number]

    @pl.when(step >= 5)
    def _():
        up[0, NS - 1] = padded[BY - 8 : BY, :]
        down[0, NS - 1] = padded[0:8, :]


def columns_kernel(
    block_list, wet_levels, mixing, damping, velocity, tracers, up, down, up_extra, down_extra,
    east, west, padded,
):
    lane = lane_ids()
    swap = slot_swap(block_list)
    step = pl.program_id(0)
    for field in range(4):
        source = Source(
            field_loader(tracers if field < 2 else velocity, field % 2, swap),
            lambda number, field=field: up[0, 5 * field + number],
            lambda number, field=field: down[0, 5 * field + number],
        )
        easts, wests = pack_columns(source, lane)
        for number in range(3):
            east[0, 3 * field + number] = easts[number]
            west[0, 3 * field + number] = wests[number]

    @pl.when(step == 0)
    def _():
        padded[...] = jnp.zeros_like(padded)
        padded[:, 0:WIDE] = damping[...]

    for number in range(3):

        @pl.when(step == number)
        def _():
            source = Source(
                column_loader(wet_levels, mixing, swap),
                lambda tile: up_extra[tile, 0],
                lambda tile: down_extra[tile, 0],
            )
            easts, wests = pack_columns(source, lane)
            east[0, EW - 1] = easts[number]
            west[0, EW - 1] = wests[number]

    @pl.when(step >= 3)
    def _():
        tiles = [up_extra[5, 0]]
        tiles += [padded[8 * j : 8 * j + 8, :] for j in range(5)]
        tiles += [down_extra[5, 0]]
        east[0, EW - 1] = merge([(2 * j, 2, turn(t, 2 * j - WIDE + 2)) for j, t in enumerate(tiles)], lane)
        west[0, EW - 1] = merge([(2 * j, 2, turn(t, 2 * j)) for j, t in enumerate(tiles)], lane)


def staggered(low, high, phases):
    state = {}
    rows = range(low, high + 1)
    for time in range(low, high + 1 + AHEAD * (len(phases) - 1)):
        for number in reversed(range(len(phases))):
            row = time - number * AHEAD
            if row in rows:
                phases[number](row + REACH, state)


def advance(values, fields, out, low, high, levels, shared, scratch):
    depth_east, depth_north, mix = shared
    scaled, held = scratch

    def rise(n, at):
        return jnp.where(levels < depth_north[at], values[n, at + 1] - values[n, at], 0.0)

    def look_east(at, state):
        for n in range(2):
            state[n, at] = turn(values[n, at], LANES - 1)

    def step_east(at, state):
        wet = levels < depth_east[at]
        for n in range(2):
            here, beside = values[n, at], state[n, at]
            step = jnp.where(wet, beside - here, 0.0)
            state[n, at] = step, turn(step, 1)
            held[n, at] = beside + here

    def scale(at, state):
        for n in range(2):
            step, back = state.pop((n, at))
            drop = state.pop(n) if n in state else rise(n, at - 1)
            state[n] = rise(n, at)
            scaled[n, at] = mix[at] * ((step - back) + (state[n] - drop))

    staggered(low - 1, high + 1, (look_east, step_east, scale))

    def north_flow(n, at):
        flow = fields[3, at] + fields[3, at + 1]
        step = scaled[n, at + 1] - scaled[n, at]
        both = flow * (values[n, at] + values[n, at + 1]) + step
        return jnp.where(levels < depth_north[at], both, 0.0)

    def look_east_again(at, state):
        flow = fields[2, at]
        state["flow", at] = turn(flow, LANES - 1)
        for n in range(2):
            state[n, at] = turn(scaled[n, at], LANES - 1)

    def east_flow(at, state):
        wet = levels < depth_east[at]
        flow = fields[2, at] + state.pop(("flow", at))
        for n in range(2):
            both = flow * held[n, at] + (state[n, at] - scaled[n, at])
            both = jnp.where(wet, both, 0.0)
            state[n, at] = both, turn(both, 1)

    def change(at, state):
        for n in range(2):
            east, back = state.pop((n, at))
            south = state.pop(n) if n in state else north_flow(n, at - 1)
            state[n] = north_flow(n, at)
            out[n, at] = values[n, at] - ((east - back) + (state[n] - south))

    staggered(low, high, (look_east_again, east_flow, change))


def surface_operator(values, couple_east, couple_north, damping):
    east = couple_east * (values - turn(values, LANES - 1))
    north = couple_north * (values - pltpu.roll(values, SURFACE - 1, 0))
    return damping * values + ((east - turn(east, 1)) + (north - pltpu.roll(north, 1, 0)))


def main_kernel(
    block_list, wet_levels, mixing, damping, velocity, tracers,
    up, down, from_west, from_east, up_extra, down_extra, west_extra, east_extra,
    new_tracers, basis, moments,
    fields, halfway, scaled, held, depth, depth_east, depth_north, mix, forcing, surface, depths, dampings,
):
    lane = lane_ids()
    swap = slot_swap(block_list)
    step = pl.program_id(0)

    @pl.when(step == 0)
    def _():
        source = Source(
            column_loader(wet_levels, mixing, swap),
            lambda tile: up_extra[tile, 0],
            lambda tile: down_extra[tile, 0],
            lambda tile: west_extra[tile, 0],
            lambda tile: east_extra[tile, 0],
        )
        depths[...] = jnp.zeros_like(depths)
        last = None
        for row, value in strip_rows(source, lane):
            here = jnp.broadcast_to(value[0:1, :], (8, LANES))
            depth[row + REACH] = here
            depth_east[row + REACH] = jnp.minimum(here, turn(here, LANES - 1))
            mix[row + REACH] = mixing_rate * jnp.broadcast_to(value[1:2, :], (8, LANES))
            depths[row + 8 : row + 9, :] = value[0:1, :]
            if last is not None:
                depth_north[row + REACH - 1] = jnp.minimum(here, last)
            last = here
        forcing[...] = jnp.zeros_like(forcing)

    for field in range(4):
        source = Source(
            field_loader(tracers if field < 2 else velocity, field % 2, swap),
            lambda number, field=field: up[0, 5 * field + number],
            lambda number, field=field: down[0, 5 * field + number],
            lambda number, field=field: from_west[0, 3 * field + number],
            lambda number, field=field: from_east[0, 3 * field + number],
        )
        for row, value in strip_rows(source, lane):
            fields[field, row + REACH] = value if field < 2 else (0.25 * advect_rate) * value

    levels = (lax.broadcasted_iota(jnp.int32, (8, LANES), 0) + 8 * step).astype(jnp.float32)
    shared = (depth_east, depth_north, mix)

    scratch = (scaled, held)
    advance(fields, fields, halfway, -5, 44, levels, shared, scratch)
    advance(halfway, fields, fields, -3, 42, levels, shared, scratch)

    for row in range(-3, 43):
        at = row + REACH
        part = fields[0, at] - salt_weight * fields[1, at]
        forcing[at] += jnp.where(levels < depth[at], part, 0.0)

    for n in range(2):
        turned = {}

        def back(r, n=n, turned=turned):
            if r not in turned:
                value = jnp.where(lane < BASE + BX, fields[n, r + REACH], fields[n, r + 1 + REACH])
                turned[r] = turn(value, BX * r - BASE)
            return turned[r]

        for number in range(15):
            for position in range(2):
                slot = swap if position == 0 else 1 - swap
                first, end = number * LANES, min((number + 1) * LANES, CELLS)
                parts = []
                for row in range(first // BX, (end - 1) // BX + 1):
                    low = max(row * BX, first)
                    parts.append((low, min((row + 1) * BX, end) - low, back(row - position)))
                value = merge(parts, lane)
                new_tracers[slot, n, :, first:end] = value[:, 0 : end - first]

    @pl.when(step == TILES - 1)
    def _():
        surface[...] = jnp.zeros_like(surface)
        for row in range(-3, 43):
            total = jnp.sum(forcing[row + REACH], axis=0, keepdims=True)
            surface[row + 8 : row + 9, :] = total * (1.0 / math.sqrt(LEVELS))
        dampings[...] = jnp.zeros_like(dampings)
        dampings[8 : 8 + BY, 0:WIDE] = damping[...]
        dampings[0:8, :] = up_extra[5, 0]
        dampings[8 + BY : 16 + BY, :] = down_extra[5, 0]
        for j in range(7):
            value = turn(dampings[8 * j : 8 * j + 8, :], BASE)
            value = jnp.where(lane < BASE, turn(west_extra[3, 0], BASE - 2 - 2 * j), value)
            value = jnp.where(lane < BASE + WIDE, value, turn(east_extra[3, 0], BASE + WIDE - 2 * j))
            dampings[8 * j : 8 * j + 8, :] = value
        here = depths[...]
        couple_east = jnp.minimum(here, turn(here, LANES - 1)) * (1.0 / LEVELS)
        couple_north = jnp.minimum(here, pltpu.roll(here, SURFACE - 1, 0)) * (1.0 / LEVELS)
        diagonal = dampings[...]
        powers = [surface[...]]
        for _ in range(3):
            powers.append(surface_operator(powers[-1], couple_east, couple_north, diagonal))
        row_id = lax.broadcasted_iota(jnp.int32, (SURFACE, LANES), 0)
        lane_id = lax.broadcasted_iota(jnp.int32, (SURFACE, LANES), 1)
        own = (row_id >= 8) & (row_id < 8 + BY) & (lane_id >= BASE) & (lane_id < BASE + WIDE)
        moments[...] = jnp.zeros_like(moments)
        for k in range(6):
            product = jnp.where(own, powers[k // 2] * powers[(k + 1) // 2], 0.0)
            moments[k : k + 1, :] = jnp.sum(product, axis=0, keepdims=True)
        for k in range(3):
            basis[k] = turn(powers[k], LANES - BASE)[8 : 8 + BY, :]


def finish_kernel(moments, basis, out):
    totals = jnp.sum(moments[...], axis=1, keepdims=True)
    m = [totals[k : k + 1, :] for k in range(6)]
    low10 = m[2] / m[1]
    low20 = m[3] / m[1]
    pivot1 = m[3] - low10 * m[2]
    part21 = m[4] - low20 * m[2]
    low21 = part21 / pivot1
    pivot2 = m[5] - low20 * m[3] - low21 * part21
    y1 = m[1] - low10 * m[0]
    y2 = m[2] - low20 * m[0] - low21 * y1
    z2 = y2 / pivot2
    z1 = y1 / pivot1 - low21 * z2
    z0 = m[0] / m[1] - low10 * z1 - low20 * z2
    value = z0 * basis[0] + z1 * basis[1] + z2 * basis[2]
    out[...] = value[:, 0:WIDE]


def quad_sum(values, axis, partner):
    count = lax.axis_size(axis)
    others = [
        lax.ppermute(values, axis, [(i, partner(i, turn)) for i in range(count)])
        for turn in range(1, 4)
    ]
    return (values + others[0]) + (others[1] + others[2])


def total_over_devices(values):
    values = values + lax.ppermute(values, "gy", [(i, i ^ 1) for i in range(lax.axis_size("gy"))])
    values = quad_sum(values, "gy", lambda i, turn: i ^ (2 * turn))
    values = quad_sum(values, "gx", lambda i, turn: i ^ turn)
    return quad_sum(values, "gx", lambda i, turn: i ^ (4 * turn))


def whole(shape):
    return pl.BlockSpec(shape, lambda k: (0,) * len(shape))


def per_device(block_list, wet_levels, mixing, velocity, tracers, damping):
    f32 = jnp.float32
    slots, fields_each, levels, cells = tracers.shape
    params = pltpu.CompilerParams(
        dimension_semantics=("arbitrary",), vmem_limit_bytes=40 * 1024 * 1024
    )
    level_block = pl.BlockSpec((slots, fields_each, 8, cells), lambda k: (0, 0, k, 0))
    rows_block = pl.BlockSpec((1, NS, 8, LANES), lambda k: (k, 0, 0, 0))
    columns_block = pl.BlockSpec((1, EW, 8, LANES), lambda k: (k, 0, 0, 0))
    rows_extra = pl.BlockSpec((TILES, 1, 8, LANES), lambda k: (0, NS - 1, 0, 0))
    columns_extra = pl.BlockSpec((TILES, 1, 8, LANES), lambda k: (0, EW - 1, 0, 0))
    own_specs = [
        pl.BlockSpec(memory_space=pltpu.SMEM),
        whole(wet_levels.shape),
        whole(mixing.shape),
        whole(damping.shape),
        level_block,
        level_block,
    ]
    own = (block_list, wet_levels, mixing, damping, velocity, tracers)
    rows_type = jax.ShapeDtypeStruct((TILES, NS, 8, LANES), f32)
    columns_type = jax.ShapeDtypeStruct((TILES, EW, 8, LANES), f32)

    up, down = pl.pallas_call(
        rows_kernel,
        grid=(TILES,),
        in_specs=own_specs,
        out_specs=[rows_block, rows_block],
        out_shape=[rows_type, rows_type],
        scratch_shapes=[pltpu.VMEM((BY, LANES), f32)],
        compiler_params=params,
        name="pack_rows",
    )(*own)
    rows_total = lax.axis_size("gy")
    up = lax.ppermute(up, "gy", [(i, i + 1) for i in range(rows_total - 1)])
    down = lax.ppermute(down, "gy", [(i + 1, i) for i in range(rows_total - 1)])

    east, west = pl.pallas_call(
        columns_kernel,
        grid=(TILES,),
        in_specs=own_specs + [rows_block, rows_block, rows_extra, rows_extra],
        out_specs=[columns_block, columns_block],
        out_shape=[columns_type, columns_type],
        scratch_shapes=[pltpu.VMEM((BY, LANES), f32)],
        compiler_params=params,
        name="pack_columns",
    )(*own, up, down, up, down)
    columns_total = lax.axis_size("gx")
    from_west = lax.ppermute(east, "gx", [(i, (i + 1) % columns_total) for i in range(columns_total)])
    from_east = lax.ppermute(west, "gx", [((i + 1) % columns_total, i) for i in range(columns_total)])

    row_store = pltpu.VMEM((ROWS, 8, LANES), f32)
    new_tracers, basis, moments = pl.pallas_call(
        main_kernel,
        grid=(TILES,),
        in_specs=own_specs
        + [rows_block, rows_block, columns_block, columns_block]
        + [rows_extra, rows_extra, columns_extra, columns_extra],
        out_specs=[level_block, whole((3, BY, LANES)), whole((8, LANES))],
        out_shape=[
            jax.ShapeDtypeStruct(tracers.shape, f32),
            jax.ShapeDtypeStruct((3, BY, LANES), f32),
            jax.ShapeDtypeStruct((8, LANES), f32),
        ],
        scratch_shapes=[
            pltpu.VMEM((4, ROWS, 8, LANES), f32),
            pltpu.VMEM((2, ROWS, 8, LANES), f32),
            pltpu.VMEM((2, ROWS, 8, LANES), f32),
            pltpu.VMEM((2, ROWS, 8, LANES), f32),
            row_store,
            row_store,
            row_store,
            row_store,
            row_store,
            pltpu.VMEM((SURFACE, LANES), f32),
            pltpu.VMEM((SURFACE, LANES), f32),
            pltpu.VMEM((SURFACE, LANES), f32),
        ],
        compiler_params=params,
        name="advance",
    )(*own, up, down, from_west, from_east, up, down, from_west, from_east)

    moments = total_over_devices(moments)
    height = pl.pallas_call(
        finish_kernel,
        out_shape=jax.ShapeDtypeStruct((BY, WIDE), f32),
        name="finish",
    )(moments, basis)
    return (new_tracers, height)


def solution(mesh):
    return jax.shard_map(
        per_device,
        mesh=mesh,
        in_specs=(
            P(("gx", "gy")),
            P(("gx", "gy"), None),
            P(("gx", "gy"), None),
            P(("gx", "gy"), None, None, None),
            P(("gx", "gy"), None, None, None),
            P("gy", "gx"),
        ),
        out_specs=(P(("gx", "gy"), None, None, None), P("gy", "gx")),
        check_vma=False,
    )
```

```python
import functools
import math

import jax
import jax.numpy as jnp
from jax import lax
from jax.experimental import pallas as pl
from jax.experimental.pallas import tpu as pltpu
from jax.sharding import PartitionSpec as P

BX = 45
BY = 40
CELLS = BX * BY
LEVELS = 62
LANES = 128
TILES = 8
REACH = 7
ROWS = BY + 2 * REACH
AHEAD = 26
BASE = 8
WIDE = 2 * BX
NS = 29
EW = 13
SURFACE = 56

advect_rate = 0.25
mixing_rate = 0.015
salt_weight = 0.8


def lane_ids():
    return lax.broadcasted_iota(jnp.int32, (8, LANES), 1)


def merge(parts, lane):
    flat = []
    for low, width, value in parts:
        low %= LANES
        if low + width > LANES:
            flat.append((low, value))
            flat.append((0, value))
        else:
            flat.append((low, value))
    flat.sort(key=lambda part: part[0])
    result = flat[0][1]
    last = result
    for low, value in flat[1:]:
        if value is last:
            continue
        result = jnp.where(lane >= low, value, result)
        last = value
    return result


def turn(value, shift):
    shift %= LANES
    return pltpu.roll(value, shift, 1) if shift else value


class Source:
    def __init__(self, own, west=None, east=None):
        self.load = {"own": own, "west": west, "east": east}
        self.kept = {}

    def tile(self, kind, position, number):
        key = (kind, position, number)
        if key not in self.kept:
            load = self.load[kind]
            self.kept[key] = load(position, number) if kind == "own" else load(number)
        return self.kept[key]

    def cells(self, position, start, width):
        parts = []
        at = start
        while at < start + width:
            number = at // LANES
            end = min(start + width, (number + 1) * LANES)
            parts.append((at, end - at, self.tile("own", position, number)))
            at = end
        return parts


def pack_columns(source, lane):
    east, west = [], []
    for group in range(3):
        rows = range(17 * group, min(17 * group + 17, BY))
        east.append(merge([c for r in rows for c in source.cells(1, BX * r + BX - REACH, REACH)], lane))
        west.append(merge([c for r in rows for c in source.cells(0, BX * r, REACH)], lane))
    return east, west


def strip_rows(source, lane):
    turned = {}

    def combined(r):
        if r in turned:
            return turned[r]
        parts = []
        if 0 <= r - 1 < BY:
            parts.append((BX * r - REACH, REACH, source.tile("west", 0, (r - 1) // 17)))
        if 0 <= r < BY:
            parts += source.cells(0, BX * r, BX)
        if 0 <= r + 1 < BY:
            parts += source.cells(1, BX * (r + 1), BX)
        if 0 <= r + 2 < BY:
            parts.append((BX * (r + 2), REACH, source.tile("east", 0, (r + 2) // 17)))
        turned[r] = turn(merge(parts, lane), BASE - BX * r)
        return turned[r]

    for row in range(BY):
        value = jnp.where(lane < BASE, combined(row + 1), combined(row))
        value = jnp.where(lane < BASE + BX, value, combined(row - 1))
        yield row, jnp.where(lane < BASE + WIDE, value, combined(row - 2))


def slot_swap(block_list):
    first = block_list[0]
    return jnp.where(first >= 0, first & 1, 1 - (block_list[1] & 1))


def field_loader(ref, which, swap):
    def load(position, number):
        slot = swap if position == 0 else 1 - swap
        if number < 14:
            return ref[slot, which, :, number * LANES : (number + 1) * LANES]
        return turn(ref[slot, which, :, CELLS - LANES : CELLS], CELLS % LANES)

    return load


def column_loader(wet_levels, mixing, swap):
    def load(position, number):
        slot = swap if position == 0 else 1 - swap
        low = number * LANES if number < 14 else CELLS - LANES
        both = wet_levels[:, low : low + LANES].astype(jnp.float32)
        depth = jnp.where(slot == 0, both[0:1, :], both[1:2, :])
        both = mixing[:, low : low + LANES]
        mix = jnp.where(slot == 0, both[0:1, :], both[1:2, :])
        sublane = lax.broadcasted_iota(jnp.int32, (8, LANES), 0)
        value = jnp.where(
            sublane == 0, jnp.broadcast_to(depth, (8, LANES)), jnp.broadcast_to(mix, (8, LANES))
        )
        return value if number < 14 else turn(value, CELLS % LANES)

    return load


def columns_kernel(block_list, wet_levels, mixing, damping, velocity, tracers, east, west, padded):
    lane = lane_ids()
    swap = slot_swap(block_list)
    step = pl.program_id(0)
    for field in range(4):
        source = Source(field_loader(tracers if field < 2 else velocity, field % 2, swap))
        easts, wests = pack_columns(source, lane)
        for number in range(3):
            east[0, 3 * field + number] = easts[number]
            west[0, 3 * field + number] = wests[number]

    for number in range(3):

        @pl.when(step == number)
        def _():
            easts, wests = pack_columns(Source(column_loader(wet_levels, mixing, swap)), lane)
            east[0, EW - 1] = easts[number]
            west[0, EW - 1] = wests[number]

    @pl.when(step >= 3)
    def _():
        padded[...] = jnp.zeros_like(padded)
        padded[:, 0:WIDE] = damping[...]
        tiles = [padded[8 * j : 8 * j + 8, :] for j in range(5)]
        east[0, EW - 1] = merge([(2 * j, 2, turn(t, 2 * j - WIDE + 2)) for j, t in enumerate(tiles)], lane)
        west[0, EW - 1] = merge([(2 * j, 2, turn(t, 2 * j)) for j, t in enumerate(tiles)], lane)


def strips_kernel(
    block_list, wet_levels, mixing, damping, velocity, tracers,
    from_west, from_east, west_extra, east_extra,
    fields, columns, up, down, padded,
):
    lane = lane_ids()
    swap = slot_swap(block_list)
    step = pl.program_id(0)

    @pl.when(step == 0)
    def _():
        padded[...] = jnp.zeros_like(padded)
        padded[:, 0:WIDE] = damping[...]
        for j in range(5):
            value = turn(padded[8 * j : 8 * j + 8, :], BASE)
            value = jnp.where(lane < BASE, turn(west_extra[3, 0], BASE - 2 - 2 * j), value)
            value = jnp.where(lane < BASE + WIDE, value, turn(east_extra[3, 0], BASE + WIDE - 2 * j))
            padded[8 * j : 8 * j + 8, :] = value
        source = Source(
            column_loader(wet_levels, mixing, swap),
            lambda tile: west_extra[tile, 0],
            lambda tile: east_extra[tile, 0],
        )
        sublane = lax.broadcasted_iota(jnp.int32, (8, LANES), 0)
        for row, value in strip_rows(source, lane):
            damp = jnp.broadcast_to(padded[row : row + 1, :], (8, LANES))
            columns[row] = jnp.where(sublane == 2, damp, value)

    for field in range(4):
        source = Source(
            field_loader(tracers if field < 2 else velocity, field % 2, swap),
            lambda number, field=field: from_west[0, 3 * field + number],
            lambda number, field=field: from_east[0, 3 * field + number],
        )
        for row, value in strip_rows(source, lane):
            value = value if field < 2 else (0.25 * advect_rate) * value
            fields[0, field, row] = value
            if row < REACH:
                down[0, REACH * field + row] = value
            if row >= BY - REACH:
                up[0, REACH * field + row - (BY - REACH)] = value
    row = jnp.minimum(step, REACH - 1)
    down[0, NS - 1] = columns[row]
    up[0, NS - 1] = columns[BY - REACH + row]


def staggered(spans, phases):
    state = {}
    length = max(high - low + 1 for low, high in spans)
    ahead = min(AHEAD, length)
    for time in range(length + ahead * (len(phases) - 1)):
        for number in reversed(range(len(phases))):
            for span, (low, high) in enumerate(spans):
                row = low + time - number * ahead
                if low <= row <= high:
                    phases[number](span, row, state)


class Band:
    def __init__(self, low, high, read, write, eastward, northward):
        self.low, self.high, self.read, self.write = low, high, read, write
        self.eastward, self.northward = eastward, northward


def advance(bands, levels, shared, scratch):
    depth_east, depth_north, mix = shared
    scaled, held = scratch

    def rise(band, n, row):
        read = bands[band].read
        return jnp.where(levels < depth_north(row), read(n, row + 1) - read(n, row), 0.0)

    def look_east(band, row, state):
        for n in range(2):
            state[band, n, row] = turn(bands[band].read(n, row), LANES - 1)

    def step_east(band, row, state):
        wet = levels < depth_east(row)
        for n in range(2):
            here, beside = bands[band].read(n, row), state[band, n, row]
            step = jnp.where(wet, beside - here, 0.0)
            state[band, n, row] = step, turn(step, 1)
            held[n, row + REACH] = beside + here

    def scale(band, row, state):
        for n in range(2):
            step, back = state.pop((band, n, row))
            drop = state.pop((band, n)) if (band, n) in state else rise(band, n, row - 1)
            state[band, n] = rise(band, n, row)
            scaled[n, row + REACH] = mix(row) * ((step - back) + (state[band, n] - drop))

    staggered([(b.low - 1, b.high + 1) for b in bands], (look_east, step_east, scale))

    def north_flow(band, n, row):
        read, northward = bands[band].read, bands[band].northward
        step = scaled[n, row + 1 + REACH] - scaled[n, row + REACH]
        both = (northward(row) + northward(row + 1)) * (read(n, row) + read(n, row + 1)) + step
        return jnp.where(levels < depth_north(row), both, 0.0)

    def look_east_again(band, row, state):
        state[band, "flow", row] = turn(bands[band].eastward(row), LANES - 1)
        for n in range(2):
            state[band, n, row] = turn(scaled[n, row + REACH], LANES - 1)

    def east_flow(band, row, state):
        wet = levels < depth_east(row)
        flow = bands[band].eastward(row) + state.pop((band, "flow", row))
        for n in range(2):
            at = row + REACH
            both = flow * held[n, at] + (state[band, n, row] - scaled[n, at])
            both = jnp.where(wet, both, 0.0)
            state[band, n, row] = both, turn(both, 1)

    def change(band, row, state):
        for n in range(2):
            east, back = state.pop((band, n, row))
            south = state.pop((band, n)) if (band, n) in state else north_flow(band, n, row - 1)
            state[band, n] = north_flow(band, n, row)
            result = bands[band].read(n, row) - ((east - back) + (state[band, n] - south))
            bands[band].write(n, row, result)

    staggered([(b.low, b.high) for b in bands], (look_east_again, east_flow, change))


def level_ids(step):
    return (lax.broadcasted_iota(jnp.int32, (8, LANES), 0) + 8 * step).astype(jnp.float32)


def spread_columns(column, rows, depth, depth_east, depth_north, mix):
    last = None
    for row in rows:
        value = column(row)
        here = jnp.broadcast_to(value[0:1, :], (8, LANES))
        depth[row + REACH] = here
        depth_east[row + REACH] = jnp.minimum(here, turn(here, LANES - 1))
        mix[row + REACH] = mixing_rate * jnp.broadcast_to(value[1:2, :], (8, LANES))
        if last is not None:
            depth_north[row + REACH - 1] = jnp.minimum(here, last)
        last = here


def contribution(levels, depth, warm, salt):
    return jnp.where(levels < depth, warm - salt_weight * salt, 0.0)


def inner_kernel(
    fields, columns, halfway, moved, forcing,
    middle, depth, depth_east, depth_north, mix, scaled, held,
):
    step = pl.program_id(0)

    @pl.when(step == 0)
    def _():
        spread_columns(lambda row: columns[row], range(BY), depth, depth_east, depth_north, mix)
        forcing[...] = jnp.zeros_like(forcing)

    levels = level_ids(step)
    shared = (
        lambda row: depth_east[row + REACH],
        lambda row: depth_north[row + REACH],
        lambda row: mix[row + REACH],
    )

    def write_middle(n, row, value):
        middle[n, row] = value
        if row < 6:
            halfway[0, n, row - 2] = value
        if row >= 34:
            halfway[0, n, row - 30] = value

    def write_moved(n, row, value):
        moved[0, n, row - 4] = value

    def eastward(row):
        return fields[0, 2, row]

    def northward(row):
        return fields[0, 3, row]

    first = Band(2, 37, lambda n, row: fields[0, n, row], write_middle, eastward, northward)
    second = Band(4, 35, lambda n, row: middle[n, row], write_moved, eastward, northward)
    advance([first], levels, shared, (scaled, held))
    advance([second], levels, shared, (scaled, held))
    for row in range(4, 36):
        forcing[row] += contribution(
            levels, depth[row + REACH], moved[0, 0, row - 4], moved[0, 1, row - 4]
        )


def surface_operator(values, couple_east, couple_north, damping):
    east = couple_east * (values - turn(values, LANES - 1))
    north = couple_north * (values - pltpu.roll(values, SURFACE - 1, 0))
    return damping * values + ((east - turn(east, 1)) + (north - pltpu.roll(north, 1, 0)))


def outer_kernel(
    low_fields, high_fields, columns, up, down, up_extra, down_extra, halfway, inner_forcing,
    moved, basis, moments,
    middle, beyond, depth, depth_east, depth_north, mix, scaled, held, forcing, surface, depths, dampings,
):
    step = pl.program_id(0)

    def column(row):
        if row < 0:
            return up_extra[row + REACH, 0]
        if row >= BY:
            return down_extra[row - BY, 0]
        return columns[row]

    rows = range(-REACH, BY + REACH)

    @pl.when(step == 0)
    def _():
        spread_columns(column, rows, depth, depth_east, depth_north, mix)
        forcing[...] = jnp.zeros_like(forcing)

    levels = level_ids(step)
    shared = (
        lambda row: depth_east[row + REACH],
        lambda row: depth_north[row + REACH],
        lambda row: mix[row + REACH],
    )

    def field(number, row):
        if row < 0:
            return up[0, REACH * number + row + REACH]
        if row >= BY:
            return down[0, REACH * number + row - BY]
        return low_fields[0, number, row] if row < 10 else high_fields[0, number, row - 30]

    def read_middle(n, row):
        if 2 <= row < 6:
            return halfway[0, n, row - 2]
        if 34 <= row < 38:
            return halfway[0, n, row - 30]
        return middle[n, row + REACH]

    def write_middle(n, row, value):
        middle[n, row + REACH] = value

    def write_beyond(n, row, value):
        beyond[n, row + REACH] = value
        if 0 <= row < 4:
            moved[0, n, row] = value
        if 36 <= row < BY:
            moved[0, n, row - 32] = value

    def eastward(row):
        return field(2, row)

    def northward(row):
        return field(3, row)

    bands = [Band(low, high, field, write_middle, eastward, northward) for low, high in ((-5, 1), (38, 44))]
    advance(bands, levels, shared, (scaled, held))
    bands = [
        Band(low, high, read_middle, write_beyond, eastward, northward) for low, high in ((-3, 3), (36, 42))
    ]
    advance(bands, levels, shared, (scaled, held))
    for row in (*range(-3, 4), *range(36, 43)):
        at = row + REACH
        forcing[at] += contribution(levels, depth[at], beyond[0, at], beyond[1, at])

    @pl.when(step == TILES - 1)
    def _():
        surface[...] = jnp.zeros_like(surface)
        for row in range(-3, 43):
            part = inner_forcing[row] if 4 <= row < 36 else forcing[row + REACH]
            total = jnp.sum(part, axis=0, keepdims=True)
            surface[row + 8 : row + 9, :] = total * (1.0 / math.sqrt(LEVELS))
        depths[...] = jnp.zeros_like(depths)
        dampings[...] = jnp.zeros_like(dampings)
        for row in rows:
            value = column(row)
            depths[row + 8 : row + 9, :] = value[0:1, :]
            dampings[row + 8 : row + 9, :] = value[2:3, :]
        here = depths[...]
        couple_east = jnp.minimum(here, turn(here, LANES - 1)) * (1.0 / LEVELS)
        couple_north = jnp.minimum(here, pltpu.roll(here, SURFACE - 1, 0)) * (1.0 / LEVELS)
        diagonal = dampings[...]
        powers = [surface[...]]
        for _ in range(3):
            powers.append(surface_operator(powers[-1], couple_east, couple_north, diagonal))
        row_id = lax.broadcasted_iota(jnp.int32, (SURFACE, LANES), 0)
        lane_id = lax.broadcasted_iota(jnp.int32, (SURFACE, LANES), 1)
        own = (row_id >= 8) & (row_id < 8 + BY) & (lane_id >= BASE) & (lane_id < BASE + WIDE)
        moments[...] = jnp.zeros_like(moments)
        for k in range(6):
            product = jnp.where(own, powers[k // 2] * powers[(k + 1) // 2], 0.0)
            moments[k : k + 1, :] = jnp.sum(product, axis=0, keepdims=True)
        for k in range(3):
            basis[k] = turn(powers[k], LANES - BASE)[8 : 8 + BY, :]


def slots_kernel(block_list, moved, edges, new_tracers):
    lane = lane_ids()
    swap = slot_swap(block_list)
    for n in range(2):
        turned = {}

        def strip(row, n=n):
            row = min(max(row, 0), BY - 1)
            if row < 4:
                return edges[0, n, row]
            return edges[0, n, row - 32] if row >= 36 else moved[0, n, row - 4]

        def back(r, strip=strip, turned=turned):
            if r not in turned:
                value = jnp.where(lane < BASE + BX, strip(r), strip(r + 1))
                turned[r] = turn(value, BX * r - BASE)
            return turned[r]

        for number in range(15):
            for position in range(2):
                slot = swap if position == 0 else 1 - swap
                first, end = number * LANES, min((number + 1) * LANES, CELLS)
                parts = []
                for row in range(first // BX, (end - 1) // BX + 1):
                    low = max(row * BX, first)
                    parts.append((low, min((row + 1) * BX, end) - low, back(row - position)))
                value = merge(parts, lane)
                new_tracers[slot, n, :, first:end] = value[:, 0 : end - first]


def finish_kernel(moments, basis, out):
    totals = jnp.sum(moments[...], axis=1, keepdims=True)
    m = [totals[k : k + 1, :] for k in range(6)]
    low10 = m[2] / m[1]
    low20 = m[3] / m[1]
    pivot1 = m[3] - low10 * m[2]
    part21 = m[4] - low20 * m[2]
    low21 = part21 / pivot1
    pivot2 = m[5] - low20 * m[3] - low21 * part21
    y1 = m[1] - low10 * m[0]
    y2 = m[2] - low20 * m[0] - low21 * y1
    z2 = y2 / pivot2
    z1 = y1 / pivot1 - low21 * z2
    z0 = m[0] / m[1] - low10 * z1 - low20 * z2
    value = z0 * basis[0] + z1 * basis[1] + z2 * basis[2]
    out[...] = value[:, 0:WIDE]


def quad_sum(values, axis, partner):
    count = lax.axis_size(axis)
    others = [
        lax.ppermute(values, axis, [(i, partner(i, turn)) for i in range(count)])
        for turn in range(1, 4)
    ]
    return (values + others[0]) + (others[1] + others[2])


def total_over_devices(values):
    values = values + lax.ppermute(values, "gy", [(i, i ^ 1) for i in range(lax.axis_size("gy"))])
    values = quad_sum(values, "gy", lambda i, turn: i ^ (2 * turn))
    values = quad_sum(values, "gx", lambda i, turn: i ^ turn)
    return quad_sum(values, "gx", lambda i, turn: i ^ (4 * turn))


def whole(shape):
    return pl.BlockSpec(shape, lambda k: (0,) * len(shape))


def per_device(block_list, wet_levels, mixing, velocity, tracers, damping):
    f32 = jnp.float32
    slots, fields_each, levels, cells = tracers.shape
    params = pltpu.CompilerParams(
        dimension_semantics=("arbitrary",), vmem_limit_bytes=40 * 1024 * 1024
    )
    level_block = pl.BlockSpec((slots, fields_each, 8, cells), lambda k: (0, 0, k, 0))

    def tiles(*shape):
        zeros = (0,) * (len(shape) + 2)
        return (
            pl.BlockSpec((1, *shape, 8, LANES), lambda k: (k, *zeros)),
            jax.ShapeDtypeStruct((TILES, *shape, 8, LANES), f32),
        )

    rows_block, rows_type = tiles(NS)
    columns_block, columns_type = tiles(EW)
    rows_extra = pl.BlockSpec((TILES, 1, 8, LANES), lambda k: (0, NS - 1, 0, 0))
    columns_extra = pl.BlockSpec((TILES, 1, 8, LANES), lambda k: (0, EW - 1, 0, 0))
    own_specs = [
        pl.BlockSpec(memory_space=pltpu.SMEM),
        whole(wet_levels.shape),
        whole(mixing.shape),
        whole(damping.shape),
        level_block,
        level_block,
    ]
    own = (block_list, wet_levels, mixing, damping, velocity, tracers)

    east, west = pl.pallas_call(
        columns_kernel,
        grid=(TILES,),
        in_specs=own_specs,
        out_specs=[columns_block, columns_block],
        out_shape=[columns_type, columns_type],
        scratch_shapes=[pltpu.VMEM((BY, LANES), f32)],
        compiler_params=params,
        name="pack_columns",
    )(*own)
    columns_total = lax.axis_size("gx")
    from_west = lax.ppermute(east, "gx", [(i, (i + 1) % columns_total) for i in range(columns_total)])
    from_east = lax.ppermute(west, "gx", [((i + 1) % columns_total, i) for i in range(columns_total)])

    fields_block, fields_type = tiles(4, BY)
    column_shape = (BY, 8, LANES)
    fields, columns, up, down = pl.pallas_call(
        strips_kernel,
        grid=(TILES,),
        in_specs=own_specs + [columns_block, columns_block, columns_extra, columns_extra],
        out_specs=[fields_block, whole(column_shape), rows_block, rows_block],
        out_shape=[fields_type, jax.ShapeDtypeStruct(column_shape, f32), rows_type, rows_type],
        scratch_shapes=[pltpu.VMEM((BY, LANES), f32)],
        compiler_params=params,
        name="strips",
    )(*own, from_west, from_east, from_west, from_east)
    rows_total = lax.axis_size("gy")
    from_below = lax.ppermute(up, "gy", [(i, i + 1) for i in range(rows_total - 1)])
    from_above = lax.ppermute(down, "gy", [(i + 1, i) for i in range(rows_total - 1)])

    row_store = pltpu.VMEM((ROWS, 8, LANES), f32)
    pair_store = pltpu.VMEM((2, ROWS, 8, LANES), f32)
    halfway_block, halfway_type = tiles(2, 8)
    moved_block, moved_type = tiles(2, 32)
    halfway, moved, forcing = pl.pallas_call(
        inner_kernel,
        grid=(TILES,),
        in_specs=[fields_block, whole(column_shape)],
        out_specs=[halfway_block, moved_block, whole(column_shape)],
        out_shape=[halfway_type, moved_type, jax.ShapeDtypeStruct(column_shape, f32)],
        scratch_shapes=[pair_store] + [row_store] * 4 + [pair_store] * 2,
        compiler_params=params,
        cost_estimate=pl.CostEstimate(flops=60_000_000, bytes_accessed=10_000_000, transcendentals=0),
        name="inner_rows",
    )(fields, columns)

    low_block = pl.BlockSpec((1, 4, 10, 8, LANES), lambda k: (k, 0, 0, 0, 0))
    high_block = pl.BlockSpec((1, 4, 10, 8, LANES), lambda k: (k, 0, 3, 0, 0))
    edges, basis, moments = pl.pallas_call(
        outer_kernel,
        grid=(TILES,),
        in_specs=[low_block, high_block, whole(column_shape), rows_block, rows_block]
        + [rows_extra, rows_extra, halfway_block, whole(column_shape)],
        out_specs=[halfway_block, whole((3, BY, LANES)), whole((8, LANES))],
        out_shape=[
            halfway_type,
            jax.ShapeDtypeStruct((3, BY, LANES), f32),
            jax.ShapeDtypeStruct((8, LANES), f32),
        ],
        scratch_shapes=[pair_store] * 2
        + [row_store] * 4
        + [pair_store] * 2
        + [row_store]
        + [pltpu.VMEM((SURFACE, LANES), f32)] * 3,
        compiler_params=params,
        name="outer_rows",
    )(fields, fields, columns, from_below, from_above, from_below, from_above, halfway, forcing)

    new_tracers = pl.pallas_call(
        slots_kernel,
        grid=(TILES,),
        in_specs=[pl.BlockSpec(memory_space=pltpu.SMEM), moved_block, halfway_block],
        out_specs=level_block,
        out_shape=jax.ShapeDtypeStruct(tracers.shape, f32),
        compiler_params=params,
        cost_estimate=pl.CostEstimate(flops=4_000_000, bytes_accessed=4_000_000, transcendentals=0),
        name="to_slots",
    )(block_list, moved, edges)

    moments = total_over_devices(moments)
    height = pl.pallas_call(
        finish_kernel,
        out_shape=jax.ShapeDtypeStruct((BY, WIDE), f32),
        name="finish",
    )(moments, basis)
    return (new_tracers, height)


def solution(mesh):
    return jax.shard_map(
        per_device,
        mesh=mesh,
        in_specs=(
            P(("gx", "gy")),
            P(("gx", "gy"), None),
            P(("gx", "gy"), None),
            P(("gx", "gy"), None, None, None),
            P(("gx", "gy"), None, None, None),
            P("gy", "gx"),
        ),
        out_specs=(P(("gx", "gy"), None, None, None), P("gy", "gx")),
        check_vma=False,
    )
```

```python
import functools
import math

import jax
import jax.numpy as jnp
from jax import lax
from jax.experimental import pallas as pl
from jax.experimental.pallas import tpu as pltpu
from jax.sharding import PartitionSpec as P

BX = 45
BY = 40
CELLS = BX * BY
LEVELS = 62
LANES = 128
TILES = 8
REACH = 7
ROWS = BY + 2 * REACH
AHEAD = 26
BASE = 8
WIDE = 2 * BX
NS = 29
EW = 13
SURFACE = 56

advect_rate = 0.25
mixing_rate = 0.015
salt_weight = 0.8


def lane_ids():
    return lax.broadcasted_iota(jnp.int32, (8, LANES), 1)


def merge(parts, lane):
    flat = []
    for low, width, value in parts:
        low %= LANES
        if low + width > LANES:
            flat.append((low, value))
            flat.append((0, value))
        else:
            flat.append((low, value))
    flat.sort(key=lambda part: part[0])
    result = flat[0][1]
    last = result
    for low, value in flat[1:]:
        if value is last:
            continue
        result = jnp.where(lane >= low, value, result)
        last = value
    return result


def turn(value, shift):
    shift %= LANES
    return pltpu.roll(value, shift, 1) if shift else value


class Source:
    def __init__(self, load):
        self.load = load
        self.kept = {}

    def tile(self, *key):
        if key not in self.kept:
            self.kept[key] = self.load(*key)
        return self.kept[key]

    def cells(self, position, start, width):
        parts = []
        at = start
        while at < start + width:
            number = at // LANES
            end = min(start + width, (number + 1) * LANES)
            parts.append((at, end - at, self.tile(position, number)))
            at = end
        return parts


def pack_columns(source, lane):
    east, west = [], []
    for group in range(3):
        rows = range(17 * group, min(17 * group + 17, BY))
        east.append(merge([c for r in rows for c in source.cells(1, BX * r + BX - REACH, REACH)], lane))
        west.append(merge([c for r in rows for c in source.cells(0, BX * r, REACH)], lane))
    return east, west


def strip_rows(source, lane):
    turned = {}

    def combined(r):
        if r not in turned:
            parts = source.cells(0, BX * r, BX) if r >= 0 else []
            if r + 1 < BY:
                parts += source.cells(1, BX * (r + 1), BX)
            turned[r] = turn(merge(parts, lane), BASE - BX * r)
        return turned[r]

    for r in range(-1, BY):
        combined(r)
    for row in range(BY):
        yield row, jnp.where(lane < BASE + BX, combined(row), combined(row - 1))


def beside_rows(rows, west, east, lane):
    turned = {}

    def combined(r):
        if r not in turned:
            low, high = (BX * r - REACH) % LANES, BX * (r + 2) % LANES
            if not 0 <= r - 1 < BY:
                value = east((r + 2) // 17)
            elif not 0 <= r + 2 < BY:
                value = west((r - 1) // 17)
            elif low < high:
                inside = lane < high if high + REACH <= LANES else (lane >= low) & (lane < high)
                value = jnp.where(inside, west((r - 1) // 17), east((r + 2) // 17))
            else:
                inside = lane < low if low + REACH <= LANES else (lane >= high) & (lane < low)
                value = jnp.where(inside, east((r + 2) // 17), west((r - 1) // 17))
            turned[r] = turn(value, BASE - BX * r)
        return turned[r]

    for r in sorted({row + 1 for row in rows} | {row - 2 for row in rows}):
        combined(r)
    for row in rows:
        yield row, combined(row + 1), combined(row - 2)


def slot_swap(block_list):
    first = block_list[0]
    return jnp.where(first >= 0, first & 1, 1 - (block_list[1] & 1))


def over_level_blocks(work):
    def body(block, carry):
        work(block, pl.ds(pl.multiple_of(8 * block, 8), 8))
        return carry

    lax.fori_loop(0, TILES - 1, body, 0)
    work(TILES - 1, pl.ds(LEVELS - 8, 8))


def field_loader(ref, which, levels, swap):
    def load(position, number):
        slot = swap if position == 0 else 1 - swap
        if number < 14:
            return ref[slot, which, levels, number * LANES : (number + 1) * LANES]
        return turn(ref[slot, which, levels, CELLS - LANES : CELLS], CELLS % LANES)

    return load


def column_loader(wet_levels, mixing, swap):
    def load(position, number):
        slot = swap if position == 0 else 1 - swap
        low = number * LANES if number < 14 else CELLS - LANES
        both = wet_levels[:, low : low + LANES].astype(jnp.float32)
        depth = jnp.where(slot == 0, both[0:1, :], both[1:2, :])
        both = mixing[:, low : low + LANES]
        mix = jnp.where(slot == 0, both[0:1, :], both[1:2, :])
        sublane = lax.broadcasted_iota(jnp.int32, (8, LANES), 0)
        value = jnp.where(
            sublane == 0, jnp.broadcast_to(depth, (8, LANES)), jnp.broadcast_to(mix, (8, LANES))
        )
        return value if number < 14 else turn(value, CELLS % LANES)

    return load


def columns_kernel(block_list, wet_levels, mixing, damping, velocity, tracers, east, west, padded):
    lane = lane_ids()
    swap = slot_swap(block_list)

    def work(block, levels):
        for field in range(4):
            ref = tracers if field < 2 else velocity
            easts, wests = pack_columns(Source(field_loader(ref, field % 2, levels, swap)), lane)
            scale = 1.0 if field < 2 else 0.25 * advect_rate
            for number in range(3):
                east[block, 3 * field + number] = easts[number] * scale
                west[block, 3 * field + number] = wests[number] * scale

    over_level_blocks(work)
    easts, wests = pack_columns(Source(column_loader(wet_levels, mixing, swap)), lane)
    padded[...] = jnp.zeros_like(padded)
    padded[:, 0:WIDE] = damping[...]
    tiles = [padded[8 * j : 8 * j + 8, :] for j in range(5)]
    easts.append(merge([(2 * j, 2, turn(t, 2 * j - WIDE + 2)) for j, t in enumerate(tiles)], lane))
    wests.append(merge([(2 * j, 2, turn(t, 2 * j)) for j, t in enumerate(tiles)], lane))
    for block in range(TILES):
        east[block, EW - 1] = easts[min(block, 3)]
        west[block, EW - 1] = wests[min(block, 3)]


def strips_kernel(block_list, wet_levels, mixing, damping, velocity, tracers, fields, columns, padded):
    lane = lane_ids()
    swap = slot_swap(block_list)
    padded[...] = jnp.zeros_like(padded)
    padded[:, 0:WIDE] = damping[...]
    for j in range(5):
        padded[8 * j : 8 * j + 8, :] = turn(padded[8 * j : 8 * j + 8, :], BASE)
    sublane = lax.broadcasted_iota(jnp.int32, (8, LANES), 0)
    for row, value in strip_rows(Source(column_loader(wet_levels, mixing, swap)), lane):
        damp = jnp.broadcast_to(padded[row : row + 1, :], (8, LANES))
        columns[row] = jnp.where(sublane == 2, damp, value)

    def work(block, levels):
        for field in range(4):
            ref = tracers if field < 2 else velocity
            for row, value in strip_rows(Source(field_loader(ref, field % 2, levels, swap)), lane):
                fields[block, field, row] = value if field < 2 else (0.25 * advect_rate) * value

    over_level_blocks(work)


def place_halos(own_fields, own_columns, from_west, from_east, low_damp, high_damp, rows, put):
    lane = lane_ids()
    sublane = lax.broadcasted_iota(jnp.int32, (8, LANES), 0)
    for j in range(5):
        low_damp[8 * j : 8 * j + 8, :] = turn(from_west[3, EW - 1], BASE - 2 - 2 * j)
        high_damp[8 * j : 8 * j + 8, :] = turn(from_east[3, EW - 1], BASE + WIDE - 2 * j)
    sides = beside_rows(rows, lambda t: from_west[t, EW - 1], lambda t: from_east[t, EW - 1], lane)
    for row, west, east in sides:
        west = jnp.where(sublane == 2, jnp.broadcast_to(low_damp[row : row + 1, :], (8, LANES)), west)
        east = jnp.where(sublane == 2, jnp.broadcast_to(high_damp[row : row + 1, :], (8, LANES)), east)
        value = jnp.where(lane < BASE, west, own_columns[row])
        put(0, 4, row, jnp.where(lane < BASE + WIDE, value, east))

    def work(block, carry):
        for field in range(4):
            sides = beside_rows(
                rows,
                lambda t, field=field: from_west[block, 3 * field + t],
                lambda t, field=field: from_east[block, 3 * field + t],
                lane,
            )
            for row, west, east in sides:
                value = jnp.where(lane < BASE, west, own_fields[block, field, row])
                put(block, field, row, jnp.where(lane < BASE + WIDE, value, east))
        return carry

    lax.fori_loop(0, TILES, work, 0)


def row_message_kernel(own_fields, own_columns, from_west, from_east, up, down, low_damp, high_damp):
    def put(block, field, row, value):
        target, row = (down, row) if row < REACH else (up, row - (BY - REACH))
        if field == 4:
            target[row, NS - 1] = value
        else:
            target[block, REACH * field + row] = value

    up[TILES - 1, NS - 1] = jnp.zeros((8, LANES), jnp.float32)
    down[TILES - 1, NS - 1] = jnp.zeros((8, LANES), jnp.float32)
    rows = (*range(REACH), *range(BY - REACH, BY))
    place_halos(own_fields, own_columns, from_west, from_east, low_damp, high_damp, rows, put)


def halo_kernel(own_fields, own_columns, from_west, from_east, fields, columns, low_damp, high_damp):
    def put(block, field, row, value):
        if field == 4:
            columns[row] = value
        else:
            fields[block, field, row] = value

    place_halos(own_fields, own_columns, from_west, from_east, low_damp, high_damp, range(BY), put)


def staggered(spans, phases):
    state = {}
    length = max(high - low + 1 for low, high in spans)
    ahead = min(AHEAD, length)
    for time in range(length + ahead * (len(phases) - 1)):
        for number in reversed(range(len(phases))):
            for span, (low, high) in enumerate(spans):
                row = low + time - number * ahead
                if low <= row <= high:
                    phases[number](span, row, state)


class Band:
    def __init__(self, low, high, read, write, eastward, northward):
        self.low, self.high, self.read, self.write = low, high, read, write
        self.eastward, self.northward = eastward, northward


def advance(bands, levels, shared, scratch):
    depth_east, depth_north, mix = shared
    scaled, held = scratch

    def rise(band, n, row):
        read = bands[band].read
        return jnp.where(levels < depth_north(row), read(n, row + 1) - read(n, row), 0.0)

    def look_east(band, row, state):
        for n in range(2):
            state[band, n, row] = turn(bands[band].read(n, row), LANES - 1)

    def step_east(band, row, state):
        wet = levels < depth_east(row)
        for n in range(2):
            here, beside = bands[band].read(n, row), state[band, n, row]
            step = jnp.where(wet, beside - here, 0.0)
            state[band, n, row] = step, turn(step, 1)
            held[n, row + REACH] = beside + here

    def scale(band, row, state):
        for n in range(2):
            step, back = state.pop((band, n, row))
            drop = state.pop((band, n)) if (band, n) in state else rise(band, n, row - 1)
            state[band, n] = rise(band, n, row)
            scaled[n, row + REACH] = mix(row) * ((step - back) + (state[band, n] - drop))

    staggered([(b.low - 1, b.high + 1) for b in bands], (look_east, step_east, scale))

    def north_flow(band, n, row):
        read, northward = bands[band].read, bands[band].northward
        step = scaled[n, row + 1 + REACH] - scaled[n, row + REACH]
        both = (northward(row) + northward(row + 1)) * (read(n, row) + read(n, row + 1)) + step
        return jnp.where(levels < depth_north(row), both, 0.0)

    def look_east_again(band, row, state):
        state[band, "flow", row] = turn(bands[band].eastward(row), LANES - 1)
        for n in range(2):
            state[band, n, row] = turn(scaled[n, row + REACH], LANES - 1)

    def east_flow(band, row, state):
        wet = levels < depth_east(row)
        flow = bands[band].eastward(row) + state.pop((band, "flow", row))
        for n in range(2):
            at = row + REACH
            both = flow * held[n, at] + (state[band, n, row] - scaled[n, at])
            both = jnp.where(wet, both, 0.0)
            state[band, n, row] = both, turn(both, 1)

    def change(band, row, state):
        for n in range(2):
            east, back = state.pop((band, n, row))
            south = state.pop((band, n)) if (band, n) in state else north_flow(band, n, row - 1)
            state[band, n] = north_flow(band, n, row)
            result = bands[band].read(n, row) - ((east - back) + (state[band, n] - south))
            bands[band].write(n, row, result)

    staggered([(b.low, b.high) for b in bands], (look_east_again, east_flow, change))


def level_ids(step):
    sublane = lax.broadcasted_iota(jnp.int32, (8, LANES), 0)
    last = step == TILES - 1
    twice = last & (sublane < 8 * TILES - LEVELS)
    numbers = sublane + jnp.where(last, LEVELS - 8, 8 * step)
    return jnp.where(twice, LEVELS, numbers).astype(jnp.float32)


def spread_columns(column, rows, depth, depth_east, depth_north, mix):
    last = None
    for row in rows:
        value = column(row)
        here = jnp.broadcast_to(value[0:1, :], (8, LANES))
        depth[row + REACH] = here
        depth_east[row + REACH] = jnp.minimum(here, turn(here, LANES - 1))
        mix[row + REACH] = mixing_rate * jnp.broadcast_to(value[1:2, :], (8, LANES))
        if last is not None:
            depth_north[row + REACH - 1] = jnp.minimum(here, last)
        last = here


def contribution(levels, depth, warm, salt):
    return jnp.where(levels < depth, warm - salt_weight * salt, 0.0)


def inner_kernel(
    fields, columns, halfway, moved, forcing,
    middle, depth, depth_east, depth_north, mix, scaled, held,
):
    step = pl.program_id(0)

    @pl.when(step == 0)
    def _():
        spread_columns(lambda row: columns[row], range(BY), depth, depth_east, depth_north, mix)
        forcing[...] = jnp.zeros_like(forcing)

    levels = level_ids(step)
    shared = (
        lambda row: depth_east[row + REACH],
        lambda row: depth_north[row + REACH],
        lambda row: mix[row + REACH],
    )

    def write_middle(n, row, value):
        middle[n, row] = value
        if row < 6:
            halfway[0, n, row - 2] = value
        if row >= 34:
            halfway[0, n, row - 30] = value

    def write_moved(n, row, value):
        moved[0, n, row - 4] = value

    def eastward(row):
        return fields[0, 2, row]

    def northward(row):
        return fields[0, 3, row]

    first = Band(2, 37, lambda n, row: fields[0, n, row], write_middle, eastward, northward)
    second = Band(4, 35, lambda n, row: middle[n, row], write_moved, eastward, northward)
    advance([first], levels, shared, (scaled, held))
    advance([second], levels, shared, (scaled, held))
    for row in range(4, 36):
        forcing[row] += contribution(
            levels, depth[row + REACH], moved[0, 0, row - 4], moved[0, 1, row - 4]
        )


def surface_operator(values, couple_east, couple_north, damping):
    east = couple_east * (values - turn(values, LANES - 1))
    north = couple_north * (values - pltpu.roll(values, SURFACE - 1, 0))
    return damping * values + ((east - turn(east, 1)) + (north - pltpu.roll(north, 1, 0)))


def outer_kernel(
    low_fields, high_fields, columns, up, down, up_extra, down_extra, halfway, inner_forcing,
    moved, basis, moments,
    middle, beyond, depth, depth_east, depth_north, mix, scaled, held, forcing, surface, depths, dampings,
):
    step = pl.program_id(0)

    def column(row):
        if row < 0:
            return up_extra[row + REACH, 0]
        if row >= BY:
            return down_extra[row - BY, 0]
        return columns[row]

    rows = range(-REACH, BY + REACH)

    @pl.when(step == 0)
    def _():
        spread_columns(column, rows, depth, depth_east, depth_north, mix)
        forcing[...] = jnp.zeros_like(forcing)

    levels = level_ids(step)
    shared = (
        lambda row: depth_east[row + REACH],
        lambda row: depth_north[row + REACH],
        lambda row: mix[row + REACH],
    )

    def field(number, row):
        if row < 0:
            return up[0, REACH * number + row + REACH]
        if row >= BY:
            return down[0, REACH * number + row - BY]
        return low_fields[0, number, row] if row < 10 else high_fields[0, number, row - 30]

    def read_middle(n, row):
        if 2 <= row < 6:
            return halfway[0, n, row - 2]
        if 34 <= row < 38:
            return halfway[0, n, row - 30]
        return middle[n, row + REACH]

    def write_middle(n, row, value):
        middle[n, row + REACH] = value

    def write_beyond(n, row, value):
        beyond[n, row + REACH] = value
        if 0 <= row < 4:
            moved[0, n, row] = value
        if 36 <= row < BY:
            moved[0, n, row - 32] = value

    def eastward(row):
        return field(2, row)

    def northward(row):
        return field(3, row)

    bands = [Band(low, high, field, write_middle, eastward, northward) for low, high in ((-5, 1), (38, 44))]
    advance(bands, levels, shared, (scaled, held))
    bands = [
        Band(low, high, read_middle, write_beyond, eastward, northward) for low, high in ((-3, 3), (36, 42))
    ]
    advance(bands, levels, shared, (scaled, held))
    for row in (*range(-3, 4), *range(36, 43)):
        at = row + REACH
        forcing[at] += contribution(levels, depth[at], beyond[0, at], beyond[1, at])

    @pl.when(step == TILES - 1)
    def _():
        surface[...] = jnp.zeros_like(surface)
        for row in range(-3, 43):
            part = inner_forcing[row] if 4 <= row < 36 else forcing[row + REACH]
            total = jnp.sum(part, axis=0, keepdims=True)
            surface[row + 8 : row + 9, :] = total * (1.0 / math.sqrt(LEVELS))
        depths[...] = jnp.zeros_like(depths)
        dampings[...] = jnp.zeros_like(dampings)
        for row in rows:
            value = column(row)
            depths[row + 8 : row + 9, :] = value[0:1, :]
            dampings[row + 8 : row + 9, :] = value[2:3, :]
        here = depths[...]
        couple_east = jnp.minimum(here, turn(here, LANES - 1)) * (1.0 / LEVELS)
        couple_north = jnp.minimum(here, pltpu.roll(here, SURFACE - 1, 0)) * (1.0 / LEVELS)
        diagonal = dampings[...]
        powers = [surface[...]]
        for _ in range(3):
            powers.append(surface_operator(powers[-1], couple_east, couple_north, diagonal))
        row_id = lax.broadcasted_iota(jnp.int32, (SURFACE, LANES), 0)
        lane_id = lax.broadcasted_iota(jnp.int32, (SURFACE, LANES), 1)
        own = (row_id >= 8) & (row_id < 8 + BY) & (lane_id >= BASE) & (lane_id < BASE + WIDE)
        moments[...] = jnp.zeros_like(moments)
        for k in range(6):
            product = jnp.where(own, powers[k // 2] * powers[(k + 1) // 2], 0.0)
            moments[k : k + 1, :] = jnp.sum(product, axis=0, keepdims=True)
        for k in range(3):
            basis[k] = turn(powers[k], LANES - BASE)[8 : 8 + BY, :]


def to_slots(numbers, start, rows, load, block_list, out):
    lane = lane_ids()
    swap = slot_swap(block_list)
    cells = [c for t in numbers for c in range(t * LANES, min((t + 1) * LANES, CELLS))]
    wanted = sorted({c // BX - p for c in cells for p in range(2)})

    def work(block, last):
        for n in range(2):
            turned = {}

            def strip(row, n=n):
                return load(block, n, min(max(row, rows[0]), rows[1]))

            def back(r, strip=strip, turned=turned):
                if r not in turned:
                    value = jnp.where(lane < BASE + BX, strip(r), strip(r + 1))
                    turned[r] = turn(value, BX * r - BASE)
                return turned[r]

            for r in wanted:
                back(r)
            for number in numbers:
                for position in range(2):
                    slot = swap if position == 0 else 1 - swap
                    first, end = number * LANES, min((number + 1) * LANES, CELLS)
                    parts = []
                    for row in range(first // BX, (end - 1) // BX + 1):
                        low = max(row * BX, first)
                        parts.append((low, min((row + 1) * BX, end) - low, back(row - position)))
                    value = merge(parts, lane)[:, 0 : end - first]
                    if last:
                        rest = value[8 * TILES - LEVELS : 8]
                        out[slot, 8 * TILES - 8 : LEVELS, n, first - start : end - start] = rest
                    else:
                        out[slot, pl.ds(8 * block, 8), n, first - start : end - start] = value

    def body(block, carry):
        work(block, False)
        return carry

    lax.fori_loop(0, TILES - 1, body, 0)
    work(TILES - 1, True)


def inner_slots_kernel(block_list, moved, out, cells, semaphore):
    to_slots(range(2, 12), 2 * LANES, (4, 35), lambda block, n, row: moved[block, n, row - 4], block_list, cells)
    copy = pltpu.make_async_copy(cells, out.at[:, :, :, 2 * LANES : 12 * LANES], semaphore)
    copy.start()
    copy.wait()


def outer_slots_kernel(block_list, moved, edges, inner, out, low, high, low_semaphore, high_semaphore):
    def load(block, n, row):
        if 4 <= row < 36:
            return moved[block, n, row - 4]
        return edges[block, n, row if row < 4 else row - 32]

    to_slots((0, 1), 0, (0, BY - 1), load, block_list, low)
    low_copy = pltpu.make_async_copy(low, out.at[:, :, :, 0 : 2 * LANES], low_semaphore)
    low_copy.start()
    to_slots((12, 13, 14), 12 * LANES, (0, BY - 1), load, block_list, high)
    high_copy = pltpu.make_async_copy(high, out.at[:, :, :, 12 * LANES : CELLS], high_semaphore)
    high_copy.start()
    low_copy.wait()
    high_copy.wait()


def finish_kernel(first, second, third, fourth, basis, out):
    moments = (first[...] + second[...]) + (third[...] + fourth[...])
    totals = jnp.sum(moments, axis=1, keepdims=True)
    m = [totals[k : k + 1, :] for k in range(6)]
    low10 = m[2] / m[1]
    low20 = m[3] / m[1]
    pivot1 = m[3] - low10 * m[2]
    part21 = m[4] - low20 * m[2]
    low21 = part21 / pivot1
    pivot2 = m[5] - low20 * m[3] - low21 * part21
    y1 = m[1] - low10 * m[0]
    y2 = m[2] - low20 * m[0] - low21 * y1
    z2 = y2 / pivot2
    z1 = y1 / pivot1 - low21 * z2
    z0 = m[0] / m[1] - low10 * z1 - low20 * z2
    value = z0 * basis[0] + z1 * basis[1] + z2 * basis[2]
    out[...] = value[:, 0:WIDE]


def quad(values, axis, partner):
    count = lax.axis_size(axis)
    others = [
        lax.ppermute(values, axis, [(i, partner(i, turn)) for i in range(count)])
        for turn in range(1, 4)
    ]
    return [values, *others]


def quad_sum(values, axis, partner):
    four = quad(values, axis, partner)
    return (four[0] + four[1]) + (four[2] + four[3])


def terms_over_devices(values):
    values = values + lax.ppermute(values, "gy", [(i, i ^ 1) for i in range(lax.axis_size("gy"))])
    values = quad_sum(values, "gy", lambda i, turn: i ^ (2 * turn))
    values = quad_sum(values, "gx", lambda i, turn: i ^ turn)
    return quad(values, "gx", lambda i, turn: i ^ (4 * turn))


def held_in_vmem(arrays):
    return [pltpu.with_memory_space_constraint(a, pltpu.VMEM) for a in arrays]


def vmem(kind):
    return pltpu.VMEM(kind.shape, kind.dtype)


def whole(shape):
    return pl.BlockSpec(shape, lambda k: (0,) * len(shape))


def per_device(block_list, wet_levels, mixing, velocity, tracers, damping):
    f32 = jnp.float32
    slots, fields_each, levels, cells = tracers.shape
    params = pltpu.CompilerParams(
        dimension_semantics=("arbitrary",), vmem_limit_bytes=40 * 1024 * 1024
    )

    def tiles(*shape):
        zeros = (0,) * (len(shape) + 2)
        return (
            pl.BlockSpec((1, *shape, 8, LANES), lambda k: (k, *zeros)),
            jax.ShapeDtypeStruct((TILES, *shape, 8, LANES), f32),
        )

    rows_block, rows_type = tiles(NS)
    _, columns_type = tiles(EW)
    rows_extra = pl.BlockSpec((TILES, 1, 8, LANES), lambda k: (0, NS - 1, 0, 0))
    in_vmem = pl.BlockSpec(memory_space=pltpu.VMEM)
    own_specs = [pl.BlockSpec(memory_space=pltpu.SMEM)] + [in_vmem] * 5
    own = (block_list, *held_in_vmem((wet_levels, mixing, damping, velocity, tracers)))
    whole_params = pltpu.CompilerParams(vmem_limit_bytes=40 * 1024 * 1024)

    east, west = pl.pallas_call(
        columns_kernel,
        in_specs=own_specs,
        out_specs=[in_vmem] * 2,
        out_shape=[vmem(columns_type)] * 2,
        scratch_shapes=[pltpu.VMEM((BY, LANES), f32)],
        compiler_params=whole_params,
        name="pack_columns",
    )(*own)
    columns_total = lax.axis_size("gx")
    from_west = lax.ppermute(east, "gx", [(i, (i + 1) % columns_total) for i in range(columns_total)])
    from_east = lax.ppermute(west, "gx", [((i + 1) % columns_total, i) for i in range(columns_total)])

    fields_block, fields_type = tiles(4, BY)
    column_shape = (BY, 8, LANES)
    column_type = jax.ShapeDtypeStruct(column_shape, f32)
    own_strips = pl.pallas_call(
        strips_kernel,
        in_specs=own_specs,
        out_specs=[in_vmem] * 2,
        out_shape=[vmem(fields_type), vmem(column_type)],
        scratch_shapes=[pltpu.VMEM((BY, LANES), f32)],
        compiler_params=whole_params,
        cost_estimate=pl.CostEstimate(flops=30_000_000, bytes_accessed=9_000_000, transcendentals=0),
        name="strips",
    )(*own)
    with_halos = held_in_vmem((*own_strips, from_west, from_east))
    up, down = pl.pallas_call(
        row_message_kernel,
        in_specs=[in_vmem] * 4,
        out_specs=[in_vmem] * 2,
        out_shape=[vmem(rows_type)] * 2,
        scratch_shapes=[pltpu.VMEM((BY, LANES), f32)] * 2,
        compiler_params=whole_params,
        name="row_message",
    )(*with_halos)
    fields, columns = pl.pallas_call(
        halo_kernel,
        in_specs=[in_vmem] * 4,
        out_specs=[in_vmem] * 2,
        out_shape=[vmem(fields_type), vmem(column_type)],
        scratch_shapes=[pltpu.VMEM((BY, LANES), f32)] * 2,
        compiler_params=whole_params,
        cost_estimate=pl.CostEstimate(flops=30_000_000, bytes_accessed=9_000_000, transcendentals=0),
        name="halos",
    )(*with_halos)
    rows_total = lax.axis_size("gy")
    from_below = lax.ppermute(up, "gy", [(i, i + 1) for i in range(rows_total - 1)])
    from_above = lax.ppermute(down, "gy", [(i + 1, i) for i in range(rows_total - 1)])

    row_store = pltpu.VMEM((ROWS, 8, LANES), f32)
    pair_store = pltpu.VMEM((2, ROWS, 8, LANES), f32)
    halfway_block, halfway_type = tiles(2, 8)
    moved_block, moved_type = tiles(2, 32)
    halfway, moved, forcing = pl.pallas_call(
        inner_kernel,
        grid=(TILES,),
        in_specs=[fields_block, whole(column_shape)],
        out_specs=[halfway_block, moved_block, whole(column_shape)],
        out_shape=[halfway_type, moved_type, jax.ShapeDtypeStruct(column_shape, f32)],
        scratch_shapes=[pair_store] + [row_store] * 4 + [pair_store] * 2,
        compiler_params=params,
        cost_estimate=pl.CostEstimate(flops=60_000_000, bytes_accessed=10_000_000, transcendentals=0),
        name="inner_rows",
    )(fields, columns)

    slots_type = jax.ShapeDtypeStruct((slots, levels, fields_each, cells), f32)
    inner_slots = pl.pallas_call(
        inner_slots_kernel,
        in_specs=[pl.BlockSpec(memory_space=pltpu.SMEM), in_vmem],
        out_specs=pl.BlockSpec(memory_space=pl.ANY),
        out_shape=slots_type,
        scratch_shapes=[
            pltpu.VMEM((slots, levels, fields_each, 10 * LANES), f32),
            pltpu.SemaphoreType.DMA,
        ],
        compiler_params=whole_params,
        cost_estimate=pl.CostEstimate(flops=20_000_000, bytes_accessed=6_000_000, transcendentals=0),
        name="inner_slots",
    )(block_list, moved)
    inner_slots, forcing = lax.optimization_barrier((inner_slots, forcing))

    low_block = pl.BlockSpec((1, 4, 10, 8, LANES), lambda k: (k, 0, 0, 0, 0))
    high_block = pl.BlockSpec((1, 4, 10, 8, LANES), lambda k: (k, 0, 3, 0, 0))
    edges, basis, moments = pl.pallas_call(
        outer_kernel,
        grid=(TILES,),
        in_specs=[low_block, high_block, whole(column_shape), rows_block, rows_block]
        + [rows_extra, rows_extra, halfway_block, whole(column_shape)],
        out_specs=[halfway_block, whole((3, BY, LANES)), whole((8, LANES))],
        out_shape=[
            halfway_type,
            jax.ShapeDtypeStruct((3, BY, LANES), f32),
            jax.ShapeDtypeStruct((8, LANES), f32),
        ],
        scratch_shapes=[pair_store] * 2
        + [row_store] * 4
        + [pair_store] * 2
        + [row_store]
        + [pltpu.VMEM((SURFACE, LANES), f32)] * 3,
        compiler_params=params,
        name="outer_rows",
    )(fields, fields, columns, from_below, from_above, from_below, from_above, halfway, forcing)

    new_tracers = pl.pallas_call(
        outer_slots_kernel,
        in_specs=[pl.BlockSpec(memory_space=pltpu.SMEM), in_vmem, in_vmem]
        + [pl.BlockSpec(memory_space=pl.ANY)],
        out_specs=pl.BlockSpec(memory_space=pl.ANY),
        out_shape=slots_type,
        scratch_shapes=[
            pltpu.VMEM((slots, levels, fields_each, 2 * LANES), f32),
            pltpu.VMEM((slots, levels, fields_each, cells - 12 * LANES), f32),
            pltpu.SemaphoreType.DMA,
            pltpu.SemaphoreType.DMA,
        ],
        input_output_aliases={3: 0},
        compiler_params=whole_params,
        cost_estimate=pl.CostEstimate(flops=2_000_000, bytes_accessed=2_000_000, transcendentals=0),
        name="outer_slots",
    )(block_list, moved, edges, inner_slots)
    new_tracers = jnp.transpose(new_tracers, (0, 2, 1, 3))

    moments = terms_over_devices(moments)
    height = pl.pallas_call(
        finish_kernel,
        out_shape=jax.ShapeDtypeStruct((BY, WIDE), f32),
        name="finish",
    )(*moments, basis)
    return (new_tracers, height)


def solution(mesh):
    return jax.shard_map(
        per_device,
        mesh=mesh,
        in_specs=(
            P(("gx", "gy")),
            P(("gx", "gy"), None),
            P(("gx", "gy"), None),
            P(("gx", "gy"), None, None, None),
            P(("gx", "gy"), None, None, None),
            P("gy", "gx"),
        ),
        out_specs=(P(("gx", "gy"), None, None, None), P("gy", "gx")),
        check_vma=False,
    )
```

```python
import functools
import math

import jax
import jax.numpy as jnp
from jax import lax
from jax.experimental import pallas as pl
from jax.experimental.pallas import tpu as pltpu
from jax.sharding import PartitionSpec as P

BX = 45
BY = 40
CELLS = BX * BY
LEVELS = 62
LANES = 128
TILES = 8
REACH = 7
ROWS = BY + 2 * REACH
PARTS = 2
AHEAD = 26
BASE = 8
WIDE = 2 * BX
NS = 29
EW = 13
SURFACE = 56

advect_rate = 0.25
mixing_rate = 0.015
salt_weight = 0.8


def lane_ids():
    return lax.broadcasted_iota(jnp.int32, (8, LANES), 1)


def merge(parts, lane):
    flat = []
    for low, width, value in parts:
        low %= LANES
        if low + width > LANES:
            flat.append((low, value))
            flat.append((0, value))
        else:
            flat.append((low, value))
    flat.sort(key=lambda part: part[0])
    result = flat[0][1]
    last = result
    for low, value in flat[1:]:
        if value is last:
            continue
        result = jnp.where(lane >= low, value, result)
        last = value
    return result


def turn(value, shift):
    shift %= LANES
    return pltpu.roll(value, shift, 1) if shift else value


class Source:
    def __init__(self, load):
        self.load = load
        self.kept = {}

    def tile(self, *key):
        if key not in self.kept:
            self.kept[key] = self.load(*key)
        return self.kept[key]

    def cells(self, position, start, width):
        parts = []
        at = start
        while at < start + width:
            number = at // LANES
            end = min(start + width, (number + 1) * LANES)
            parts.append((at, end - at, self.tile(position, number)))
            at = end
        return parts


def pack_columns(source, lane):
    east, west = [], []
    for group in range(3):
        rows = range(17 * group, min(17 * group + 17, BY))
        east.append(merge([c for r in rows for c in source.cells(1, BX * r + BX - REACH, REACH)], lane))
        west.append(merge([c for r in rows for c in source.cells(0, BX * r, REACH)], lane))
    return east, west


def strip_rows(source, lane):
    turned = {}

    def combined(r):
        if r not in turned:
            parts = source.cells(0, BX * r, BX) if r >= 0 else []
            if r + 1 < BY:
                parts += source.cells(1, BX * (r + 1), BX)
            turned[r] = turn(merge(parts, lane), BASE - BX * r)
        return turned[r]

    for r in range(-1, BY):
        combined(r)
    for row in range(BY):
        yield row, jnp.where(lane < BASE + BX, combined(row), combined(row - 1))


def beside_rows(rows, west, east, lane):
    turned = {}

    def combined(r):
        if r not in turned:
            low, high = (BX * r - REACH) % LANES, BX * (r + 2) % LANES
            if not 0 <= r - 1 < BY:
                value = east((r + 2) // 17)
            elif not 0 <= r + 2 < BY:
                value = west((r - 1) // 17)
            elif low < high:
                inside = lane < high if high + REACH <= LANES else (lane >= low) & (lane < high)
                value = jnp.where(inside, west((r - 1) // 17), east((r + 2) // 17))
            else:
                inside = lane < low if low + REACH <= LANES else (lane >= high) & (lane < low)
                value = jnp.where(inside, east((r + 2) // 17), west((r - 1) // 17))
            turned[r] = turn(value, BASE - BX * r)
        return turned[r]

    for r in sorted({row + 1 for row in rows} | {row - 2 for row in rows}):
        combined(r)
    for row in rows:
        yield row, combined(row + 1), combined(row - 2)


def slot_swap(block_list):
    first = block_list[0]
    return jnp.where(first >= 0, first & 1, 1 - (block_list[1] & 1))


def over_level_blocks(work):
    def body(block, carry):
        work(block, pl.ds(pl.multiple_of(8 * block, 8), 8))
        return carry

    lax.fori_loop(0, TILES - 1, body, 0)
    work(TILES - 1, pl.ds(LEVELS - 8, 8))


def field_loader(ref, which, levels, swap):
    def load(position, number):
        slot = swap if position == 0 else 1 - swap
        if number < 14:
            return ref[slot, which, levels, number * LANES : (number + 1) * LANES]
        return turn(ref[slot, which, levels, CELLS - LANES : CELLS], CELLS % LANES)

    return load


def column_loader(wet_levels, mixing, swap):
    def load(position, number):
        slot = swap if position == 0 else 1 - swap
        low = number * LANES if number < 14 else CELLS - LANES
        both = wet_levels[:, low : low + LANES].astype(jnp.float32)
        depth = jnp.where(slot == 0, both[0:1, :], both[1:2, :])
        both = mixing[:, low : low + LANES]
        mix = jnp.where(slot == 0, both[0:1, :], both[1:2, :])
        sublane = lax.broadcasted_iota(jnp.int32, (8, LANES), 0)
        value = jnp.where(
            sublane == 0, jnp.broadcast_to(depth, (8, LANES)), jnp.broadcast_to(mix, (8, LANES))
        )
        return value if number < 14 else turn(value, CELLS % LANES)

    return load


def columns_kernel(block_list, wet_levels, mixing, damping, velocity, tracers, east, west, padded):
    lane = lane_ids()
    swap = slot_swap(block_list)

    def work(block, levels):
        for field in range(4):
            ref = tracers if field < 2 else velocity
            easts, wests = pack_columns(Source(field_loader(ref, field % 2, levels, swap)), lane)
            scale = 1.0 if field < 2 else 0.25 * advect_rate
            for number in range(3):
                east[block, 3 * field + number] = easts[number] * scale
                west[block, 3 * field + number] = wests[number] * scale

    over_level_blocks(work)
    easts, wests = pack_columns(Source(column_loader(wet_levels, mixing, swap)), lane)
    padded[...] = jnp.zeros_like(padded)
    padded[:, 0:WIDE] = damping[...]
    tiles = [padded[8 * j : 8 * j + 8, :] for j in range(5)]
    easts.append(merge([(2 * j, 2, turn(t, 2 * j - WIDE + 2)) for j, t in enumerate(tiles)], lane))
    wests.append(merge([(2 * j, 2, turn(t, 2 * j)) for j, t in enumerate(tiles)], lane))
    for block in range(TILES):
        east[block, EW - 1] = easts[min(block, 3)]
        west[block, EW - 1] = wests[min(block, 3)]


def strips_kernel(block_list, wet_levels, mixing, damping, velocity, tracers, fields, columns, padded):
    lane = lane_ids()
    swap = slot_swap(block_list)
    padded[...] = jnp.zeros_like(padded)
    padded[:, 0:WIDE] = damping[...]
    for j in range(5):
        padded[8 * j : 8 * j + 8, :] = turn(padded[8 * j : 8 * j + 8, :], BASE)
    sublane = lax.broadcasted_iota(jnp.int32, (8, LANES), 0)
    for row, value in strip_rows(Source(column_loader(wet_levels, mixing, swap)), lane):
        damp = jnp.broadcast_to(padded[row : row + 1, :], (8, LANES))
        columns[row] = jnp.where(sublane == 2, damp, value)

    def work(block, levels):
        for field in range(4):
            ref = tracers if field < 2 else velocity
            for row, value in strip_rows(Source(field_loader(ref, field % 2, levels, swap)), lane):
                fields[block, field, row] = value if field < 2 else (0.25 * advect_rate) * value

    over_level_blocks(work)


def place_halos(own_fields, own_columns, from_west, from_east, low_damp, high_damp, rows, put):
    lane = lane_ids()
    sublane = lax.broadcasted_iota(jnp.int32, (8, LANES), 0)
    for j in range(5):
        low_damp[8 * j : 8 * j + 8, :] = turn(from_west[3, EW - 1], BASE - 2 - 2 * j)
        high_damp[8 * j : 8 * j + 8, :] = turn(from_east[3, EW - 1], BASE + WIDE - 2 * j)
    sides = beside_rows(rows, lambda t: from_west[t, EW - 1], lambda t: from_east[t, EW - 1], lane)
    for row, west, east in sides:
        west = jnp.where(sublane == 2, jnp.broadcast_to(low_damp[row : row + 1, :], (8, LANES)), west)
        east = jnp.where(sublane == 2, jnp.broadcast_to(high_damp[row : row + 1, :], (8, LANES)), east)
        value = jnp.where(lane < BASE, west, own_columns[row])
        put(0, 4, row, jnp.where(lane < BASE + WIDE, value, east))

    def work(block, carry):
        for field in range(4):
            sides = beside_rows(
                rows,
                lambda t, field=field: from_west[block, 3 * field + t],
                lambda t, field=field: from_east[block, 3 * field + t],
                lane,
            )
            for row, west, east in sides:
                value = jnp.where(lane < BASE, west, own_fields[block, field, row])
                put(block, field, row, jnp.where(lane < BASE + WIDE, value, east))
        return carry

    lax.fori_loop(0, TILES, work, 0)


def row_message_kernel(own_fields, own_columns, from_west, from_east, up, down, low_damp, high_damp):
    def put(block, field, row, value):
        target, row = (down, row) if row < REACH else (up, row - (BY - REACH))
        if field == 4:
            target[row, NS - 1] = value
        else:
            target[block, REACH * field + row] = value

    up[TILES - 1, NS - 1] = jnp.zeros((8, LANES), jnp.float32)
    down[TILES - 1, NS - 1] = jnp.zeros((8, LANES), jnp.float32)
    rows = (*range(REACH), *range(BY - REACH, BY))
    place_halos(own_fields, own_columns, from_west, from_east, low_damp, high_damp, rows, put)


def halo_kernel(own_fields, own_columns, from_west, from_east, fields, columns, low_damp, high_damp):
    def put(block, field, row, value):
        if field == 4:
            columns[row] = value
        else:
            fields[block, field, row] = value

    place_halos(own_fields, own_columns, from_west, from_east, low_damp, high_damp, range(BY), put)


def staggered(spans, phases):
    state = {}
    length = max(high - low + 1 for low, high in spans)
    ahead = min(AHEAD, length)
    for time in range(length + ahead * (len(phases) - 1)):
        for number in reversed(range(len(phases))):
            for span, (low, high) in enumerate(spans):
                row = low + time - number * ahead
                if low <= row <= high:
                    phases[number](span, row, state)


class Band:
    def __init__(self, low, high, read, write, eastward, northward, levels, part=0):
        self.low, self.high, self.read, self.write = low, high, read, write
        self.eastward, self.northward = eastward, northward
        self.levels, self.part = levels, 2 * part


def advance(bands, shared, scratch):
    depth_east, depth_north, mix = shared
    scaled, held = scratch

    def rise(band, n, row):
        read = bands[band].read
        return jnp.where(bands[band].levels < depth_north(row), read(n, row + 1) - read(n, row), 0.0)

    def look_east(band, row, state):
        for n in range(2):
            state[band, n, row] = turn(bands[band].read(n, row), LANES - 1)

    def step_east(band, row, state):
        wet = bands[band].levels < depth_east(row)
        for n in range(2):
            here, beside = bands[band].read(n, row), state[band, n, row]
            step = jnp.where(wet, beside - here, 0.0)
            state[band, n, row] = step, turn(step, 1)
            held[bands[band].part + n, row + REACH] = beside + here

    def scale(band, row, state):
        for n in range(2):
            step, back = state.pop((band, n, row))
            drop = state.pop((band, n)) if (band, n) in state else rise(band, n, row - 1)
            state[band, n] = rise(band, n, row)
            scaled[bands[band].part + n, row + REACH] = mix(row) * ((step - back) + (state[band, n] - drop))

    staggered([(b.low - 1, b.high + 1) for b in bands], (look_east, step_east, scale))

    def north_flow(band, n, row):
        read, northward = bands[band].read, bands[band].northward
        step = scaled[bands[band].part + n, row + 1 + REACH] - scaled[bands[band].part + n, row + REACH]
        both = (northward(row) + northward(row + 1)) * (read(n, row) + read(n, row + 1)) + step
        return jnp.where(bands[band].levels < depth_north(row), both, 0.0)

    def look_east_again(band, row, state):
        state[band, "flow", row] = turn(bands[band].eastward(row), LANES - 1)
        for n in range(2):
            state[band, n, row] = turn(scaled[bands[band].part + n, row + REACH], LANES - 1)

    def east_flow(band, row, state):
        wet = bands[band].levels < depth_east(row)
        flow = bands[band].eastward(row) + state.pop((band, "flow", row))
        for n in range(2):
            at = row + REACH
            both = flow * held[bands[band].part + n, at] + (state[band, n, row] - scaled[bands[band].part + n, at])
            both = jnp.where(wet, both, 0.0)
            state[band, n, row] = both, turn(both, 1)

    def change(band, row, state):
        for n in range(2):
            east, back = state.pop((band, n, row))
            south = state.pop((band, n)) if (band, n) in state else north_flow(band, n, row - 1)
            state[band, n] = north_flow(band, n, row)
            result = bands[band].read(n, row) - ((east - back) + (state[band, n] - south))
            bands[band].write(n, row, result)

    staggered([(b.low, b.high) for b in bands], (look_east_again, east_flow, change))


def level_ids(step):
    sublane = lax.broadcasted_iota(jnp.int32, (8, LANES), 0)
    last = step == TILES - 1
    twice = last & (sublane < 8 * TILES - LEVELS)
    numbers = sublane + jnp.where(last, LEVELS - 8, 8 * step)
    return jnp.where(twice, LEVELS, numbers).astype(jnp.float32)


def spread_columns(column, rows, depth, depth_east, depth_north, mix):
    last = None
    for row in rows:
        value = column(row)
        here = jnp.broadcast_to(value[0:1, :], (8, LANES))
        depth[row + REACH] = here
        depth_east[row + REACH] = jnp.minimum(here, turn(here, LANES - 1))
        mix[row + REACH] = mixing_rate * jnp.broadcast_to(value[1:2, :], (8, LANES))
        if last is not None:
            depth_north[row + REACH - 1] = jnp.minimum(here, last)
        last = here


def contribution(levels, depth, warm, salt):
    return jnp.where(levels < depth, warm - salt_weight * salt, 0.0)


def inner_kernel(
    fields, columns, halfway, moved, forcing,
    middle, depth, depth_east, depth_north, mix, scaled, held,
):
    step = pl.program_id(0)

    @pl.when(step == 0)
    def _():
        spread_columns(lambda row: columns[row], range(BY), depth, depth_east, depth_north, mix)
        forcing[...] = jnp.zeros_like(forcing)

    levels = level_ids(step)
    shared = (
        lambda row: depth_east[row + REACH],
        lambda row: depth_north[row + REACH],
        lambda row: mix[row + REACH],
    )

    def write_middle(n, row, value):
        middle[n, row] = value
        if row < 6:
            halfway[0, n, row - 2] = value
        if row >= 34:
            halfway[0, n, row - 30] = value

    def write_moved(n, row, value):
        moved[0, n, row - 4] = value

    def eastward(row):
        return fields[0, 2, row]

    def northward(row):
        return fields[0, 3, row]

    first = Band(2, 37, lambda n, row: fields[0, n, row], write_middle, eastward, northward, levels)
    second = Band(4, 35, lambda n, row: middle[n, row], write_moved, eastward, northward, levels)
    advance([first], shared, (scaled, held))
    advance([second], shared, (scaled, held))
    for row in range(4, 36):
        forcing[row] += contribution(
            levels, depth[row + REACH], moved[0, 0, row - 4], moved[0, 1, row - 4]
        )


def surface_operator(values, couple_east, couple_north, damping):
    east = couple_east * (values - turn(values, LANES - 1))
    north = couple_north * (values - pltpu.roll(values, SURFACE - 1, 0))
    return damping * values + ((east - turn(east, 1)) + (north - pltpu.roll(north, 1, 0)))


def outer_kernel(
    low_fields, high_fields, columns, up, down, up_extra, down_extra, halfway, inner_forcing,
    moved, basis, moments,
    middle, beyond, depth, depth_east, depth_north, mix, scaled, held, forcing, surface, depths, dampings,
):
    step = pl.program_id(0)

    def column(row):
        if row < 0:
            return up_extra[row + REACH, 0]
        if row >= BY:
            return down_extra[row - BY, 0]
        return columns[row]

    rows = range(-REACH, BY + REACH)

    @pl.when(step == 0)
    def _():
        spread_columns(column, rows, depth, depth_east, depth_north, mix)
        forcing[...] = jnp.zeros_like(forcing)

    shared = (
        lambda row: depth_east[row + REACH],
        lambda row: depth_north[row + REACH],
        lambda row: mix[row + REACH],
    )
    first, second = [], []
    for part in range(PARTS):
        levels = level_ids(PARTS * step + part)

        def field(number, row, part=part):
            if row < 0:
                return up[part, REACH * number + row + REACH]
            if row >= BY:
                return down[part, REACH * number + row - BY]
            return low_fields[part, number, row] if row < 10 else high_fields[part, number, row - 30]

        def read_middle(n, row, part=part):
            if 2 <= row < 6:
                return halfway[part, n, row - 2]
            if 34 <= row < 38:
                return halfway[part, n, row - 30]
            return middle[2 * part + n, row + REACH]

        def write_middle(n, row, value, part=part):
            middle[2 * part + n, row + REACH] = value

        def write_beyond(n, row, value, part=part):
            beyond[2 * part + n, row + REACH] = value
            if 0 <= row < 4:
                moved[part, n, row] = value
            if 36 <= row < BY:
                moved[part, n, row - 32] = value

        flows = (functools.partial(field, 2), functools.partial(field, 3), levels, part)
        first += [Band(low, high, field, write_middle, *flows) for low, high in ((-5, 1), (38, 44))]
        second += [Band(low, high, read_middle, write_beyond, *flows) for low, high in ((-3, 3), (36, 42))]
    advance(first, shared, (scaled, held))
    advance(second, shared, (scaled, held))
    for row in (*range(-3, 4), *range(36, 43)):
        at = row + REACH
        for part in range(PARTS):
            forcing[at] += contribution(
                second[2 * part].levels, depth[at], beyond[2 * part, at], beyond[2 * part + 1, at]
            )

    @pl.when(step == TILES // PARTS - 1)
    def _():
        surface[...] = jnp.zeros_like(surface)
        for row in range(-3, 43):
            part = inner_forcing[row] if 4 <= row < 36 else forcing[row + REACH]
            total = jnp.sum(part, axis=0, keepdims=True)
            surface[row + 8 : row + 9, :] = total * (1.0 / math.sqrt(LEVELS))
        depths[...] = jnp.zeros_like(depths)
        dampings[...] = jnp.zeros_like(dampings)
        for row in rows:
            value = column(row)
            depths[row + 8 : row + 9, :] = value[0:1, :]
            dampings[row + 8 : row + 9, :] = value[2:3, :]
        here = depths[...]
        couple_east = jnp.minimum(here, turn(here, LANES - 1)) * (1.0 / LEVELS)
        couple_north = jnp.minimum(here, pltpu.roll(here, SURFACE - 1, 0)) * (1.0 / LEVELS)
        diagonal = dampings[...]
        powers = [surface[...]]
        for _ in range(3):
            powers.append(surface_operator(powers[-1], couple_east, couple_north, diagonal))
        row_id = lax.broadcasted_iota(jnp.int32, (SURFACE, LANES), 0)
        lane_id = lax.broadcasted_iota(jnp.int32, (SURFACE, LANES), 1)
        own = (row_id >= 8) & (row_id < 8 + BY) & (lane_id >= BASE) & (lane_id < BASE + WIDE)
        moments[...] = jnp.zeros_like(moments)
        for k in range(6):
            product = jnp.where(own, powers[k // 2] * powers[(k + 1) // 2], 0.0)
            moments[k : k + 1, :] = jnp.sum(product, axis=0, keepdims=True)
        for k in range(3):
            basis[k] = turn(powers[k], LANES - BASE)[8 : 8 + BY, :]


def to_slots(numbers, start, rows, load, block_list, out):
    lane = lane_ids()
    swap = slot_swap(block_list)
    cells = [c for t in numbers for c in range(t * LANES, min((t + 1) * LANES, CELLS))]
    wanted = sorted({c // BX - p for c in cells for p in range(2)})

    def work(block, last):
        for n in range(2):
            turned = {}

            def strip(row, n=n):
                return load(block, n, min(max(row, rows[0]), rows[1]))

            def back(r, strip=strip, turned=turned):
                if r not in turned:
                    value = jnp.where(lane < BASE + BX, strip(r), strip(r + 1))
                    turned[r] = turn(value, BX * r - BASE)
                return turned[r]

            for r in wanted:
                back(r)
            for number in numbers:
                for position in range(2):
                    slot = swap if position == 0 else 1 - swap
                    first, end = number * LANES, min((number + 1) * LANES, CELLS)
                    parts = []
                    for row in range(first // BX, (end - 1) // BX + 1):
                        low = max(row * BX, first)
                        parts.append((low, min((row + 1) * BX, end) - low, back(row - position)))
                    value = merge(parts, lane)[:, 0 : end - first]
                    if last:
                        rest = value[8 * TILES - LEVELS : 8]
                        out[slot, 8 * TILES - 8 : LEVELS, n, first - start : end - start] = rest
                    else:
                        out[slot, pl.ds(8 * block, 8), n, first - start : end - start] = value

    def body(block, carry):
        work(block, False)
        return carry

    lax.fori_loop(0, TILES - 1, body, 0)
    work(TILES - 1, True)


def inner_slots_kernel(block_list, moved, out, cells, semaphore):
    to_slots(range(2, 12), 2 * LANES, (4, 35), lambda block, n, row: moved[block, n, row - 4], block_list, cells)
    copy = pltpu.make_async_copy(cells, out.at[:, :, :, 2 * LANES : 12 * LANES], semaphore)
    copy.start()
    copy.wait()


def outer_slots_kernel(numbers, block_list, moved, edges, inner, out, cells, semaphore):
    def load(block, n, row):
        if 4 <= row < 36:
            return moved[block, n, row - 4]
        return edges[block, n, row if row < 4 else row - 32]

    start, end = numbers[0] * LANES, min((numbers[-1] + 1) * LANES, CELLS)
    to_slots(numbers, start, (0, BY - 1), load, block_list, cells)
    copy = pltpu.make_async_copy(cells, out.at[:, :, :, start:end], semaphore)
    copy.start()
    copy.wait()


def finish_kernel(first, second, third, fourth, basis, out):
    moments = (first[...] + second[...]) + (third[...] + fourth[...])
    totals = jnp.sum(moments, axis=1, keepdims=True)
    m = [totals[k : k + 1, :] for k in range(6)]
    low10 = m[2] / m[1]
    low20 = m[3] / m[1]
    pivot1 = m[3] - low10 * m[2]
    part21 = m[4] - low20 * m[2]
    low21 = part21 / pivot1
    pivot2 = m[5] - low20 * m[3] - low21 * part21
    y1 = m[1] - low10 * m[0]
    y2 = m[2] - low20 * m[0] - low21 * y1
    z2 = y2 / pivot2
    z1 = y1 / pivot1 - low21 * z2
    z0 = m[0] / m[1] - low10 * z1 - low20 * z2
    value = z0 * basis[0] + z1 * basis[1] + z2 * basis[2]
    out[...] = value[:, 0:WIDE]


def quad(values, axis, partner):
    count = lax.axis_size(axis)
    others = [
        lax.ppermute(values, axis, [(i, partner(i, turn)) for i in range(count)])
        for turn in range(1, 4)
    ]
    return [values, *others]


def quad_sum(values, axis, partner):
    four = quad(values, axis, partner)
    return (four[0] + four[1]) + (four[2] + four[3])


def terms_over_devices(values, beside):
    values = values + lax.ppermute(values, "gy", [(i, i ^ 1) for i in range(lax.axis_size("gy"))])
    values = quad_sum(values, "gy", lambda i, turn: i ^ (2 * turn))
    values, done = lax.optimization_barrier((values, beside[0]()))
    values = quad_sum(values, "gx", lambda i, turn: i ^ turn)
    values, done = lax.optimization_barrier((values, beside[1](done)))
    return quad(values, "gx", lambda i, turn: i ^ (4 * turn)), done


def held_in_vmem(arrays):
    return [pltpu.with_memory_space_constraint(a, pltpu.VMEM) for a in arrays]


def vmem(kind):
    return pltpu.VMEM(kind.shape, kind.dtype)


def whole(shape):
    return pl.BlockSpec(shape, lambda k: (0,) * len(shape))


def per_device(block_list, wet_levels, mixing, velocity, tracers, damping):
    f32 = jnp.float32
    slots, fields_each, levels, cells = tracers.shape
    params = pltpu.CompilerParams(
        dimension_semantics=("arbitrary",), vmem_limit_bytes=40 * 1024 * 1024
    )

    def tiles(*shape):
        zeros = (0,) * (len(shape) + 2)
        return (
            pl.BlockSpec((1, *shape, 8, LANES), lambda k: (k, *zeros)),
            jax.ShapeDtypeStruct((TILES, *shape, 8, LANES), f32),
        )

    _, rows_type = tiles(NS)
    _, columns_type = tiles(EW)
    rows_extra = pl.BlockSpec((TILES, 1, 8, LANES), lambda k: (0, NS - 1, 0, 0))
    in_vmem = pl.BlockSpec(memory_space=pltpu.VMEM)
    own_specs = [pl.BlockSpec(memory_space=pltpu.SMEM)] + [in_vmem] * 5
    own = (block_list, *held_in_vmem((wet_levels, mixing, damping, velocity, tracers)))
    whole_params = pltpu.CompilerParams(vmem_limit_bytes=40 * 1024 * 1024)

    east, west = pl.pallas_call(
        columns_kernel,
        in_specs=own_specs,
        out_specs=[in_vmem] * 2,
        out_shape=[vmem(columns_type)] * 2,
        scratch_shapes=[pltpu.VMEM((BY, LANES), f32)],
        compiler_params=whole_params,
        name="pack_columns",
    )(*own)
    columns_total = lax.axis_size("gx")
    from_west = lax.ppermute(east, "gx", [(i, (i + 1) % columns_total) for i in range(columns_total)])
    from_east = lax.ppermute(west, "gx", [((i + 1) % columns_total, i) for i in range(columns_total)])

    fields_block, fields_type = tiles(4, BY)
    column_shape = (BY, 8, LANES)
    column_type = jax.ShapeDtypeStruct(column_shape, f32)
    own_strips = pl.pallas_call(
        strips_kernel,
        in_specs=own_specs,
        out_specs=[in_vmem] * 2,
        out_shape=[vmem(fields_type), vmem(column_type)],
        scratch_shapes=[pltpu.VMEM((BY, LANES), f32)],
        compiler_params=whole_params,
        cost_estimate=pl.CostEstimate(flops=30_000_000, bytes_accessed=9_000_000, transcendentals=0),
        name="strips",
    )(*own)
    with_halos = held_in_vmem((*own_strips, from_west, from_east))
    up, down = pl.pallas_call(
        row_message_kernel,
        in_specs=[in_vmem] * 4,
        out_specs=[in_vmem] * 2,
        out_shape=[vmem(rows_type)] * 2,
        scratch_shapes=[pltpu.VMEM((BY, LANES), f32)] * 2,
        compiler_params=whole_params,
        name="row_message",
    )(*with_halos)
    fields, columns = pl.pallas_call(
        halo_kernel,
        in_specs=[in_vmem] * 4,
        out_specs=[in_vmem] * 2,
        out_shape=[vmem(fields_type), vmem(column_type)],
        scratch_shapes=[pltpu.VMEM((BY, LANES), f32)] * 2,
        compiler_params=whole_params,
        cost_estimate=pl.CostEstimate(flops=30_000_000, bytes_accessed=9_000_000, transcendentals=0),
        name="halos",
    )(*with_halos)
    rows_total = lax.axis_size("gy")
    from_below = lax.ppermute(up, "gy", [(i, i + 1) for i in range(rows_total - 1)])
    from_above = lax.ppermute(down, "gy", [(i + 1, i) for i in range(rows_total - 1)])

    row_store = pltpu.VMEM((ROWS, 8, LANES), f32)
    pair_store = pltpu.VMEM((2, ROWS, 8, LANES), f32)
    halfway_block, halfway_type = tiles(2, 8)
    moved_block, moved_type = tiles(2, 32)
    halfway, moved, forcing = pl.pallas_call(
        inner_kernel,
        grid=(TILES,),
        in_specs=[fields_block, whole(column_shape)],
        out_specs=[halfway_block, moved_block, whole(column_shape)],
        out_shape=[halfway_type, moved_type, jax.ShapeDtypeStruct(column_shape, f32)],
        scratch_shapes=[pair_store] + [row_store] * 4 + [pair_store] * 2,
        compiler_params=params,
        cost_estimate=pl.CostEstimate(flops=60_000_000, bytes_accessed=10_000_000, transcendentals=0),
        name="inner_rows",
    )(fields, columns)

    slots_type = jax.ShapeDtypeStruct((slots, levels, fields_each, cells), f32)
    inner_slots = pl.pallas_call(
        inner_slots_kernel,
        in_specs=[pl.BlockSpec(memory_space=pltpu.SMEM), in_vmem],
        out_specs=pl.BlockSpec(memory_space=pl.ANY),
        out_shape=slots_type,
        scratch_shapes=[
            pltpu.VMEM((slots, levels, fields_each, 10 * LANES), f32),
            pltpu.SemaphoreType.DMA,
        ],
        compiler_params=whole_params,
        cost_estimate=pl.CostEstimate(flops=20_000_000, bytes_accessed=6_000_000, transcendentals=0),
        name="inner_slots",
    )(block_list, moved)
    inner_slots, forcing = lax.optimization_barrier((inner_slots, forcing))

    low_block = pl.BlockSpec((PARTS, 4, 10, 8, LANES), lambda k: (k, 0, 0, 0, 0))
    high_block = pl.BlockSpec((PARTS, 4, 10, 8, LANES), lambda k: (k, 0, 3, 0, 0))
    part_rows = pl.BlockSpec((PARTS, NS, 8, LANES), lambda k: (k, 0, 0, 0))
    part_halfway = pl.BlockSpec((PARTS, 2, 8, 8, LANES), lambda k: (k, 0, 0, 0, 0))
    parts_store = pltpu.VMEM((2 * PARTS, ROWS, 8, LANES), f32)
    edges, basis, moments = pl.pallas_call(
        outer_kernel,
        grid=(TILES // PARTS,),
        in_specs=[low_block, high_block, whole(column_shape), part_rows, part_rows]
        + [rows_extra, rows_extra, part_halfway, whole(column_shape)],
        out_specs=[part_halfway, whole((3, BY, LANES)), whole((8, LANES))],
        out_shape=[
            halfway_type,
            jax.ShapeDtypeStruct((3, BY, LANES), f32),
            jax.ShapeDtypeStruct((8, LANES), f32),
        ],
        scratch_shapes=[parts_store] * 2
        + [row_store] * 4
        + [parts_store] * 2
        + [row_store]
        + [pltpu.VMEM((SURFACE, LANES), f32)] * 3,
        compiler_params=params,
        name="outer_rows",
    )(fields, fields, columns, from_below, from_above, from_below, from_above, halfway, forcing)

    def outer_slots(numbers, before):
        width = min((numbers[-1] + 1) * LANES, cells) - numbers[0] * LANES
        return pl.pallas_call(
            functools.partial(outer_slots_kernel, numbers),
            in_specs=[pl.BlockSpec(memory_space=pltpu.SMEM), in_vmem, in_vmem]
            + [pl.BlockSpec(memory_space=pl.ANY)],
            out_specs=pl.BlockSpec(memory_space=pl.ANY),
            out_shape=slots_type,
            scratch_shapes=[
                pltpu.VMEM((slots, levels, fields_each, width), f32),
                pltpu.SemaphoreType.DMA,
            ],
            input_output_aliases={3: 0},
            compiler_params=whole_params,
            cost_estimate=pl.CostEstimate(flops=2_000_000, bytes_accessed=2_000_000, transcendentals=0),
            name="outer_slots",
        )(block_list, moved, edges, before)

    beside = (lambda: outer_slots((0, 1), inner_slots), lambda before: outer_slots((12, 13, 14), before))
    moments, new_tracers = terms_over_devices(moments, beside)
    new_tracers = jnp.transpose(new_tracers, (0, 2, 1, 3))
    height = pl.pallas_call(
        finish_kernel,
        in_specs=[in_vmem] * 5,
        out_specs=in_vmem,
        out_shape=jax.ShapeDtypeStruct((BY, WIDE), f32),
        name="finish",
    )(*held_in_vmem((*moments, basis)))
    return (new_tracers, height)


def solution(mesh):
    return jax.shard_map(
        per_device,
        mesh=mesh,
        in_specs=(
            P(("gx", "gy")),
            P(("gx", "gy"), None),
            P(("gx", "gy"), None),
            P(("gx", "gy"), None, None, None),
            P(("gx", "gy"), None, None, None),
            P("gy", "gx"),
        ),
        out_specs=(P(("gx", "gy"), None, None, None), P("gy", "gx")),
        check_vma=False,
    )
```

```python
import functools
import math

import jax
import jax.numpy as jnp
from jax import lax
from jax.experimental import pallas as pl
from jax.experimental.pallas import tpu as pltpu
from jax.sharding import PartitionSpec as P

BX = 45
BY = 40
CELLS = BX * BY
LEVELS = 62
LANES = 128
TILES = 8
REACH = 7
ROWS = BY + 2 * REACH
PARTS = 2
AHEAD = 26
BASE = 8
WIDE = 2 * BX
NS = 27
FIELD_AT = (0, 7, 14, 20)
EW = 11
SHARED = 16
SURFACE = 56

advect_rate = 0.25
mixing_rate = 0.015
salt_weight = 0.8


def lane_ids():
    return lax.broadcasted_iota(jnp.int32, (8, LANES), 1)


def merge(parts, lane):
    flat = []
    for low, width, value in parts:
        low %= LANES
        if low + width > LANES:
            flat.append((low, value))
            flat.append((0, value))
        else:
            flat.append((low, value))
    flat.sort(key=lambda part: part[0])
    result = flat[0][1]
    last = result
    for low, value in flat[1:]:
        if value is last:
            continue
        result = jnp.where(lane >= low, value, result)
        last = value
    return result


def turn(value, shift):
    shift %= LANES
    return pltpu.roll(value, shift, 1) if shift else value


class Source:
    def __init__(self, load):
        self.load = load
        self.kept = {}

    def tile(self, *key):
        if key not in self.kept:
            self.kept[key] = self.load(*key)
        return self.kept[key]

    def cells(self, position, start, width):
        parts = []
        at = start
        while at < start + width:
            number = at // LANES
            end = min(start + width, (number + 1) * LANES)
            parts.append((at, end - at, self.tile(position, number)))
            at = end
        return parts


def pack_columns(source, lane):
    east, west = [], []
    for group in range(3):
        rows = range(17 * group, min(17 * group + 17, BY))
        east.append(merge([c for r in rows for c in source.cells(1, BX * r + BX - REACH, REACH)], lane))
        west.append(merge([c for r in rows for c in source.cells(0, BX * r, REACH)], lane))
    return east, west


def strip_rows(source, lane):
    turned = {}

    def combined(r):
        if r not in turned:
            parts = source.cells(0, BX * r, BX) if r >= 0 else []
            if r + 1 < BY:
                parts += source.cells(1, BX * (r + 1), BX)
            turned[r] = turn(merge(parts, lane), BASE - BX * r)
        return turned[r]

    for r in range(-1, BY):
        combined(r)
    for row in range(BY):
        yield row, jnp.where(lane < BASE + BX, combined(row), combined(row - 1))


def message_tiles(message, block, field):
    tiles = [message[block, 2 * field], message[block, 2 * field + 1]]
    last = message[block, 8 + field // 2]
    tiles.append(turn(last, LANES - SHARED) if field % 2 else last)
    return lambda number: tiles[number]


def beside_rows(rows, west, east, lane):
    turned = {}

    def combined(r):
        if r not in turned:
            low, high = (BX * r - REACH) % LANES, BX * (r + 2) % LANES
            if not 0 <= r - 1 < BY:
                value = east((r + 2) // 17)
            elif not 0 <= r + 2 < BY:
                value = west((r - 1) // 17)
            elif low < high:
                inside = lane < high if high + REACH <= LANES else (lane >= low) & (lane < high)
                value = jnp.where(inside, west((r - 1) // 17), east((r + 2) // 17))
            else:
                inside = lane < low if low + REACH <= LANES else (lane >= high) & (lane < low)
                value = jnp.where(inside, east((r + 2) // 17), west((r - 1) // 17))
            turned[r] = turn(value, BASE - BX * r)
        return turned[r]

    for r in sorted({row + 1 for row in rows} | {row - 2 for row in rows}):
        combined(r)
    for row in rows:
        yield row, combined(row + 1), combined(row - 2)


def slot_swap(block_list):
    first = block_list[0]
    return jnp.where(first >= 0, first & 1, 1 - (block_list[1] & 1))


def over_level_blocks(work):
    def body(block, carry):
        work(block, pl.ds(pl.multiple_of(8 * block, 8), 8))
        return carry

    lax.fori_loop(0, TILES - 1, body, 0)
    work(TILES - 1, pl.ds(LEVELS - 8, 8))


def field_loader(ref, which, levels, swap):
    def load(position, number):
        slot = swap if position == 0 else 1 - swap
        if number < 14:
            return ref[slot, which, levels, number * LANES : (number + 1) * LANES]
        return turn(ref[slot, which, levels, CELLS - LANES : CELLS], CELLS % LANES)

    return load


def column_loader(wet_levels, mixing, swap):
    def load(position, number):
        slot = swap if position == 0 else 1 - swap
        low = number * LANES if number < 14 else CELLS - LANES
        both = wet_levels[:, low : low + LANES].astype(jnp.float32)
        depth = jnp.where(slot == 0, both[0:1, :], both[1:2, :])
        both = mixing[:, low : low + LANES]
        mix = jnp.where(slot == 0, both[0:1, :], both[1:2, :])
        sublane = lax.broadcasted_iota(jnp.int32, (8, LANES), 0)
        value = jnp.where(
            sublane == 0, jnp.broadcast_to(depth, (8, LANES)), jnp.broadcast_to(mix, (8, LANES))
        )
        return value if number < 14 else turn(value, CELLS % LANES)

    return load


def columns_kernel(block_list, wet_levels, mixing, damping, velocity, tracers, east, west, padded):
    lane = lane_ids()
    swap = slot_swap(block_list)

    def work(block, levels):
        lasts = []
        for field in range(4):
            ref = tracers if field < 2 else velocity
            easts, wests = pack_columns(Source(field_loader(ref, field % 2, levels, swap)), lane)
            scale = 1.0 if field < 2 else 0.25 * advect_rate
            for number in range(2):
                east[block, 2 * field + number] = easts[number] * scale
                west[block, 2 * field + number] = wests[number] * scale
            lasts.append((easts[2] * scale, wests[2] * scale))
        for pair in range(2):
            for side, message in enumerate((east, west)):
                first = BX - REACH if side == 0 else 0
                lows = [BX * row + first for row in range(34, BY)]
                one, two = lasts[2 * pair][side], turn(lasts[2 * pair + 1][side], SHARED)
                parts = [(low, REACH, one) for low in lows] + [(low + SHARED, REACH, two) for low in lows]
                message[block, 8 + pair] = merge(parts, lane)

    over_level_blocks(work)
    easts, wests = pack_columns(Source(column_loader(wet_levels, mixing, swap)), lane)
    padded[...] = jnp.zeros_like(padded)
    padded[:, 0:WIDE] = damping[...]
    tiles = [padded[8 * j : 8 * j + 8, :] for j in range(5)]
    easts.append(merge([(2 * j, 2, turn(t, 2 * j - WIDE + 2)) for j, t in enumerate(tiles)], lane))
    wests.append(merge([(2 * j, 2, turn(t, 2 * j)) for j, t in enumerate(tiles)], lane))
    for block in range(TILES):
        east[block, EW - 1] = easts[min(block, 3)]
        west[block, EW - 1] = wests[min(block, 3)]


def strips_kernel(block_list, wet_levels, mixing, damping, velocity, tracers, fields, columns, padded):
    lane = lane_ids()
    swap = slot_swap(block_list)
    padded[...] = jnp.zeros_like(padded)
    padded[:, 0:WIDE] = damping[...]
    for j in range(5):
        padded[8 * j : 8 * j + 8, :] = turn(padded[8 * j : 8 * j + 8, :], BASE)
    sublane = lax.broadcasted_iota(jnp.int32, (8, LANES), 0)
    for row, value in strip_rows(Source(column_loader(wet_levels, mixing, swap)), lane):
        damp = jnp.broadcast_to(padded[row : row + 1, :], (8, LANES))
        columns[row] = jnp.where(sublane == 2, damp, value)

    def work(block, levels):
        for field in range(4):
            ref = tracers if field < 2 else velocity
            for row, value in strip_rows(Source(field_loader(ref, field % 2, levels, swap)), lane):
                fields[block, field, row] = value if field < 2 else (0.25 * advect_rate) * value

    over_level_blocks(work)


def place_halos(own_fields, own_columns, from_west, from_east, low_damp, high_damp, rows, put):
    lane = lane_ids()
    sublane = lax.broadcasted_iota(jnp.int32, (8, LANES), 0)
    for j in range(5):
        low_damp[8 * j : 8 * j + 8, :] = turn(from_west[3, EW - 1], BASE - 2 - 2 * j)
        high_damp[8 * j : 8 * j + 8, :] = turn(from_east[3, EW - 1], BASE + WIDE - 2 * j)
    sides = beside_rows(rows, lambda t: from_west[t, EW - 1], lambda t: from_east[t, EW - 1], lane)
    for row, west, east in sides:
        west = jnp.where(sublane == 2, jnp.broadcast_to(low_damp[row : row + 1, :], (8, LANES)), west)
        east = jnp.where(sublane == 2, jnp.broadcast_to(high_damp[row : row + 1, :], (8, LANES)), east)
        value = jnp.where(lane < BASE, west, own_columns[row])
        put(0, 4, row, jnp.where(lane < BASE + WIDE, value, east))

    def work(block, carry):
        for field in range(4):
            sides = beside_rows(
                rows,
                message_tiles(from_west, block, field),
                message_tiles(from_east, block, field),
                lane,
            )
            for row, west, east in sides:
                value = jnp.where(lane < BASE, west, own_fields[block, field, row])
                put(block, field, row, jnp.where(lane < BASE + WIDE, value, east))
        return carry

    lax.fori_loop(0, TILES, work, 0)


def row_message_kernel(parity, own_fields, own_columns, from_west, from_east, chip, link, low_damp, high_damp):
    def write(up, down):
        def put(block, field, row, value):
            if row < REACH:
                target, number = down, row
            else:
                target, number = up, row - (BY - REACH)
            if field == 4:
                target[number, NS - 1] = value
            elif field < 2:
                target[block, FIELD_AT[field] + number] = value
            elif row < REACH - 1:
                target[block, FIELD_AT[field] + number] = value
            elif row > BY - REACH:
                target[block, FIELD_AT[field] + number - 1] = value

        rows = (*range(REACH), *range(BY - REACH, BY))
        place_halos(own_fields, own_columns, from_west, from_east, low_damp, high_damp, rows, put)

    for message in (chip, link):
        message[TILES - 1, NS - 1] = jnp.zeros((8, LANES), jnp.float32)

    @pl.when(parity[0] == 0)
    def _():
        write(chip, link)

    @pl.when(parity[0] != 0)
    def _():
        write(link, chip)


def halo_kernel(own_fields, own_columns, from_west, from_east, fields, columns, low_damp, high_damp):
    def put(block, field, row, value):
        if field == 4:
            columns[row] = value
        else:
            fields[block, field, row] = value

    place_halos(own_fields, own_columns, from_west, from_east, low_damp, high_damp, range(BY), put)


def staggered(spans, phases):
    state = {}
    length = max(high - low + 1 for low, high in spans)
    ahead = min(AHEAD, length)
    for time in range(length + ahead * (len(phases) - 1)):
        for number in reversed(range(len(phases))):
            for span, (low, high) in enumerate(spans):
                row = low + time - number * ahead
                if low <= row <= high:
                    phases[number](span, row, state)


class Band:
    def __init__(self, low, high, read, write, eastward, northward, levels, part=0):
        self.low, self.high, self.read, self.write = low, high, read, write
        self.eastward, self.northward = eastward, northward
        self.levels, self.part = levels, 2 * part


def advance(bands, shared, scratch):
    depth_east, depth_north, mix = shared
    scaled, held = scratch

    def rise(band, n, row):
        read = bands[band].read
        return jnp.where(bands[band].levels < depth_north(row), read(n, row + 1) - read(n, row), 0.0)

    def look_east(band, row, state):
        for n in range(2):
            state[band, n, row] = turn(bands[band].read(n, row), LANES - 1)

    def step_east(band, row, state):
        wet = bands[band].levels < depth_east(row)
        for n in range(2):
            here, beside = bands[band].read(n, row), state[band, n, row]
            step = jnp.where(wet, beside - here, 0.0)
            state[band, n, row] = step, turn(step, 1)
            held[bands[band].part + n, row + REACH] = beside + here

    def scale(band, row, state):
        for n in range(2):
            step, back = state.pop((band, n, row))
            drop = state.pop((band, n)) if (band, n) in state else rise(band, n, row - 1)
            state[band, n] = rise(band, n, row)
            scaled[bands[band].part + n, row + REACH] = mix(row) * ((step - back) + (state[band, n] - drop))

    staggered([(b.low - 1, b.high + 1) for b in bands], (look_east, step_east, scale))

    def north_flow(band, n, row):
        read, northward = bands[band].read, bands[band].northward
        step = scaled[bands[band].part + n, row + 1 + REACH] - scaled[bands[band].part + n, row + REACH]
        both = (northward(row) + northward(row + 1)) * (read(n, row) + read(n, row + 1)) + step
        return jnp.where(bands[band].levels < depth_north(row), both, 0.0)

    def look_east_again(band, row, state):
        state[band, "flow", row] = turn(bands[band].eastward(row), LANES - 1)
        for n in range(2):
            state[band, n, row] = turn(scaled[bands[band].part + n, row + REACH], LANES - 1)

    def east_flow(band, row, state):
        wet = bands[band].levels < depth_east(row)
        flow = bands[band].eastward(row) + state.pop((band, "flow", row))
        for n in range(2):
            at = row + REACH
            both = flow * held[bands[band].part + n, at] + (state[band, n, row] - scaled[bands[band].part + n, at])
            both = jnp.where(wet, both, 0.0)
            state[band, n, row] = both, turn(both, 1)

    def change(band, row, state):
        for n in range(2):
            east, back = state.pop((band, n, row))
            south = state.pop((band, n)) if (band, n) in state else north_flow(band, n, row - 1)
            state[band, n] = north_flow(band, n, row)
            result = bands[band].read(n, row) - ((east - back) + (state[band, n] - south))
            bands[band].write(n, row, result)

    staggered([(b.low, b.high) for b in bands], (look_east_again, east_flow, change))


def level_ids(step):
    sublane = lax.broadcasted_iota(jnp.int32, (8, LANES), 0)
    last = step == TILES - 1
    twice = last & (sublane < 8 * TILES - LEVELS)
    numbers = sublane + jnp.where(last, LEVELS - 8, 8 * step)
    return jnp.where(twice, LEVELS, numbers).astype(jnp.float32)


def spread_columns(column, rows, depth, depth_east, depth_north, mix):
    last = None
    for row in rows:
        value = column(row)
        here = jnp.broadcast_to(value[0:1, :], (8, LANES))
        depth[row + REACH] = here
        depth_east[row + REACH] = jnp.minimum(here, turn(here, LANES - 1))
        mix[row + REACH] = mixing_rate * jnp.broadcast_to(value[1:2, :], (8, LANES))
        if last is not None:
            depth_north[row + REACH - 1] = jnp.minimum(here, last)
        last = here


def contribution(levels, depth, warm, salt):
    return jnp.where(levels < depth, warm - salt_weight * salt, 0.0)


def inner_kernel(
    fields, columns, halfway, moved, forcing,
    middle, depth, depth_east, depth_north, mix, scaled, held,
):
    step = pl.program_id(0)

    @pl.when(step == 0)
    def _():
        spread_columns(lambda row: columns[row], range(BY), depth, depth_east, depth_north, mix)
        forcing[...] = jnp.zeros_like(forcing)

    levels = level_ids(step)
    shared = (
        lambda row: depth_east[row + REACH],
        lambda row: depth_north[row + REACH],
        lambda row: mix[row + REACH],
    )

    def write_middle(n, row, value):
        middle[n, row] = value
        if row < 6:
            halfway[0, n, row - 2] = value
        if row >= 34:
            halfway[0, n, row - 30] = value

    def write_moved(n, row, value):
        moved[0, n, row - 4] = value

    def eastward(row):
        return fields[0, 2, row]

    def northward(row):
        return fields[0, 3, row]

    first = Band(2, 37, lambda n, row: fields[0, n, row], write_middle, eastward, northward, levels)
    second = Band(4, 35, lambda n, row: middle[n, row], write_moved, eastward, northward, levels)
    advance([first], shared, (scaled, held))
    advance([second], shared, (scaled, held))
    for row in range(4, 36):
        forcing[row] += contribution(
            levels, depth[row + REACH], moved[0, 0, row - 4], moved[0, 1, row - 4]
        )


def surface_operator(values, couple_east, couple_north, damping):
    east = couple_east * (values - turn(values, LANES - 1))
    north = couple_north * (values - pltpu.roll(values, SURFACE - 1, 0))
    return damping * values + ((east - turn(east, 1)) + (north - pltpu.roll(north, 1, 0)))


def outer_kernel(parity, low_fields, high_fields, columns, chip, link, chip_extra, link_extra, *others):
    @pl.when(parity[0] == 0)
    def _():
        outer_rows(low_fields, high_fields, columns, link, chip, link_extra, chip_extra, *others)

    @pl.when(parity[0] != 0)
    def _():
        outer_rows(low_fields, high_fields, columns, chip, link, chip_extra, link_extra, *others)


def outer_rows(
    low_fields, high_fields, columns, up, down, up_extra, down_extra, halfway, inner_forcing,
    moved, basis, moments,
    middle, beyond, depth, depth_east, depth_north, mix, scaled, held, forcing, surface, depths, dampings,
):
    step = pl.program_id(0)

    def column(row):
        if row < 0:
            return up_extra[row + REACH, 0]
        if row >= BY:
            return down_extra[row - BY, 0]
        return columns[row]

    rows = range(-REACH, BY + REACH)

    @pl.when(step == 0)
    def _():
        spread_columns(column, rows, depth, depth_east, depth_north, mix)
        forcing[...] = jnp.zeros_like(forcing)

    shared = (
        lambda row: depth_east[row + REACH],
        lambda row: depth_north[row + REACH],
        lambda row: mix[row + REACH],
    )
    first, second = [], []
    for part in range(PARTS):
        levels = level_ids(PARTS * step + part)

        def field(number, row, part=part):
            if row < 0:
                return up[part, FIELD_AT[number] + row + (REACH if number < 2 else REACH - 1)]
            if row >= BY:
                return down[part, FIELD_AT[number] + row - BY]
            return low_fields[part, number, row] if row < 10 else high_fields[part, number, row - 30]

        def read_middle(n, row, part=part):
            if 2 <= row < 6:
                return halfway[part, n, row - 2]
            if 34 <= row < 38:
                return halfway[part, n, row - 30]
            return middle[2 * part + n, row + REACH]

        def write_middle(n, row, value, part=part):
            middle[2 * part + n, row + REACH] = value

        def write_beyond(n, row, value, part=part):
            beyond[2 * part + n, row + REACH] = value
            if 0 <= row < 4:
                moved[part, n, row] = value
            if 36 <= row < BY:
                moved[part, n, row - 32] = value

        flows = (functools.partial(field, 2), functools.partial(field, 3), levels, part)
        first += [Band(low, high, field, write_middle, *flows) for low, high in ((-5, 1), (38, 44))]
        second += [Band(low, high, read_middle, write_beyond, *flows) for low, high in ((-3, 3), (36, 42))]
    advance(first, shared, (scaled, held))
    advance(second, shared, (scaled, held))
    for row in (*range(-3, 4), *range(36, 43)):
        at = row + REACH
        for part in range(PARTS):
            forcing[at] += contribution(
                second[2 * part].levels, depth[at], beyond[2 * part, at], beyond[2 * part + 1, at]
            )

    @pl.when(step == TILES // PARTS - 1)
    def _():
        surface[...] = jnp.zeros_like(surface)
        for row in range(-3, 43):
            part = inner_forcing[row] if 4 <= row < 36 else forcing[row + REACH]
            total = jnp.sum(part, axis=0, keepdims=True)
            surface[row + 8 : row + 9, :] = total * (1.0 / math.sqrt(LEVELS))
        depths[...] = jnp.zeros_like(depths)
        dampings[...] = jnp.zeros_like(dampings)
        for row in rows:
            value = column(row)
            depths[row + 8 : row + 9, :] = value[0:1, :]
            dampings[row + 8 : row + 9, :] = value[2:3, :]
        here = depths[...]
        couple_east = jnp.minimum(here, turn(here, LANES - 1)) * (1.0 / LEVELS)
        couple_north = jnp.minimum(here, pltpu.roll(here, SURFACE - 1, 0)) * (1.0 / LEVELS)
        diagonal = dampings[...]
        powers = [surface[...]]
        for _ in range(3):
            powers.append(surface_operator(powers[-1], couple_east, couple_north, diagonal))
        row_id = lax.broadcasted_iota(jnp.int32, (SURFACE, LANES), 0)
        lane_id = lax.broadcasted_iota(jnp.int32, (SURFACE, LANES), 1)
        own = (row_id >= 8) & (row_id < 8 + BY) & (lane_id >= BASE) & (lane_id < BASE + WIDE)
        moments[...] = jnp.zeros_like(moments)
        for k in range(6):
            product = jnp.where(own, powers[k // 2] * powers[(k + 1) // 2], 0.0)
            moments[k : k + 1, :] = jnp.sum(product, axis=0, keepdims=True)
        for k in range(3):
            basis[k] = turn(powers[k], LANES - BASE)[8 : 8 + BY, :]


def to_slots(numbers, start, rows, load, block_list, out, group):
    lane = lane_ids()
    swap = slot_swap(block_list)
    cells = [c for t in numbers for c in range(t * LANES, min((t + 1) * LANES, CELLS))]
    wanted = sorted({c // BX - p for c in cells for p in range(2)})

    def work(blocks):
        turned = {}
        chosen = list(enumerate(blocks))
        for index, (block, last) in chosen:
            for n in range(2):
                for r in wanted:
                    low, high = (min(max(row, rows[0]), rows[1]) for row in (r, r + 1))
                    value = jnp.where(lane < BASE + BX, load(block, n, low), load(block, n, high))
                    turned[index, n, r] = turn(value, BX * r - BASE)
        for index, (block, last) in chosen:
            for n in range(2):
                for number in numbers:
                    for position in range(2):
                        slot = swap if position == 0 else 1 - swap
                        first, end = number * LANES, min((number + 1) * LANES, CELLS)
                        parts = []
                        for row in range(first // BX, (end - 1) // BX + 1):
                            low = max(row * BX, first)
                            width = min((row + 1) * BX, end) - low
                            parts.append((low, width, turned[index, n, row - position]))
                        value = merge(parts, lane)[:, 0 : end - first]
                        if last:
                            rest = value[8 * TILES - LEVELS : 8]
                            out[slot, 8 * TILES - 8 : LEVELS, n, first - start : end - start] = rest
                        else:
                            out[slot, pl.ds(8 * block, 8), n, first - start : end - start] = value

    def body(index, carry):
        work([(group * index + i, False) for i in range(group)])
        return carry

    lax.fori_loop(0, TILES // group - 1, body, 0)
    work([(block, block == TILES - 1) for block in range(TILES - group, TILES)])


def inner_slots_kernel(block_list, moved, out, cells, semaphore):
    to_slots(range(2, 12), 2 * LANES, (4, 35), lambda block, n, row: moved[block, n, row - 4], block_list, cells, 1)
    copy = pltpu.make_async_copy(cells, out.at[:, :, :, 2 * LANES : 12 * LANES], semaphore)
    copy.start()
    copy.wait()


def outer_slots_kernel(numbers, block_list, moved, edges, inner, out, cells, semaphore):
    def load(block, n, row):
        if 4 <= row < 36:
            return moved[block, n, row - 4]
        return edges[block, n, row if row < 4 else row - 32]

    start, end = numbers[0] * LANES, min((numbers[-1] + 1) * LANES, CELLS)
    to_slots(numbers, start, (0, BY - 1), load, block_list, cells, 2)
    copy = pltpu.make_async_copy(cells, out.at[:, :, :, start:end], semaphore)
    copy.start()
    copy.wait()


def finish_kernel(first, second, third, fourth, basis, out):
    moments = (first[...] + second[...]) + (third[...] + fourth[...])
    totals = jnp.sum(moments, axis=1, keepdims=True)
    m = [totals[k : k + 1, :] for k in range(6)]
    low10 = m[2] / m[1]
    low20 = m[3] / m[1]
    pivot1 = m[3] - low10 * m[2]
    part21 = m[4] - low20 * m[2]
    low21 = part21 / pivot1
    pivot2 = m[5] - low20 * m[3] - low21 * part21
    y1 = m[1] - low10 * m[0]
    y2 = m[2] - low20 * m[0] - low21 * y1
    z2 = y2 / pivot2
    z1 = y1 / pivot1 - low21 * z2
    z0 = m[0] / m[1] - low10 * z1 - low20 * z2
    value = z0 * basis[0] + z1 * basis[1] + z2 * basis[2]
    out[...] = value[:, 0:WIDE]


def quad(values, axis, partner):
    count = lax.axis_size(axis)
    others = [
        lax.ppermute(values, axis, [(i, partner(i, turn)) for i in range(count)])
        for turn in range(1, 4)
    ]
    return [values, *others]


def quad_sum(values, axis, partner):
    four = quad(values, axis, partner)
    return (four[0] + four[1]) + (four[2] + four[3])


def terms_over_devices(values, beside):
    values = values + lax.ppermute(values, "gy", [(i, i ^ 1) for i in range(lax.axis_size("gy"))])
    values = quad_sum(values, "gy", lambda i, turn: i ^ (2 * turn))
    values, done = lax.optimization_barrier((values, beside[0]()))
    values = quad_sum(values, "gx", lambda i, turn: i ^ turn)
    values, done = lax.optimization_barrier((values, beside[1](done)))
    return quad(values, "gx", lambda i, turn: i ^ (4 * turn)), done


def held_in_vmem(arrays):
    return [pltpu.with_memory_space_constraint(a, pltpu.VMEM) for a in arrays]


def vmem(kind):
    return pltpu.VMEM(kind.shape, kind.dtype)


def whole(shape):
    return pl.BlockSpec(shape, lambda k: (0,) * len(shape))


def per_device(block_list, wet_levels, mixing, velocity, tracers, damping):
    f32 = jnp.float32
    slots, fields_each, levels, cells = tracers.shape
    params = pltpu.CompilerParams(
        dimension_semantics=("arbitrary",), vmem_limit_bytes=40 * 1024 * 1024
    )

    def tiles(*shape):
        zeros = (0,) * (len(shape) + 2)
        return (
            pl.BlockSpec((1, *shape, 8, LANES), lambda k: (k, *zeros)),
            jax.ShapeDtypeStruct((TILES, *shape, 8, LANES), f32),
        )

    _, rows_type = tiles(NS)
    _, columns_type = tiles(EW)
    rows_extra = pl.BlockSpec((TILES, 1, 8, LANES), lambda k: (0, NS - 1, 0, 0))
    in_vmem = pl.BlockSpec(memory_space=pltpu.VMEM)
    own_specs = [pl.BlockSpec(memory_space=pltpu.SMEM)] + [in_vmem] * 5
    own = (block_list, *held_in_vmem((wet_levels, mixing, damping, velocity, tracers)))
    whole_params = pltpu.CompilerParams(vmem_limit_bytes=40 * 1024 * 1024)

    east, west = pl.pallas_call(
        columns_kernel,
        in_specs=own_specs,
        out_specs=[in_vmem] * 2,
        out_shape=[vmem(columns_type)] * 2,
        scratch_shapes=[pltpu.VMEM((BY, LANES), f32)],
        compiler_params=whole_params,
        name="pack_columns",
    )(*own)
    columns_total = lax.axis_size("gx")
    from_west = lax.ppermute(east, "gx", [(i, (i + 1) % columns_total) for i in range(columns_total)])
    from_east = lax.ppermute(west, "gx", [((i + 1) % columns_total, i) for i in range(columns_total)])

    fields_block, fields_type = tiles(4, BY)
    column_shape = (BY, 8, LANES)
    column_type = jax.ShapeDtypeStruct(column_shape, f32)
    own_strips = pl.pallas_call(
        strips_kernel,
        in_specs=own_specs,
        out_specs=[in_vmem] * 2,
        out_shape=[vmem(fields_type), vmem(column_type)],
        scratch_shapes=[pltpu.VMEM((BY, LANES), f32)],
        compiler_params=whole_params,
        cost_estimate=pl.CostEstimate(flops=30_000_000, bytes_accessed=9_000_000, transcendentals=0),
        name="strips",
    )(*own)
    with_halos = held_in_vmem((*own_strips, from_west, from_east))
    parity = (lax.axis_index("gy") & 1).astype(jnp.int32).reshape(1)
    chip, link = pl.pallas_call(
        row_message_kernel,
        in_specs=[pl.BlockSpec(memory_space=pltpu.SMEM)] + [in_vmem] * 4,
        out_specs=[in_vmem] * 2,
        out_shape=[vmem(rows_type)] * 2,
        scratch_shapes=[pltpu.VMEM((BY, LANES), f32)] * 2,
        compiler_params=whole_params,
        name="row_message",
    )(parity, *with_halos)
    fields, columns = pl.pallas_call(
        halo_kernel,
        in_specs=[in_vmem] * 4,
        out_specs=[in_vmem] * 2,
        out_shape=[vmem(fields_type), vmem(column_type)],
        scratch_shapes=[pltpu.VMEM((BY, LANES), f32)] * 2,
        compiler_params=whole_params,
        cost_estimate=pl.CostEstimate(flops=30_000_000, bytes_accessed=9_000_000, transcendentals=0),
        name="halos",
    )(*with_halos)
    rows_total = lax.axis_size("gy")
    pairs = [(i, i ^ 1) for i in range(rows_total)]
    from_chip = lax.ppermute(chip, "gy", pairs)
    pairs = [pair for i in range(1, rows_total - 1, 2) for pair in ((i, i + 1), (i + 1, i))]
    from_link = lax.ppermute(link, "gy", pairs)

    row_store = pltpu.VMEM((ROWS, 8, LANES), f32)
    pair_store = pltpu.VMEM((2, ROWS, 8, LANES), f32)
    halfway_block, halfway_type = tiles(2, 8)
    moved_block, moved_type = tiles(2, 32)
    halfway, moved, forcing = pl.pallas_call(
        inner_kernel,
        grid=(TILES,),
        in_specs=[fields_block, whole(column_shape)],
        out_specs=[halfway_block, moved_block, whole(column_shape)],
        out_shape=[halfway_type, moved_type, jax.ShapeDtypeStruct(column_shape, f32)],
        scratch_shapes=[pair_store] + [row_store] * 4 + [pair_store] * 2,
        compiler_params=params,
        cost_estimate=pl.CostEstimate(flops=60_000_000, bytes_accessed=10_000_000, transcendentals=0),
        name="inner_rows",
    )(fields, columns)

    slots_type = jax.ShapeDtypeStruct((slots, levels, fields_each, cells), f32)
    inner_slots = pl.pallas_call(
        inner_slots_kernel,
        in_specs=[pl.BlockSpec(memory_space=pltpu.SMEM), in_vmem],
        out_specs=pl.BlockSpec(memory_space=pl.ANY),
        out_shape=slots_type,
        scratch_shapes=[
            pltpu.VMEM((slots, levels, fields_each, 10 * LANES), f32),
            pltpu.SemaphoreType.DMA,
        ],
        compiler_params=whole_params,
        cost_estimate=pl.CostEstimate(flops=20_000_000, bytes_accessed=6_000_000, transcendentals=0),
        name="inner_slots",
    )(block_list, moved)
    inner_slots, forcing = lax.optimization_barrier((inner_slots, forcing))

    low_block = pl.BlockSpec((PARTS, 4, 10, 8, LANES), lambda k: (k, 0, 0, 0, 0))
    high_block = pl.BlockSpec((PARTS, 4, 10, 8, LANES), lambda k: (k, 0, 3, 0, 0))
    part_rows = pl.BlockSpec((PARTS, NS, 8, LANES), lambda k: (k, 0, 0, 0))
    part_halfway = pl.BlockSpec((PARTS, 2, 8, 8, LANES), lambda k: (k, 0, 0, 0, 0))
    parts_store = pltpu.VMEM((2 * PARTS, ROWS, 8, LANES), f32)
    edges, basis, moments = pl.pallas_call(
        outer_kernel,
        grid=(TILES // PARTS,),
        in_specs=[pl.BlockSpec(memory_space=pltpu.SMEM), low_block, high_block, whole(column_shape)]
        + [part_rows, part_rows]
        + [rows_extra, rows_extra, part_halfway, whole(column_shape)],
        out_specs=[part_halfway, whole((3, BY, LANES)), whole((8, LANES))],
        out_shape=[
            halfway_type,
            jax.ShapeDtypeStruct((3, BY, LANES), f32),
            jax.ShapeDtypeStruct((8, LANES), f32),
        ],
        scratch_shapes=[parts_store] * 2
        + [row_store] * 4
        + [parts_store] * 2
        + [row_store]
        + [pltpu.VMEM((SURFACE, LANES), f32)] * 3,
        compiler_params=params,
        name="outer_rows",
    )(parity, fields, fields, columns, from_chip, from_link, from_chip, from_link, halfway, forcing)

    def outer_slots(numbers, before):
        width = min((numbers[-1] + 1) * LANES, cells) - numbers[0] * LANES
        return pl.pallas_call(
            functools.partial(outer_slots_kernel, numbers),
            in_specs=[pl.BlockSpec(memory_space=pltpu.SMEM), in_vmem, in_vmem]
            + [pl.BlockSpec(memory_space=pl.ANY)],
            out_specs=pl.BlockSpec(memory_space=pl.ANY),
            out_shape=slots_type,
            scratch_shapes=[
                pltpu.VMEM((slots, levels, fields_each, width), f32),
                pltpu.SemaphoreType.DMA,
            ],
            input_output_aliases={3: 0},
            compiler_params=whole_params,
            cost_estimate=pl.CostEstimate(flops=2_000_000, bytes_accessed=2_000_000, transcendentals=0),
            name="outer_slots",
        )(block_list, moved, edges, before)

    beside = (lambda: outer_slots((0, 1), inner_slots), lambda before: outer_slots((12, 13, 14), before))
    moments, new_tracers = terms_over_devices(moments, beside)
    new_tracers = jnp.transpose(new_tracers, (0, 2, 1, 3))
    height = pl.pallas_call(
        finish_kernel,
        in_specs=[in_vmem] * 5,
        out_specs=in_vmem,
        out_shape=jax.ShapeDtypeStruct((BY, WIDE), f32),
        name="finish",
    )(*held_in_vmem((*moments, basis)))
    return (new_tracers, height)


def solution(mesh):
    return jax.shard_map(
        per_device,
        mesh=mesh,
        in_specs=(
            P(("gx", "gy")),
            P(("gx", "gy"), None),
            P(("gx", "gy"), None),
            P(("gx", "gy"), None, None, None),
            P(("gx", "gy"), None, None, None),
            P("gy", "gx"),
        ),
        out_specs=(P(("gx", "gy"), None, None, None), P("gy", "gx")),
        check_vma=False,
    )
```

```python
import functools
import math

import jax
import jax.numpy as jnp
from jax import lax
from jax.experimental import pallas as pl
from jax.experimental.pallas import tpu as pltpu
from jax.sharding import PartitionSpec as P

BX = 45
BY = 40
CELLS = BX * BY
LEVELS = 62
LANES = 128
TILES = 8
REACH = 7
ROWS = BY + 2 * REACH
PARTS = 2
INNER_PLAN = (2, 5, 2)
OUTER_PLAN = (4, 3, 4)
AHEAD = 26
BASE = 8
WIDE = 2 * BX
NS = 27
FIELD_AT = (0, 7, 14, 20)
EW = 11
SHARED = 16
SURFACE = 56

advect_rate = 0.25
mixing_rate = 0.015
salt_weight = 0.8


def lane_ids():
    return lax.broadcasted_iota(jnp.int32, (8, LANES), 1)


def merge(parts, lane):
    flat = []
    for low, width, value in parts:
        low %= LANES
        if low + width > LANES:
            flat.append((low, value))
            flat.append((0, value))
        else:
            flat.append((low, value))
    flat.sort(key=lambda part: part[0])
    result = flat[0][1]
    last = result
    for low, value in flat[1:]:
        if value is last:
            continue
        result = jnp.where(lane >= low, value, result)
        last = value
    return result


def turn(value, shift):
    shift %= LANES
    return pltpu.roll(value, shift, 1) if shift else value


class Source:
    def __init__(self, load):
        self.load = load
        self.kept = {}

    def tile(self, *key):
        if key not in self.kept:
            self.kept[key] = self.load(*key)
        return self.kept[key]

    def cells(self, position, start, width):
        parts = []
        at = start
        while at < start + width:
            number = at // LANES
            end = min(start + width, (number + 1) * LANES)
            parts.append((at, end - at, self.tile(position, number)))
            at = end
        return parts


def pack_columns(source, lane, group):
    rows = range(17 * group, min(17 * group + 17, BY))
    east = merge([c for r in rows for c in source.cells(1, BX * r + BX - REACH, REACH)], lane)
    west = merge([c for r in rows for c in source.cells(0, BX * r, REACH)], lane)
    return east, west


def strip_rows(source, lane):
    turned = {}

    def combined(r):
        if r not in turned:
            parts = source.cells(0, BX * r, BX) if r >= 0 else []
            if r + 1 < BY:
                parts += source.cells(1, BX * (r + 1), BX)
            turned[r] = turn(merge(parts, lane), BASE - BX * r)
        return turned[r]

    for r in range(-1, BY):
        combined(r)
    for row in range(BY):
        yield row, jnp.where(lane < BASE + BX, combined(row), combined(row - 1))


def message_tiles(message, block, field):
    tiles = [message[block, 2 * field], message[block, 2 * field + 1]]
    last = message[block, 8 + field // 2]
    tiles.append(turn(last, LANES - SHARED) if field % 2 else last)
    return lambda number: tiles[number]


def beside_rows(rows, west, east, lane):
    turned = {}

    def combined(r):
        if r not in turned:
            low, high = (BX * r - REACH) % LANES, BX * (r + 2) % LANES
            if not 0 <= r - 1 < BY:
                value = east((r + 2) // 17)
            elif not 0 <= r + 2 < BY:
                value = west((r - 1) // 17)
            elif low < high:
                inside = lane < high if high + REACH <= LANES else (lane >= low) & (lane < high)
                value = jnp.where(inside, west((r - 1) // 17), east((r + 2) // 17))
            else:
                inside = lane < low if low + REACH <= LANES else (lane >= high) & (lane < low)
                value = jnp.where(inside, east((r + 2) // 17), west((r - 1) // 17))
            turned[r] = turn(value, BASE - BX * r)
        return turned[r]

    for r in sorted({row + 1 for row in rows} | {row - 2 for row in rows}):
        combined(r)
    for row in rows:
        yield row, combined(row + 1), combined(row - 2)


def slot_swap(block_list):
    first = block_list[0]
    return jnp.where(first >= 0, first & 1, 1 - (block_list[1] & 1))


def over_level_blocks(work):
    def body(block, carry):
        work(block, pl.ds(pl.multiple_of(8 * block, 8), 8))
        return carry

    lax.fori_loop(0, TILES - 1, body, 0)
    work(TILES - 1, pl.ds(LEVELS - 8, 8))


def field_loader(ref, which, levels, swap):
    def load(position, number):
        slot = swap if position == 0 else 1 - swap
        if number < 14:
            return ref[slot, which, levels, number * LANES : (number + 1) * LANES]
        return turn(ref[slot, which, levels, CELLS - LANES : CELLS], CELLS % LANES)

    return load


def column_loader(wet_levels, mixing, swap):
    def load(position, number):
        slot = swap if position == 0 else 1 - swap
        low = number * LANES if number < 14 else CELLS - LANES
        both = wet_levels[:, low : low + LANES].astype(jnp.float32)
        depth = jnp.where(slot == 0, both[0:1, :], both[1:2, :])
        both = mixing[:, low : low + LANES]
        mix = jnp.where(slot == 0, both[0:1, :], both[1:2, :])
        sublane = lax.broadcasted_iota(jnp.int32, (8, LANES), 0)
        value = jnp.where(
            sublane == 0, jnp.broadcast_to(depth, (8, LANES)), jnp.broadcast_to(mix, (8, LANES))
        )
        return value if number < 14 else turn(value, CELLS % LANES)

    return load


def columns_kernel(
    block_list, wet_levels_far, mixing_far, damping_far, velocity, tracers,
    east, west, padded, wet_levels, mixing, damping, semaphores,
):
    lane = lane_ids()
    swap = slot_swap(block_list)
    sides = (east, west)
    copies = [
        pltpu.make_async_copy(far, near, semaphores.at[number])
        for number, (far, near) in enumerate(
            ((wet_levels_far, wet_levels), (mixing_far, mixing), (damping_far, damping))
        )
    ]
    for copy in copies:
        copy.start()

    def work(block, levels):
        sources = [Source(field_loader(ref, n, levels, swap)) for ref in (tracers, velocity) for n in range(2)]
        scales = (1.0, 1.0, 0.25 * advect_rate, 0.25 * advect_rate)
        lasts = [pack_columns(source, lane, 2) for source in sources]
        lasts = [[tile * scale for tile in both] for both, scale in zip(lasts, scales)]
        lasts = [[turn(tile, SHARED * (field % 2)) for tile in both] for field, both in enumerate(lasts)]
        for field, source in enumerate(sources):
            for number in range(2):
                for message, tile in zip(sides, pack_columns(source, lane, number)):
                    message[block, 2 * field + number] = tile * scales[field]
        for pair in range(2):
            for side, message in enumerate(sides):
                first = BX - REACH if side == 0 else 0
                lows = [BX * row + first for row in range(34, BY)]
                one, two = lasts[2 * pair][side], lasts[2 * pair + 1][side]
                parts = [(low, REACH, one) for low in lows] + [(low + SHARED, REACH, two) for low in lows]
                message[block, 8 + pair] = merge(parts, lane)

    over_level_blocks(work)
    for copy in copies:
        copy.wait()
    source = Source(column_loader(wet_levels, mixing, swap))
    extras = [pack_columns(source, lane, number) for number in range(3)]
    padded[...] = jnp.zeros_like(padded)
    padded[:, 0:WIDE] = damping[...]
    tiles = [padded[8 * j : 8 * j + 8, :] for j in range(5)]
    extras.append(
        (
            merge([(2 * j, 2, turn(t, 2 * j - WIDE + 2)) for j, t in enumerate(tiles)], lane),
            merge([(2 * j, 2, turn(t, 2 * j)) for j, t in enumerate(tiles)], lane),
        )
    )
    for block in range(TILES):
        for side, message in enumerate(sides):
            message[block, EW - 1] = extras[min(block, 3)][side]


def strips_kernel(block_list, wet_levels, mixing, damping, velocity, tracers, fields, columns, padded):
    lane = lane_ids()
    swap = slot_swap(block_list)
    padded[...] = jnp.zeros_like(padded)
    padded[:, 0:WIDE] = damping[...]
    for j in range(5):
        padded[8 * j : 8 * j + 8, :] = turn(padded[8 * j : 8 * j + 8, :], BASE)
    sublane = lax.broadcasted_iota(jnp.int32, (8, LANES), 0)
    for row, value in strip_rows(Source(column_loader(wet_levels, mixing, swap)), lane):
        damp = jnp.broadcast_to(padded[row : row + 1, :], (8, LANES))
        columns[row] = jnp.where(sublane == 2, damp, value)

    def work(block, levels):
        for field in range(4):
            ref = tracers if field < 2 else velocity
            for row, value in strip_rows(Source(field_loader(ref, field % 2, levels, swap)), lane):
                fields[block, field, row] = value if field < 2 else (0.25 * advect_rate) * value

    over_level_blocks(work)


def place_halos(own_fields, own_columns, from_west, from_east, low_damp, high_damp, rows, put):
    lane = lane_ids()
    sublane = lax.broadcasted_iota(jnp.int32, (8, LANES), 0)
    for j in range(5):
        low_damp[8 * j : 8 * j + 8, :] = turn(from_west[3, EW - 1], BASE - 2 - 2 * j)
        high_damp[8 * j : 8 * j + 8, :] = turn(from_east[3, EW - 1], BASE + WIDE - 2 * j)
    sides = beside_rows(rows, lambda t: from_west[t, EW - 1], lambda t: from_east[t, EW - 1], lane)
    for row, west, east in sides:
        west = jnp.where(sublane == 2, jnp.broadcast_to(low_damp[row : row + 1, :], (8, LANES)), west)
        east = jnp.where(sublane == 2, jnp.broadcast_to(high_damp[row : row + 1, :], (8, LANES)), east)
        value = jnp.where(lane < BASE, west, own_columns[row])
        put(0, 4, row, jnp.where(lane < BASE + WIDE, value, east))

    def work(block, carry):
        for field in range(4):
            sides = beside_rows(
                rows,
                message_tiles(from_west, block, field),
                message_tiles(from_east, block, field),
                lane,
            )
            for row, west, east in sides:
                value = jnp.where(lane < BASE, west, own_fields[block, field, row])
                put(block, field, row, jnp.where(lane < BASE + WIDE, value, east))
        return carry

    lax.fori_loop(0, TILES, work, 0)


def row_message_kernel(parity, own_fields, own_columns, from_west, from_east, chip, link, low_damp, high_damp):
    def write(up, down):
        def put(block, field, row, value):
            if row < REACH:
                target, number = down, row
            else:
                target, number = up, row - (BY - REACH)
            if field == 4:
                target[number, NS - 1] = value
            elif field < 2:
                target[block, FIELD_AT[field] + number] = value
            elif row < REACH - 1:
                target[block, FIELD_AT[field] + number] = value
            elif row > BY - REACH:
                target[block, FIELD_AT[field] + number - 1] = value

        rows = (*range(REACH), *range(BY - REACH, BY))
        place_halos(own_fields, own_columns, from_west, from_east, low_damp, high_damp, rows, put)

    for message in (chip, link):
        message[TILES - 1, NS - 1] = jnp.zeros((8, LANES), jnp.float32)

    @pl.when(parity[0] == 0)
    def _():
        write(chip, link)

    @pl.when(parity[0] != 0)
    def _():
        write(link, chip)


def halo_kernel(own_fields, own_columns, from_west, from_east, fields, columns, low_damp, high_damp):
    def put(block, field, row, value):
        if field == 4:
            columns[row] = value
        else:
            fields[block, field, row] = value

    place_halos(own_fields, own_columns, from_west, from_east, low_damp, high_damp, range(BY), put)


def staggered(spans, phases):
    state = {}
    length = max(high - low + 1 for low, high in spans)
    ahead = min(AHEAD, length)
    for time in range(length + ahead * (len(phases) - 1)):
        for number in reversed(range(len(phases))):
            for span, (low, high) in enumerate(spans):
                row = low + time - number * ahead
                if low <= row <= high:
                    phases[number](span, row, state)


class Band:
    def __init__(self, low, high, read, write, eastward, northward, levels, part=0):
        self.low, self.high, self.read, self.write = low, high, read, write
        self.eastward, self.northward = eastward, northward
        self.levels, self.part = levels, 2 * part


def advance(bands, shared, scratch):
    depth_east, depth_north, mix = shared
    scaled, held = scratch

    def rise(band, n, row):
        read = bands[band].read
        return jnp.where(bands[band].levels < depth_north(row), read(n, row + 1) - read(n, row), 0.0)

    def look_east(band, row, state):
        for n in range(2):
            state[band, n, row] = turn(bands[band].read(n, row), LANES - 1)

    def step_east(band, row, state):
        wet = bands[band].levels < depth_east(row)
        for n in range(2):
            here, beside = bands[band].read(n, row), state[band, n, row]
            step = jnp.where(wet, beside - here, 0.0)
            state[band, n, row] = step, turn(step, 1)
            held[bands[band].part + n, row + REACH] = beside + here

    def scale(band, row, state):
        for n in range(2):
            step, back = state.pop((band, n, row))
            drop = state.pop((band, n)) if (band, n) in state else rise(band, n, row - 1)
            state[band, n] = rise(band, n, row)
            scaled[bands[band].part + n, row + REACH] = mix(row) * ((step - back) + (state[band, n] - drop))

    staggered([(b.low - 1, b.high + 1) for b in bands], (look_east, step_east, scale))

    def north_flow(band, n, row):
        read, northward = bands[band].read, bands[band].northward
        step = scaled[bands[band].part + n, row + 1 + REACH] - scaled[bands[band].part + n, row + REACH]
        both = (northward(row) + northward(row + 1)) * (read(n, row) + read(n, row + 1)) + step
        return jnp.where(bands[band].levels < depth_north(row), both, 0.0)

    def look_east_again(band, row, state):
        state[band, "flow", row] = turn(bands[band].eastward(row), LANES - 1)
        for n in range(2):
            state[band, n, row] = turn(scaled[bands[band].part + n, row + REACH], LANES - 1)

    def east_flow(band, row, state):
        wet = bands[band].levels < depth_east(row)
        flow = bands[band].eastward(row) + state.pop((band, "flow", row))
        for n in range(2):
            at = row + REACH
            both = flow * held[bands[band].part + n, at] + (state[band, n, row] - scaled[bands[band].part + n, at])
            both = jnp.where(wet, both, 0.0)
            state[band, n, row] = both, turn(both, 1)

    def change(band, row, state):
        for n in range(2):
            east, back = state.pop((band, n, row))
            south = state.pop((band, n)) if (band, n) in state else north_flow(band, n, row - 1)
            state[band, n] = north_flow(band, n, row)
            result = bands[band].read(n, row) - ((east - back) + (state[band, n] - south))
            bands[band].write(n, row, result)

    staggered([(b.low, b.high) for b in bands], (look_east_again, east_flow, change))


def level_ids(step):
    sublane = lax.broadcasted_iota(jnp.int32, (8, LANES), 0)
    last = step == TILES - 1
    twice = last & (sublane < 8 * TILES - LEVELS)
    numbers = sublane + jnp.where(last, LEVELS - 8, 8 * step)
    return jnp.where(twice, LEVELS, numbers).astype(jnp.float32)


def spread_columns(column, rows, depth, depth_east, depth_north, mix):
    last = None
    for row in rows:
        value = column(row)
        here = jnp.broadcast_to(value[0:1, :], (8, LANES))
        depth[row + REACH] = here
        depth_east[row + REACH] = jnp.minimum(here, turn(here, LANES - 1))
        mix[row + REACH] = mixing_rate * jnp.broadcast_to(value[1:2, :], (8, LANES))
        if last is not None:
            depth_north[row + REACH - 1] = jnp.minimum(here, last)
        last = here


def contribution(levels, depth, warm, salt):
    return jnp.where(levels < depth, warm - salt_weight * salt, 0.0)


def inner_kernel(
    fields, columns, halfway, moved, forcing,
    middle, depth, depth_east, depth_north, mix, scaled, held,
):
    step = pl.program_id(0)

    @pl.when(step == 0)
    def _():
        spread_columns(lambda row: columns[row], range(BY), depth, depth_east, depth_north, mix)
        forcing[...] = jnp.zeros_like(forcing)

    levels = level_ids(step)
    shared = (
        lambda row: depth_east[row + REACH],
        lambda row: depth_north[row + REACH],
        lambda row: mix[row + REACH],
    )

    def write_middle(n, row, value):
        middle[n, row] = value
        if row < 6:
            halfway[0, n, row - 2] = value
        if row >= 34:
            halfway[0, n, row - 30] = value

    def write_moved(n, row, value):
        moved[0, n, row - 4] = value

    def eastward(row):
        return fields[0, 2, row]

    def northward(row):
        return fields[0, 3, row]

    first = Band(2, 37, lambda n, row: fields[0, n, row], write_middle, eastward, northward, levels)
    second = Band(4, 35, lambda n, row: middle[n, row], write_moved, eastward, northward, levels)
    advance([first], shared, (scaled, held))
    advance([second], shared, (scaled, held))
    for row in range(4, 36):
        forcing[row] += contribution(
            levels, depth[row + REACH], moved[0, 0, row - 4], moved[0, 1, row - 4]
        )


def surface_operator(values, couple_east, couple_north, damping):
    east = couple_east * (values - turn(values, LANES - 1))
    north = couple_north * (values - pltpu.roll(values, SURFACE - 1, 0))
    return damping * values + ((east - turn(east, 1)) + (north - pltpu.roll(north, 1, 0)))


def outer_kernel(parity, low_fields, high_fields, columns, chip, link, chip_extra, link_extra, *others):
    @pl.when(parity[0] == 0)
    def _():
        outer_rows(low_fields, high_fields, columns, link, chip, link_extra, chip_extra, *others)

    @pl.when(parity[0] != 0)
    def _():
        outer_rows(low_fields, high_fields, columns, chip, link, chip_extra, link_extra, *others)


def outer_rows(
    low_fields, high_fields, columns, up, down, up_extra, down_extra, halfway, inner_forcing,
    moved, basis, moments,
    middle, beyond, depth, depth_east, depth_north, mix, scaled, held, forcing, surface, depths, dampings,
):
    step = pl.program_id(0)

    def column(row):
        if row < 0:
            return up_extra[row + REACH, 0]
        if row >= BY:
            return down_extra[row - BY, 0]
        return columns[row]

    rows = range(-REACH, BY + REACH)

    @pl.when(step == 0)
    def _():
        spread_columns(column, rows, depth, depth_east, depth_north, mix)
        forcing[...] = jnp.zeros_like(forcing)

    shared = (
        lambda row: depth_east[row + REACH],
        lambda row: depth_north[row + REACH],
        lambda row: mix[row + REACH],
    )
    first, second = [], []
    for part in range(PARTS):
        levels = level_ids(PARTS * step + part)

        def field(number, row, part=part):
            if row < 0:
                return up[part, FIELD_AT[number] + row + (REACH if number < 2 else REACH - 1)]
            if row >= BY:
                return down[part, FIELD_AT[number] + row - BY]
            return low_fields[part, number, row] if row < 10 else high_fields[part, number, row - 30]

        def read_middle(n, row, part=part):
            if 2 <= row < 6:
                return halfway[part, n, row - 2]
            if 34 <= row < 38:
                return halfway[part, n, row - 30]
            return middle[2 * part + n, row + REACH]

        def write_middle(n, row, value, part=part):
            middle[2 * part + n, row + REACH] = value

        def write_beyond(n, row, value, part=part):
            beyond[2 * part + n, row + REACH] = value
            if 0 <= row < 4:
                moved[part, n, row] = value
            if 36 <= row < BY:
                moved[part, n, row - 32] = value

        flows = (functools.partial(field, 2), functools.partial(field, 3), levels, part)
        first += [Band(low, high, field, write_middle, *flows) for low, high in ((-5, 1), (38, 44))]
        second += [Band(low, high, read_middle, write_beyond, *flows) for low, high in ((-3, 3), (36, 42))]
    advance(first, shared, (scaled, held))
    advance(second, shared, (scaled, held))
    for row in (*range(-3, 4), *range(36, 43)):
        at = row + REACH
        for part in range(PARTS):
            forcing[at] += contribution(
                second[2 * part].levels, depth[at], beyond[2 * part, at], beyond[2 * part + 1, at]
            )

    @pl.when(step == TILES // PARTS - 1)
    def _():
        surface[...] = jnp.zeros_like(surface)
        for row in range(-3, 43):
            part = inner_forcing[row] if 4 <= row < 36 else forcing[row + REACH]
            total = jnp.sum(part, axis=0, keepdims=True)
            surface[row + 8 : row + 9, :] = total * (1.0 / math.sqrt(LEVELS))
        depths[...] = jnp.zeros_like(depths)
        dampings[...] = jnp.zeros_like(dampings)
        for row in rows:
            value = column(row)
            depths[row + 8 : row + 9, :] = value[0:1, :]
            dampings[row + 8 : row + 9, :] = value[2:3, :]
        here = depths[...]
        couple_east = jnp.minimum(here, turn(here, LANES - 1)) * (1.0 / LEVELS)
        couple_north = jnp.minimum(here, pltpu.roll(here, SURFACE - 1, 0)) * (1.0 / LEVELS)
        diagonal = dampings[...]
        powers = [surface[...]]
        for _ in range(3):
            powers.append(surface_operator(powers[-1], couple_east, couple_north, diagonal))
        row_id = lax.broadcasted_iota(jnp.int32, (SURFACE, LANES), 0)
        lane_id = lax.broadcasted_iota(jnp.int32, (SURFACE, LANES), 1)
        own = (row_id >= 8) & (row_id < 8 + BY) & (lane_id >= BASE) & (lane_id < BASE + WIDE)
        moments[...] = jnp.zeros_like(moments)
        for k in range(6):
            product = jnp.where(own, powers[k // 2] * powers[(k + 1) // 2], 0.0)
            moments[k : k + 1, :] = jnp.sum(product, axis=0, keepdims=True)
        for k in range(3):
            basis[k] = turn(powers[k], LANES - BASE)[8 : 8 + BY, :]


def to_slots(numbers, start, rows, load, block_list, out, group, width, ahead):
    lane = lane_ids()
    swap = slot_swap(block_list)
    pieces = [numbers[i : i + width] for i in range(0, len(numbers), width)]

    def rotations(block, n, piece):
        cells = [c for t in piece for c in range(t * LANES, min((t + 1) * LANES, CELLS))]
        turned = {}
        for r in sorted({c // BX - p for c in cells for p in range(2)}):
            low, high = (min(max(row, rows[0]), rows[1]) for row in (r, r + 1))
            value = jnp.where(lane < BASE + BX, load(block, n, low), load(block, n, high))
            turned[r] = turn(value, BX * r - BASE)
        return turned

    def place(block, last, n, piece, turned):
        for number in piece:
            for position in range(2):
                slot = swap if position == 0 else 1 - swap
                first, end = number * LANES, min((number + 1) * LANES, CELLS)
                parts = []
                for row in range(first // BX, (end - 1) // BX + 1):
                    low = max(row * BX, first)
                    parts.append((low, min((row + 1) * BX, end) - low, turned[row - position]))
                value = merge(parts, lane)[:, 0 : end - first]
                if last:
                    rest = value[8 * TILES - LEVELS : 8]
                    out[slot, 8 * TILES - 8 : LEVELS, n, first - start : end - start] = rest
                else:
                    out[slot, pl.ds(8 * block, 8), n, first - start : end - start] = value

    def work(blocks):
        jobs = [(block, last, n, piece) for block, last in blocks for n in range(2) for piece in pieces]
        ready = [rotations(block, n, piece) for block, _, n, piece in jobs[:ahead]]
        for index, (block, last, n, piece) in enumerate(jobs):
            if index + ahead < len(jobs):
                later = jobs[index + ahead]
                ready.append(rotations(later[0], later[2], later[3]))
            place(block, last, n, piece, ready[index])
            ready[index] = None

    def body(index, carry):
        work([(group * index + i, False) for i in range(group)])
        return carry

    lax.fori_loop(0, TILES // group - 1, body, 0)
    work([(block, block == TILES - 1) for block in range(TILES - group, TILES)])


def inner_slots_kernel(block_list, moved, out, cells, semaphore):
    to_slots(tuple(range(2, 12)), 2 * LANES, (4, 35), lambda block, n, row: moved[block, n, row - 4], block_list, cells, *INNER_PLAN)
    copy = pltpu.make_async_copy(cells, out.at[:, :, :, 2 * LANES : 12 * LANES], semaphore)
    copy.start()
    copy.wait()


def outer_slots_kernel(numbers, block_list, moved, edges, inner, out, cells, semaphore):
    def load(block, n, row):
        if 4 <= row < 36:
            return moved[block, n, row - 4]
        return edges[block, n, row if row < 4 else row - 32]

    start, end = numbers[0] * LANES, min((numbers[-1] + 1) * LANES, CELLS)
    to_slots(numbers, start, (0, BY - 1), load, block_list, cells, *OUTER_PLAN)
    copy = pltpu.make_async_copy(cells, out.at[:, :, :, start:end], semaphore)
    copy.start()
    copy.wait()


def finish_kernel(first, second, third, fourth, basis, out):
    moments = (first[...] + second[...]) + (third[...] + fourth[...])
    totals = jnp.sum(moments, axis=1, keepdims=True)
    m = [totals[k : k + 1, :] for k in range(6)]
    low10 = m[2] / m[1]
    low20 = m[3] / m[1]
    pivot1 = m[3] - low10 * m[2]
    part21 = m[4] - low20 * m[2]
    low21 = part21 / pivot1
    pivot2 = m[5] - low20 * m[3] - low21 * part21
    y1 = m[1] - low10 * m[0]
    y2 = m[2] - low20 * m[0] - low21 * y1
    z2 = y2 / pivot2
    z1 = y1 / pivot1 - low21 * z2
    z0 = m[0] / m[1] - low10 * z1 - low20 * z2
    value = z0 * basis[0] + z1 * basis[1] + z2 * basis[2]
    out[...] = value[:, 0:WIDE]


def quad(values, axis, partner):
    count = lax.axis_size(axis)
    others = [
        lax.ppermute(values, axis, [(i, partner(i, turn)) for i in range(count)])
        for turn in range(1, 4)
    ]
    return [values, *others]


def quad_sum(values, axis, partner):
    four = quad(values, axis, partner)
    return (four[0] + four[1]) + (four[2] + four[3])


def terms_over_devices(values, beside):
    values = values + lax.ppermute(values, "gy", [(i, i ^ 1) for i in range(lax.axis_size("gy"))])
    values = quad_sum(values, "gy", lambda i, turn: i ^ (2 * turn))
    values, done = lax.optimization_barrier((values, beside[0]()))
    values = quad_sum(values, "gx", lambda i, turn: i ^ turn)
    values, done = lax.optimization_barrier((values, beside[1](done)))
    return quad(values, "gx", lambda i, turn: i ^ (4 * turn)), done


def held_in_vmem(arrays):
    return [pltpu.with_memory_space_constraint(a, pltpu.VMEM) for a in arrays]


def vmem(kind):
    return pltpu.VMEM(kind.shape, kind.dtype)


def whole(shape):
    return pl.BlockSpec(shape, lambda k: (0,) * len(shape))


def per_device(block_list, wet_levels, mixing, velocity, tracers, damping):
    f32 = jnp.float32
    slots, fields_each, levels, cells = tracers.shape
    params = pltpu.CompilerParams(
        dimension_semantics=("arbitrary",), vmem_limit_bytes=40 * 1024 * 1024
    )

    def tiles(*shape):
        zeros = (0,) * (len(shape) + 2)
        return (
            pl.BlockSpec((1, *shape, 8, LANES), lambda k: (k, *zeros)),
            jax.ShapeDtypeStruct((TILES, *shape, 8, LANES), f32),
        )

    _, rows_type = tiles(NS)
    _, columns_type = tiles(EW)
    rows_extra = pl.BlockSpec((TILES, 1, 8, LANES), lambda k: (0, NS - 1, 0, 0))
    in_vmem = pl.BlockSpec(memory_space=pltpu.VMEM)
    own_specs = [pl.BlockSpec(memory_space=pltpu.SMEM)] + [in_vmem] * 5
    own = (block_list, *held_in_vmem((wet_levels, mixing, damping, velocity, tracers)))
    whole_params = pltpu.CompilerParams(vmem_limit_bytes=40 * 1024 * 1024)

    east, west = pl.pallas_call(
        columns_kernel,
        in_specs=own_specs[:1] + [pl.BlockSpec(memory_space=pl.ANY)] * 3 + [in_vmem] * 2,
        out_specs=[in_vmem] * 2,
        out_shape=[vmem(columns_type)] * 2,
        scratch_shapes=[
            pltpu.VMEM((BY, LANES), f32),
            pltpu.VMEM(wet_levels.shape, jnp.int32),
            pltpu.VMEM(mixing.shape, f32),
            pltpu.VMEM(damping.shape, f32),
            pltpu.SemaphoreType.DMA((3,)),
        ],
        compiler_params=whole_params,
        name="pack_columns",
    )(block_list, wet_levels, mixing, damping, *own[4:])
    columns_total = lax.axis_size("gx")
    from_west = lax.ppermute(east, "gx", [(i, (i + 1) % columns_total) for i in range(columns_total)])
    from_east = lax.ppermute(west, "gx", [((i + 1) % columns_total, i) for i in range(columns_total)])

    fields_block, fields_type = tiles(4, BY)
    column_shape = (BY, 8, LANES)
    column_type = jax.ShapeDtypeStruct(column_shape, f32)
    own_strips = pl.pallas_call(
        strips_kernel,
        in_specs=own_specs,
        out_specs=[in_vmem] * 2,
        out_shape=[vmem(fields_type), vmem(column_type)],
        scratch_shapes=[pltpu.VMEM((BY, LANES), f32)],
        compiler_params=whole_params,
        cost_estimate=pl.CostEstimate(flops=30_000_000, bytes_accessed=9_000_000, transcendentals=0),
        name="strips",
    )(*own)
    with_halos = held_in_vmem((*own_strips, from_west, from_east))
    parity = (lax.axis_index("gy") & 1).astype(jnp.int32).reshape(1)
    chip, link = pl.pallas_call(
        row_message_kernel,
        in_specs=[pl.BlockSpec(memory_space=pltpu.SMEM)] + [in_vmem] * 4,
        out_specs=[in_vmem] * 2,
        out_shape=[vmem(rows_type)] * 2,
        scratch_shapes=[pltpu.VMEM((BY, LANES), f32)] * 2,
        compiler_params=whole_params,
        name="row_message",
    )(parity, *with_halos)
    fields, columns = pl.pallas_call(
        halo_kernel,
        in_specs=[in_vmem] * 4,
        out_specs=[in_vmem] * 2,
        out_shape=[vmem(fields_type), vmem(column_type)],
        scratch_shapes=[pltpu.VMEM((BY, LANES), f32)] * 2,
        compiler_params=whole_params,
        cost_estimate=pl.CostEstimate(flops=30_000_000, bytes_accessed=9_000_000, transcendentals=0),
        name="halos",
    )(*with_halos)
    rows_total = lax.axis_size("gy")
    pairs = [(i, i ^ 1) for i in range(rows_total)]
    from_chip = lax.ppermute(chip, "gy", pairs)
    pairs = [pair for i in range(1, rows_total - 1, 2) for pair in ((i, i + 1), (i + 1, i))]
    from_link = lax.ppermute(link, "gy", pairs)

    row_store = pltpu.VMEM((ROWS, 8, LANES), f32)
    pair_store = pltpu.VMEM((2, ROWS, 8, LANES), f32)
    halfway_block, halfway_type = tiles(2, 8)
    moved_block, moved_type = tiles(2, 32)
    halfway, moved, forcing = pl.pallas_call(
        inner_kernel,
        grid=(TILES,),
        in_specs=[fields_block, whole(column_shape)],
        out_specs=[halfway_block, moved_block, whole(column_shape)],
        out_shape=[halfway_type, moved_type, jax.ShapeDtypeStruct(column_shape, f32)],
        scratch_shapes=[pair_store] + [row_store] * 4 + [pair_store] * 2,
        compiler_params=params,
        cost_estimate=pl.CostEstimate(flops=60_000_000, bytes_accessed=10_000_000, transcendentals=0),
        name="inner_rows",
    )(fields, columns)

    slots_type = jax.ShapeDtypeStruct((slots, levels, fields_each, cells), f32)
    inner_slots = pl.pallas_call(
        inner_slots_kernel,
        in_specs=[pl.BlockSpec(memory_space=pltpu.SMEM), in_vmem],
        out_specs=pl.BlockSpec(memory_space=pl.ANY),
        out_shape=slots_type,
        scratch_shapes=[
            pltpu.VMEM((slots, levels, fields_each, 10 * LANES), f32),
            pltpu.SemaphoreType.DMA,
        ],
        compiler_params=whole_params,
        cost_estimate=pl.CostEstimate(flops=20_000_000, bytes_accessed=6_000_000, transcendentals=0),
        name="inner_slots",
    )(block_list, moved)
    inner_slots, forcing = lax.optimization_barrier((inner_slots, forcing))

    low_block = pl.BlockSpec((PARTS, 4, 10, 8, LANES), lambda k: (k, 0, 0, 0, 0))
    high_block = pl.BlockSpec((PARTS, 4, 10, 8, LANES), lambda k: (k, 0, 3, 0, 0))
    part_rows = pl.BlockSpec((PARTS, NS, 8, LANES), lambda k: (k, 0, 0, 0))
    part_halfway = pl.BlockSpec((PARTS, 2, 8, 8, LANES), lambda k: (k, 0, 0, 0, 0))
    parts_store = pltpu.VMEM((2 * PARTS, ROWS, 8, LANES), f32)
    edges, basis, moments = pl.pallas_call(
        outer_kernel,
        grid=(TILES // PARTS,),
        in_specs=[pl.BlockSpec(memory_space=pltpu.SMEM), low_block, high_block, whole(column_shape)]
        + [part_rows, part_rows]
        + [rows_extra, rows_extra, part_halfway, whole(column_shape)],
        out_specs=[part_halfway, whole((3, BY, LANES)), whole((8, LANES))],
        out_shape=[
            halfway_type,
            jax.ShapeDtypeStruct((3, BY, LANES), f32),
            jax.ShapeDtypeStruct((8, LANES), f32),
        ],
        scratch_shapes=[parts_store] * 2
        + [row_store] * 4
        + [parts_store] * 2
        + [row_store]
        + [pltpu.VMEM((SURFACE, LANES), f32)] * 3,
        compiler_params=params,
        name="outer_rows",
    )(parity, fields, fields, columns, from_chip, from_link, from_chip, from_link, halfway, forcing)

    def outer_slots(numbers, before):
        width = min((numbers[-1] + 1) * LANES, cells) - numbers[0] * LANES
        return pl.pallas_call(
            functools.partial(outer_slots_kernel, numbers),
            in_specs=[pl.BlockSpec(memory_space=pltpu.SMEM), in_vmem, in_vmem]
            + [pl.BlockSpec(memory_space=pl.ANY)],
            out_specs=pl.BlockSpec(memory_space=pl.ANY),
            out_shape=slots_type,
            scratch_shapes=[
                pltpu.VMEM((slots, levels, fields_each, width), f32),
                pltpu.SemaphoreType.DMA,
            ],
            input_output_aliases={3: 0},
            compiler_params=whole_params,
            cost_estimate=pl.CostEstimate(flops=2_000_000, bytes_accessed=2_000_000, transcendentals=0),
            name="outer_slots",
        )(block_list, moved, edges, before)

    beside = (lambda: outer_slots((0, 1), inner_slots), lambda before: outer_slots((12, 13, 14), before))
    moments, new_tracers = terms_over_devices(moments, beside)
    new_tracers = jnp.transpose(new_tracers, (0, 2, 1, 3))
    height = pl.pallas_call(
        finish_kernel,
        in_specs=[in_vmem] * 5,
        out_specs=in_vmem,
        out_shape=jax.ShapeDtypeStruct((BY, WIDE), f32),
        name="finish",
    )(*held_in_vmem((*moments, basis)))
    return (new_tracers, height)


def solution(mesh):
    return jax.shard_map(
        per_device,
        mesh=mesh,
        in_specs=(
            P(("gx", "gy")),
            P(("gx", "gy"), None),
            P(("gx", "gy"), None),
            P(("gx", "gy"), None, None, None),
            P(("gx", "gy"), None, None, None),
            P("gy", "gx"),
        ),
        out_specs=(P(("gx", "gy"), None, None, None), P("gy", "gx")),
        check_vma=False,
    )
```

```python
import functools
import math

import jax
import jax.numpy as jnp
from jax import lax
from jax.experimental import pallas as pl
from jax.experimental.pallas import tpu as pltpu
from jax.sharding import PartitionSpec as P

BX = 45
BY = 40
CELLS = BX * BY
LEVELS = 62
LANES = 128
TILES = 8
REACH = 7
ROWS = BY + 2 * REACH
PARTS = 2
INNER_PLAN = (2, 5, 2)
OUTER_PLAN = (4, 3, 4)
AHEAD = 26
BASE = 8
WIDE = 2 * BX
NS = 27
FIELD_AT = (0, 7, 14, 20)
EW = 11
SHARED = 16
SURFACE = 56

advect_rate = 0.25
mixing_rate = 0.015
salt_weight = 0.8


def lane_ids():
    return lax.broadcasted_iota(jnp.int32, (8, LANES), 1)


def merge(parts, lane):
    flat = []
    for low, width, value in parts:
        low %= LANES
        if low + width > LANES:
            flat.append((low, value))
            flat.append((0, value))
        else:
            flat.append((low, value))
    flat.sort(key=lambda part: part[0])
    result = flat[0][1]
    last = result
    for low, value in flat[1:]:
        if value is last:
            continue
        result = jnp.where(lane >= low, value, result)
        last = value
    return result


def turn(value, shift):
    shift %= LANES
    return pltpu.roll(value, shift, 1) if shift else value


class Source:
    def __init__(self, load):
        self.load = load
        self.kept = {}

    def tile(self, *key):
        if key not in self.kept:
            self.kept[key] = self.load(*key)
        return self.kept[key]

    def cells(self, position, start, width):
        parts = []
        at = start
        while at < start + width:
            number = at // LANES
            end = min(start + width, (number + 1) * LANES)
            parts.append((at, end - at, self.tile(position, number)))
            at = end
        return parts


def pack_columns(source, lane, group):
    rows = range(17 * group, min(17 * group + 17, BY))
    east = merge([c for r in rows for c in source.cells(1, BX * r + BX - REACH, REACH)], lane)
    west = merge([c for r in rows for c in source.cells(0, BX * r, REACH)], lane)
    return east, west


def strip_rows(source, lane):
    turned = {}

    def combined(r):
        if r not in turned:
            parts = source.cells(0, BX * r, BX) if r >= 0 else []
            if r + 1 < BY:
                parts += source.cells(1, BX * (r + 1), BX)
            turned[r] = turn(merge(parts, lane), BASE - BX * r)
        return turned[r]

    for r in range(-1, BY):
        combined(r)
    for row in range(BY):
        yield row, jnp.where(lane < BASE + BX, combined(row), combined(row - 1))


def message_tiles(message, block, field):
    tiles = [message[block, 2 * field], message[block, 2 * field + 1]]
    last = message[block, 8 + field // 2]
    tiles.append(turn(last, LANES - SHARED) if field % 2 else last)
    return lambda number: tiles[number]


def beside_rows(rows, west, east, lane):
    turned = {}

    def combined(r):
        if r not in turned:
            low, high = (BX * r - REACH) % LANES, BX * (r + 2) % LANES
            if not 0 <= r - 1 < BY:
                value = east((r + 2) // 17)
            elif not 0 <= r + 2 < BY:
                value = west((r - 1) // 17)
            elif low < high:
                inside = lane < high if high + REACH <= LANES else (lane >= low) & (lane < high)
                value = jnp.where(inside, west((r - 1) // 17), east((r + 2) // 17))
            else:
                inside = lane < low if low + REACH <= LANES else (lane >= high) & (lane < low)
                value = jnp.where(inside, east((r + 2) // 17), west((r - 1) // 17))
            turned[r] = turn(value, BASE - BX * r)
        return turned[r]

    for r in sorted({row + 1 for row in rows} | {row - 2 for row in rows}):
        combined(r)
    for row in rows:
        yield row, combined(row + 1), combined(row - 2)


def slot_swap(block_list):
    first = block_list[0]
    return jnp.where(first >= 0, first & 1, 1 - (block_list[1] & 1))


def over_level_blocks(work):
    def body(block, carry):
        work(block, pl.ds(pl.multiple_of(8 * block, 8), 8))
        return carry

    lax.fori_loop(0, TILES - 1, body, 0)
    work(TILES - 1, pl.ds(LEVELS - 8, 8))


def field_loader(ref, which, levels, swap):
    def load(position, number):
        slot = swap if position == 0 else 1 - swap
        if number < 14:
            return ref[slot, which, levels, number * LANES : (number + 1) * LANES]
        return turn(ref[slot, which, levels, CELLS - LANES : CELLS], CELLS % LANES)

    return load


def column_loader(wet_levels, mixing, swap):
    def load(position, number):
        slot = swap if position == 0 else 1 - swap
        low = number * LANES if number < 14 else CELLS - LANES
        both = wet_levels[:, low : low + LANES].astype(jnp.float32)
        depth = jnp.where(slot == 0, both[0:1, :], both[1:2, :])
        both = mixing[:, low : low + LANES]
        mix = jnp.where(slot == 0, both[0:1, :], both[1:2, :])
        sublane = lax.broadcasted_iota(jnp.int32, (8, LANES), 0)
        value = jnp.where(
            sublane == 0, jnp.broadcast_to(depth, (8, LANES)), jnp.broadcast_to(mix, (8, LANES))
        )
        return value if number < 14 else turn(value, CELLS % LANES)

    return load


def columns_kernel(
    block_list, wet_levels_far, mixing_far, damping_far, velocity, tracers,
    east, west, padded, wet_levels, mixing, damping, semaphores,
):
    lane = lane_ids()
    swap = slot_swap(block_list)
    sides = (east, west)
    copies = [
        pltpu.make_async_copy(far, near, semaphores.at[number])
        for number, (far, near) in enumerate(
            ((wet_levels_far, wet_levels), (mixing_far, mixing), (damping_far, damping))
        )
    ]
    for copy in copies:
        copy.start()

    def work(block, levels):
        sources = [Source(field_loader(ref, n, levels, swap)) for ref in (tracers, velocity) for n in range(2)]
        scales = (1.0, 1.0, 0.25 * advect_rate, 0.25 * advect_rate)
        lasts = [pack_columns(source, lane, 2) for source in sources]
        lasts = [[tile * scale for tile in both] for both, scale in zip(lasts, scales)]
        lasts = [[turn(tile, SHARED * (field % 2)) for tile in both] for field, both in enumerate(lasts)]
        for field, source in enumerate(sources):
            for number in range(2):
                for message, tile in zip(sides, pack_columns(source, lane, number)):
                    message[block, 2 * field + number] = tile * scales[field]
        for pair in range(2):
            for side, message in enumerate(sides):
                first = BX - REACH if side == 0 else 0
                lows = [BX * row + first for row in range(34, BY)]
                one, two = lasts[2 * pair][side], lasts[2 * pair + 1][side]
                parts = [(low, REACH, one) for low in lows] + [(low + SHARED, REACH, two) for low in lows]
                message[block, 8 + pair] = merge(parts, lane)

    over_level_blocks(work)
    for copy in copies:
        copy.wait()
    source = Source(column_loader(wet_levels, mixing, swap))
    extras = [pack_columns(source, lane, number) for number in range(3)]
    padded[...] = jnp.zeros_like(padded)
    padded[:, 0:WIDE] = damping[...]
    tiles = [padded[8 * j : 8 * j + 8, :] for j in range(5)]
    extras.append(
        (
            merge([(2 * j, 2, turn(t, 2 * j - WIDE + 2)) for j, t in enumerate(tiles)], lane),
            merge([(2 * j, 2, turn(t, 2 * j)) for j, t in enumerate(tiles)], lane),
        )
    )
    for block in range(TILES):
        for side, message in enumerate(sides):
            message[block, EW - 1] = extras[min(block, 3)][side]


def strips_kernel(block_list, wet_levels, mixing, damping, velocity, tracers, fields, columns, padded):
    lane = lane_ids()
    swap = slot_swap(block_list)
    padded[...] = jnp.zeros_like(padded)
    padded[:, 0:WIDE] = damping[...]
    for j in range(5):
        padded[8 * j : 8 * j + 8, :] = turn(padded[8 * j : 8 * j + 8, :], BASE)
    sublane = lax.broadcasted_iota(jnp.int32, (8, LANES), 0)
    for row, value in strip_rows(Source(column_loader(wet_levels, mixing, swap)), lane):
        damp = jnp.broadcast_to(padded[row : row + 1, :], (8, LANES))
        columns[row] = jnp.where(sublane == 2, damp, value)

    def work(block, levels):
        for field in range(4):
            ref = tracers if field < 2 else velocity
            for row, value in strip_rows(Source(field_loader(ref, field % 2, levels, swap)), lane):
                fields[block, field, row] = value if field < 2 else (0.25 * advect_rate) * value

    over_level_blocks(work)


def place_halos(own_fields, own_columns, from_west, from_east, low_damp, high_damp, rows, put):
    lane = lane_ids()
    sublane = lax.broadcasted_iota(jnp.int32, (8, LANES), 0)
    for j in range(5):
        low_damp[8 * j : 8 * j + 8, :] = turn(from_west[3, EW - 1], BASE - 2 - 2 * j)
        high_damp[8 * j : 8 * j + 8, :] = turn(from_east[3, EW - 1], BASE + WIDE - 2 * j)
    sides = beside_rows(rows, lambda t: from_west[t, EW - 1], lambda t: from_east[t, EW - 1], lane)
    for row, west, east in sides:
        west = jnp.where(sublane == 2, jnp.broadcast_to(low_damp[row : row + 1, :], (8, LANES)), west)
        east = jnp.where(sublane == 2, jnp.broadcast_to(high_damp[row : row + 1, :], (8, LANES)), east)
        value = jnp.where(lane < BASE, west, own_columns[row])
        put(0, 4, row, jnp.where(lane < BASE + WIDE, value, east))

    def work(block, carry):
        for field in range(4):
            sides = beside_rows(
                rows,
                message_tiles(from_west, block, field),
                message_tiles(from_east, block, field),
                lane,
            )
            for row, west, east in sides:
                value = jnp.where(lane < BASE, west, own_fields[block, field, row])
                put(block, field, row, jnp.where(lane < BASE + WIDE, value, east))
        return carry

    lax.fori_loop(0, TILES, work, 0)


def row_message_kernel(parity, own_fields, own_columns, from_west, from_east, chip, link, low_damp, high_damp):
    def write(up, down):
        def put(block, field, row, value):
            if row < REACH:
                target, number = down, row
            else:
                target, number = up, row - (BY - REACH)
            if field == 4:
                target[number, NS - 1] = value
            elif field < 2:
                target[block, FIELD_AT[field] + number] = value
            elif row < REACH - 1:
                target[block, FIELD_AT[field] + number] = value
            elif row > BY - REACH:
                target[block, FIELD_AT[field] + number - 1] = value

        rows = (*range(REACH), *range(BY - REACH, BY))
        place_halos(own_fields, own_columns, from_west, from_east, low_damp, high_damp, rows, put)

    for message in (chip, link):
        message[TILES - 1, NS - 1] = jnp.zeros((8, LANES), jnp.float32)

    @pl.when(parity[0] == 0)
    def _():
        write(chip, link)

    @pl.when(parity[0] != 0)
    def _():
        write(link, chip)


def halo_kernel(own_fields, own_columns, from_west, from_east, fields, columns, low_damp, high_damp):
    def put(block, field, row, value):
        if field == 4:
            columns[row] = value
        else:
            fields[block, field, row] = value

    place_halos(own_fields, own_columns, from_west, from_east, low_damp, high_damp, range(BY), put)


def staggered(spans, phases):
    state = {}
    length = max(high - low + 1 for low, high in spans)
    ahead = min(AHEAD, length)
    for time in range(length + ahead * (len(phases) - 1)):
        for number in reversed(range(len(phases))):
            for span, (low, high) in enumerate(spans):
                row = low + time - number * ahead
                if low <= row <= high:
                    phases[number](span, row, state)


class Band:
    def __init__(self, low, high, read, write, eastward, northward, levels, part=0):
        self.low, self.high, self.read, self.write = low, high, read, write
        self.eastward, self.northward = eastward, northward
        self.levels, self.part = levels, 2 * part


def advance(bands, shared, scratch):
    depth_east, depth_north, mix = shared
    scaled, held = scratch

    def rise(band, n, row):
        read = bands[band].read
        return jnp.where(bands[band].levels < depth_north(row), read(n, row + 1) - read(n, row), 0.0)

    def look_east(band, row, state):
        for n in range(2):
            state[band, n, row] = turn(bands[band].read(n, row), LANES - 1)

    def step_east(band, row, state):
        wet = bands[band].levels < depth_east(row)
        for n in range(2):
            here, beside = bands[band].read(n, row), state[band, n, row]
            step = jnp.where(wet, beside - here, 0.0)
            state[band, n, row] = step, turn(step, 1)
            held[bands[band].part + n, row + REACH] = beside + here

    def scale(band, row, state):
        for n in range(2):
            step, back = state.pop((band, n, row))
            drop = state.pop((band, n)) if (band, n) in state else rise(band, n, row - 1)
            state[band, n] = rise(band, n, row)
            scaled[bands[band].part + n, row + REACH] = mix(row) * ((step - back) + (state[band, n] - drop))

    staggered([(b.low - 1, b.high + 1) for b in bands], (look_east, step_east, scale))

    def north_flow(band, n, row):
        read, northward = bands[band].read, bands[band].northward
        step = scaled[bands[band].part + n, row + 1 + REACH] - scaled[bands[band].part + n, row + REACH]
        both = (northward(row) + northward(row + 1)) * (read(n, row) + read(n, row + 1)) + step
        return jnp.where(bands[band].levels < depth_north(row), both, 0.0)

    def look_east_again(band, row, state):
        state[band, "flow", row] = turn(bands[band].eastward(row), LANES - 1)
        for n in range(2):
            state[band, n, row] = turn(scaled[bands[band].part + n, row + REACH], LANES - 1)

    def east_flow(band, row, state):
        wet = bands[band].levels < depth_east(row)
        flow = bands[band].eastward(row) + state.pop((band, "flow", row))
        for n in range(2):
            at = row + REACH
            both = flow * held[bands[band].part + n, at] + (state[band, n, row] - scaled[bands[band].part + n, at])
            both = jnp.where(wet, both, 0.0)
            state[band, n, row] = both, turn(both, 1)

    def change(band, row, state):
        for n in range(2):
            east, back = state.pop((band, n, row))
            south = state.pop((band, n)) if (band, n) in state else north_flow(band, n, row - 1)
            state[band, n] = north_flow(band, n, row)
            result = bands[band].read(n, row) - ((east - back) + (state[band, n] - south))
            bands[band].write(n, row, result)

    staggered([(b.low, b.high) for b in bands], (look_east_again, east_flow, change))


def level_ids(step):
    sublane = lax.broadcasted_iota(jnp.int32, (8, LANES), 0)
    last = step == TILES - 1
    twice = last & (sublane < 8 * TILES - LEVELS)
    numbers = sublane + jnp.where(last, LEVELS - 8, 8 * step)
    return jnp.where(twice, LEVELS, numbers).astype(jnp.float32)


def spread_columns(column, rows, depth, depth_east, depth_north, mix):
    last = None
    for row in rows:
        value = column(row)
        here = jnp.broadcast_to(value[0:1, :], (8, LANES))
        depth[row + REACH] = here
        depth_east[row + REACH] = jnp.minimum(here, turn(here, LANES - 1))
        mix[row + REACH] = mixing_rate * jnp.broadcast_to(value[1:2, :], (8, LANES))
        if last is not None:
            depth_north[row + REACH - 1] = jnp.minimum(here, last)
        last = here


def contribution(levels, depth, warm, salt):
    return jnp.where(levels < depth, warm - salt_weight * salt, 0.0)


def inner_kernel(
    fields, columns, halfway, moved, forcing,
    middle, depth, depth_east, depth_north, mix, scaled, held,
):
    step = pl.program_id(0)

    @pl.when(step == 0)
    def _():
        spread_columns(lambda row: columns[row], range(BY), depth, depth_east, depth_north, mix)
        forcing[...] = jnp.zeros_like(forcing)

    levels = level_ids(step)
    shared = (
        lambda row: depth_east[row + REACH],
        lambda row: depth_north[row + REACH],
        lambda row: mix[row + REACH],
    )

    def write_middle(n, row, value):
        middle[n, row] = value
        if row < 6:
            halfway[0, n, row - 2] = value
        if row >= 34:
            halfway[0, n, row - 30] = value

    def write_moved(n, row, value):
        moved[0, n, row - 4] = value

    def eastward(row):
        return fields[0, 2, row]

    def northward(row):
        return fields[0, 3, row]

    first = Band(2, 37, lambda n, row: fields[0, n, row], write_middle, eastward, northward, levels)
    second = Band(4, 35, lambda n, row: middle[n, row], write_moved, eastward, northward, levels)
    advance([first], shared, (scaled, held))
    advance([second], shared, (scaled, held))
    for row in range(4, 36):
        forcing[row] += contribution(
            levels, depth[row + REACH], moved[0, 0, row - 4], moved[0, 1, row - 4]
        )


def surface_operator(values, couple_east, couple_north, damping):
    east = couple_east * (values - turn(values, LANES - 1))
    north = couple_north * (values - pltpu.roll(values, SURFACE - 1, 0))
    return damping * values + ((east - turn(east, 1)) + (north - pltpu.roll(north, 1, 0)))


def outer_kernel(parity, low_fields, high_fields, columns, chip, link, chip_extra, link_extra, *others):
    @pl.when(parity[0] == 0)
    def _():
        outer_rows(low_fields, high_fields, columns, link, chip, link_extra, chip_extra, *others)

    @pl.when(parity[0] != 0)
    def _():
        outer_rows(low_fields, high_fields, columns, chip, link, chip_extra, link_extra, *others)


def outer_rows(
    low_fields, high_fields, columns, up, down, up_extra, down_extra, halfway, inner_forcing,
    moved, basis, moments,
    middle, beyond, depth, depth_east, depth_north, mix, scaled, held, forcing, surface, depths, dampings,
):
    step = pl.program_id(0)

    def column(row):
        if row < 0:
            return up_extra[row + REACH, 0]
        if row >= BY:
            return down_extra[row - BY, 0]
        return columns[row]

    rows = range(-REACH, BY + REACH)

    @pl.when(step == 0)
    def _():
        spread_columns(column, rows, depth, depth_east, depth_north, mix)
        forcing[...] = jnp.zeros_like(forcing)

    shared = (
        lambda row: depth_east[row + REACH],
        lambda row: depth_north[row + REACH],
        lambda row: mix[row + REACH],
    )
    first, second = [], []
    for part in range(PARTS):
        levels = level_ids(PARTS * step + part)

        def field(number, row, part=part):
            if row < 0:
                return up[part, FIELD_AT[number] + row + (REACH if number < 2 else REACH - 1)]
            if row >= BY:
                return down[part, FIELD_AT[number] + row - BY]
            return low_fields[part, number, row] if row < 10 else high_fields[part, number, row - 30]

        def read_middle(n, row, part=part):
            if 2 <= row < 6:
                return halfway[part, n, row - 2]
            if 34 <= row < 38:
                return halfway[part, n, row - 30]
            return middle[2 * part + n, row + REACH]

        def write_middle(n, row, value, part=part):
            middle[2 * part + n, row + REACH] = value

        def write_beyond(n, row, value, part=part):
            beyond[2 * part + n, row + REACH] = value
            if 0 <= row < 4:
                moved[part, n, row] = value
            if 36 <= row < BY:
                moved[part, n, row - 32] = value

        flows = (functools.partial(field, 2), functools.partial(field, 3), levels, part)
        first += [Band(low, high, field, write_middle, *flows) for low, high in ((-5, 1), (38, 44))]
        second += [Band(low, high, read_middle, write_beyond, *flows) for low, high in ((-3, 3), (36, 42))]
    advance(first, shared, (scaled, held))
    advance(second, shared, (scaled, held))
    for row in (*range(-3, 4), *range(36, 43)):
        at = row + REACH
        for part in range(PARTS):
            forcing[at] += contribution(
                second[2 * part].levels, depth[at], beyond[2 * part, at], beyond[2 * part + 1, at]
            )

    @pl.when(step == TILES // PARTS - 1)
    def _():
        surface[...] = jnp.zeros_like(surface)
        for row in range(-3, 43):
            part = inner_forcing[row] if 4 <= row < 36 else forcing[row + REACH]
            total = jnp.sum(part, axis=0, keepdims=True)
            surface[row + 8 : row + 9, :] = total * (1.0 / math.sqrt(LEVELS))
        depths[...] = jnp.zeros_like(depths)
        dampings[...] = jnp.zeros_like(dampings)
        for row in rows:
            value = column(row)
            depths[row + 8 : row + 9, :] = value[0:1, :]
            dampings[row + 8 : row + 9, :] = value[2:3, :]
        here = depths[...]
        couple_east = jnp.minimum(here, turn(here, LANES - 1)) * (1.0 / LEVELS)
        couple_north = jnp.minimum(here, pltpu.roll(here, SURFACE - 1, 0)) * (1.0 / LEVELS)
        diagonal = dampings[...]
        powers = [surface[...]]
        for _ in range(3):
            powers.append(surface_operator(powers[-1], couple_east, couple_north, diagonal))
        row_id = lax.broadcasted_iota(jnp.int32, (SURFACE, LANES), 0)
        lane_id = lax.broadcasted_iota(jnp.int32, (SURFACE, LANES), 1)
        own = (row_id >= 8) & (row_id < 8 + BY) & (lane_id >= BASE) & (lane_id < BASE + WIDE)
        moments[...] = jnp.zeros_like(moments)
        for k in range(6):
            product = jnp.where(own, powers[k // 2] * powers[(k + 1) // 2], 0.0)
            moments[k : k + 1, :] = jnp.sum(product, axis=0, keepdims=True)
        for k in range(3):
            basis[k] = turn(powers[k], LANES - BASE)[8 : 8 + BY, :]


def to_slots(numbers, start, rows, load, block_list, out, group, width, ahead):
    lane = lane_ids()
    swap = slot_swap(block_list)
    pieces = [numbers[i : i + width] for i in range(0, len(numbers), width)]

    def rotations(block, n, piece):
        cells = [c for t in piece for c in range(t * LANES, min((t + 1) * LANES, CELLS))]
        turned = {}
        for r in sorted({c // BX - p for c in cells for p in range(2)}):
            low, high = (min(max(row, rows[0]), rows[1]) for row in (r, r + 1))
            value = jnp.where(lane < BASE + BX, load(block, n, low), load(block, n, high))
            turned[r] = turn(value, BX * r - BASE)
        return turned

    def place(block, last, n, piece, turned):
        for number in piece:
            for position in range(2):
                slot = swap if position == 0 else 1 - swap
                first, end = number * LANES, min((number + 1) * LANES, CELLS)
                parts = []
                for row in range(first // BX, (end - 1) // BX + 1):
                    low = max(row * BX, first)
                    parts.append((low, min((row + 1) * BX, end) - low, turned[row - position]))
                value = merge(parts, lane)[:, 0 : end - first]
                if last:
                    rest = value[8 * TILES - LEVELS : 8]
                    out[slot, 8 * TILES - 8 : LEVELS, n, first - start : end - start] = rest
                else:
                    out[slot, pl.ds(8 * block, 8), n, first - start : end - start] = value

    def work(blocks):
        jobs = [(block, last, n, piece) for block, last in blocks for n in range(2) for piece in pieces]
        ready = [rotations(block, n, piece) for block, _, n, piece in jobs[:ahead]]
        for index, (block, last, n, piece) in enumerate(jobs):
            if index + ahead < len(jobs):
                later = jobs[index + ahead]
                ready.append(rotations(later[0], later[2], later[3]))
            place(block, last, n, piece, ready[index])
            ready[index] = None

    def body(index, carry):
        work([(group * index + i, False) for i in range(group)])
        return carry

    lax.fori_loop(0, TILES // group - 1, body, 0)
    work([(block, block == TILES - 1) for block in range(TILES - group, TILES)])


def inner_slots_kernel(block_list, moved, out, cells, semaphore):
    to_slots(tuple(range(2, 12)), 2 * LANES, (4, 35), lambda block, n, row: moved[block, n, row - 4], block_list, cells, *INNER_PLAN)
    copy = pltpu.make_async_copy(cells, out.at[:, :, :, 2 * LANES : 12 * LANES], semaphore)
    copy.start()
    copy.wait()


def outer_slots_kernel(numbers, block_list, moved, edges, inner, out, cells, semaphore):
    def load(block, n, row):
        if 4 <= row < 36:
            return moved[block, n, row - 4]
        return edges[block, n, row if row < 4 else row - 32]

    start, end = numbers[0] * LANES, min((numbers[-1] + 1) * LANES, CELLS)
    to_slots(numbers, start, (0, BY - 1), load, block_list, cells, *OUTER_PLAN)
    copy = pltpu.make_async_copy(cells, out.at[:, :, :, start:end], semaphore)
    copy.start()
    copy.wait()


def finish_kernel(first, second, third, fourth, basis, out):
    moments = (first[...] + second[...]) + (third[...] + fourth[...])
    totals = jnp.sum(moments, axis=1, keepdims=True)
    m = [totals[k : k + 1, :] for k in range(6)]
    low10 = m[2] / m[1]
    low20 = m[3] / m[1]
    pivot1 = m[3] - low10 * m[2]
    part21 = m[4] - low20 * m[2]
    low21 = part21 / pivot1
    pivot2 = m[5] - low20 * m[3] - low21 * part21
    y1 = m[1] - low10 * m[0]
    y2 = m[2] - low20 * m[0] - low21 * y1
    z2 = y2 / pivot2
    z1 = y1 / pivot1 - low21 * z2
    z0 = m[0] / m[1] - low10 * z1 - low20 * z2
    value = z0 * basis[0] + z1 * basis[1] + z2 * basis[2]
    out[...] = value[:, 0:WIDE]


def quad(values, axis, partner):
    count = lax.axis_size(axis)
    others = [
        lax.ppermute(values, axis, [(i, partner(i, turn)) for i in range(count)])
        for turn in range(1, 4)
    ]
    return [values, *others]


def quad_sum(values, axis, partner):
    four = quad(values, axis, partner)
    return (four[0] + four[1]) + (four[2] + four[3])


def terms_over_devices(values, beside):
    values = values + lax.ppermute(values, "gy", [(i, i ^ 1) for i in range(lax.axis_size("gy"))])
    values = quad_sum(values, "gy", lambda i, turn: i ^ (2 * turn))
    values, done = lax.optimization_barrier((values, beside[0]()))
    values = quad_sum(values, "gx", lambda i, turn: i ^ turn)
    values, done = lax.optimization_barrier((values, beside[1](done)))
    return quad(values, "gx", lambda i, turn: i ^ (4 * turn)), done


def held_in_vmem(arrays):
    return [pltpu.with_memory_space_constraint(a, pltpu.VMEM) for a in arrays]


def vmem(kind):
    return pltpu.VMEM(kind.shape, kind.dtype)


def whole(shape):
    return pl.BlockSpec(shape, lambda k: (0,) * len(shape))


def per_device(block_list, wet_levels, mixing, velocity, tracers, damping):
    f32 = jnp.float32
    slots, fields_each, levels, cells = tracers.shape
    params = pltpu.CompilerParams(
        dimension_semantics=("arbitrary",), vmem_limit_bytes=20 * 1024 * 1024
    )

    def tiles(*shape):
        zeros = (0,) * (len(shape) + 2)
        return (
            pl.BlockSpec((1, *shape, 8, LANES), lambda k: (k, *zeros)),
            jax.ShapeDtypeStruct((TILES, *shape, 8, LANES), f32),
        )

    _, rows_type = tiles(NS)
    _, columns_type = tiles(EW)
    rows_extra = pl.BlockSpec((TILES, 1, 8, LANES), lambda k: (0, NS - 1, 0, 0))
    in_vmem = pl.BlockSpec(memory_space=pltpu.VMEM)
    own_specs = [pl.BlockSpec(memory_space=pltpu.SMEM)] + [in_vmem] * 5
    own = (block_list, *held_in_vmem((wet_levels, mixing, damping, velocity, tracers)))
    whole_params = pltpu.CompilerParams(vmem_limit_bytes=10 * 1024 * 1024)

    east, west = pl.pallas_call(
        columns_kernel,
        in_specs=own_specs[:1] + [pl.BlockSpec(memory_space=pl.ANY)] * 3 + [in_vmem] * 2,
        out_specs=[in_vmem] * 2,
        out_shape=[vmem(columns_type)] * 2,
        scratch_shapes=[
            pltpu.VMEM((BY, LANES), f32),
            pltpu.VMEM(wet_levels.shape, jnp.int32),
            pltpu.VMEM(mixing.shape, f32),
            pltpu.VMEM(damping.shape, f32),
            pltpu.SemaphoreType.DMA((3,)),
        ],
        compiler_params=whole_params,
        name="pack_columns",
    )(block_list, wet_levels, mixing, damping, *own[4:])
    columns_total = lax.axis_size("gx")
    from_west = lax.ppermute(east, "gx", [(i, (i + 1) % columns_total) for i in range(columns_total)])
    from_east = lax.ppermute(west, "gx", [((i + 1) % columns_total, i) for i in range(columns_total)])

    fields_block, fields_type = tiles(4, BY)
    column_shape = (BY, 8, LANES)
    column_type = jax.ShapeDtypeStruct(column_shape, f32)
    own_strips = pl.pallas_call(
        strips_kernel,
        in_specs=own_specs,
        out_specs=[in_vmem] * 2,
        out_shape=[vmem(fields_type), vmem(column_type)],
        scratch_shapes=[pltpu.VMEM((BY, LANES), f32)],
        compiler_params=whole_params,
        cost_estimate=pl.CostEstimate(flops=30_000_000, bytes_accessed=9_000_000, transcendentals=0),
        name="strips",
    )(*own)
    with_halos = held_in_vmem((*own_strips, from_west, from_east))
    parity = (lax.axis_index("gy") & 1).astype(jnp.int32).reshape(1)
    chip, link = pl.pallas_call(
        row_message_kernel,
        in_specs=[pl.BlockSpec(memory_space=pltpu.SMEM)] + [in_vmem] * 4,
        out_specs=[in_vmem] * 2,
        out_shape=[vmem(rows_type)] * 2,
        scratch_shapes=[pltpu.VMEM((BY, LANES), f32)] * 2,
        compiler_params=whole_params,
        name="row_message",
    )(parity, *with_halos)
    fields, columns = pl.pallas_call(
        halo_kernel,
        in_specs=[in_vmem] * 4,
        out_specs=[in_vmem] * 2,
        out_shape=[vmem(fields_type), vmem(column_type)],
        scratch_shapes=[pltpu.VMEM((BY, LANES), f32)] * 2,
        compiler_params=whole_params,
        cost_estimate=pl.CostEstimate(flops=30_000_000, bytes_accessed=9_000_000, transcendentals=0),
        name="halos",
    )(*with_halos)
    rows_total = lax.axis_size("gy")
    pairs = [(i, i ^ 1) for i in range(rows_total)]
    from_chip = lax.ppermute(chip, "gy", pairs)
    pairs = [pair for i in range(1, rows_total - 1, 2) for pair in ((i, i + 1), (i + 1, i))]
    from_link = lax.ppermute(link, "gy", pairs)

    row_store = pltpu.VMEM((ROWS, 8, LANES), f32)
    pair_store = pltpu.VMEM((2, ROWS, 8, LANES), f32)
    halfway_block, halfway_type = tiles(2, 8)
    moved_block, moved_type = tiles(2, 32)
    halfway, moved, forcing = pl.pallas_call(
        inner_kernel,
        grid=(TILES,),
        in_specs=[fields_block, whole(column_shape)],
        out_specs=[halfway_block, moved_block, whole(column_shape)],
        out_shape=[halfway_type, moved_type, jax.ShapeDtypeStruct(column_shape, f32)],
        scratch_shapes=[pair_store] + [row_store] * 4 + [pair_store] * 2,
        compiler_params=params,
        cost_estimate=pl.CostEstimate(flops=60_000_000, bytes_accessed=10_000_000, transcendentals=0),
        name="inner_rows",
    )(fields, columns)

    slots_type = jax.ShapeDtypeStruct((slots, levels, fields_each, cells), f32)
    inner_slots = pl.pallas_call(
        inner_slots_kernel,
        in_specs=[pl.BlockSpec(memory_space=pltpu.SMEM), in_vmem],
        out_specs=pl.BlockSpec(memory_space=pl.ANY),
        out_shape=slots_type,
        scratch_shapes=[
            pltpu.VMEM((slots, levels, fields_each, 10 * LANES), f32),
            pltpu.SemaphoreType.DMA,
        ],
        compiler_params=whole_params,
        cost_estimate=pl.CostEstimate(flops=20_000_000, bytes_accessed=6_000_000, transcendentals=0),
        name="inner_slots",
    )(block_list, moved)
    inner_slots, forcing = lax.optimization_barrier((inner_slots, forcing))

    low_block = pl.BlockSpec((PARTS, 4, 10, 8, LANES), lambda k: (k, 0, 0, 0, 0))
    high_block = pl.BlockSpec((PARTS, 4, 10, 8, LANES), lambda k: (k, 0, 3, 0, 0))
    part_rows = pl.BlockSpec((PARTS, NS, 8, LANES), lambda k: (k, 0, 0, 0))
    part_halfway = pl.BlockSpec((PARTS, 2, 8, 8, LANES), lambda k: (k, 0, 0, 0, 0))
    parts_store = pltpu.VMEM((2 * PARTS, ROWS, 8, LANES), f32)
    edges, basis, moments = pl.pallas_call(
        outer_kernel,
        grid=(TILES // PARTS,),
        in_specs=[pl.BlockSpec(memory_space=pltpu.SMEM), low_block, high_block, whole(column_shape)]
        + [part_rows, part_rows]
        + [rows_extra, rows_extra, part_halfway, whole(column_shape)],
        out_specs=[part_halfway, whole((3, BY, LANES)), whole((8, LANES))],
        out_shape=[
            halfway_type,
            jax.ShapeDtypeStruct((3, BY, LANES), f32),
            jax.ShapeDtypeStruct((8, LANES), f32),
        ],
        scratch_shapes=[parts_store] * 2
        + [row_store] * 4
        + [parts_store] * 2
        + [row_store]
        + [pltpu.VMEM((SURFACE, LANES), f32)] * 3,
        compiler_params=params,
        name="outer_rows",
    )(parity, fields, fields, columns, from_chip, from_link, from_chip, from_link, halfway, forcing)

    def outer_slots(numbers, before):
        width = min((numbers[-1] + 1) * LANES, cells) - numbers[0] * LANES
        return pl.pallas_call(
            functools.partial(outer_slots_kernel, numbers),
            in_specs=[pl.BlockSpec(memory_space=pltpu.SMEM), in_vmem, in_vmem]
            + [pl.BlockSpec(memory_space=pl.ANY)],
            out_specs=pl.BlockSpec(memory_space=pl.ANY),
            out_shape=slots_type,
            scratch_shapes=[
                pltpu.VMEM((slots, levels, fields_each, width), f32),
                pltpu.SemaphoreType.DMA,
            ],
            input_output_aliases={3: 0},
            compiler_params=whole_params,
            cost_estimate=pl.CostEstimate(flops=2_000_000, bytes_accessed=2_000_000, transcendentals=0),
            name="outer_slots",
        )(block_list, moved, edges, before)

    beside = (lambda: outer_slots((0, 1), inner_slots), lambda before: outer_slots((12, 13, 14), before))
    moments, new_tracers = terms_over_devices(moments, beside)
    new_tracers = jnp.transpose(new_tracers, (0, 2, 1, 3))
    height = pl.pallas_call(
        finish_kernel,
        in_specs=[in_vmem] * 5,
        out_specs=in_vmem,
        out_shape=jax.ShapeDtypeStruct((BY, WIDE), f32),
        name="finish",
    )(*held_in_vmem((*moments, basis)))
    return (new_tracers, height)


def solution(mesh):
    return jax.shard_map(
        per_device,
        mesh=mesh,
        in_specs=(
            P(("gx", "gy")),
            P(("gx", "gy"), None),
            P(("gx", "gy"), None),
            P(("gx", "gy"), None, None, None),
            P(("gx", "gy"), None, None, None),
            P("gy", "gx"),
        ),
        out_specs=(P(("gx", "gy"), None, None, None), P("gy", "gx")),
        check_vma=False,
    )
```

```python
import functools
import math

import jax
import jax.numpy as jnp
from jax import lax
from jax.experimental import pallas as pl
from jax.experimental.pallas import tpu as pltpu
from jax.sharding import PartitionSpec as P

BX = 45
BY = 40
CELLS = BX * BY
LEVELS = 62
LANES = 128
TILES = 8
REACH = 7
ROWS = BY + 2 * REACH
PARTS = 2
INNER_PLAN = (2, 5, 2)
OUTER_PLAN = (4, 3, 4)
AHEAD = 40
BASE = 8
WIDE = 2 * BX
NS = 27
FIELD_AT = (0, 7, 14, 20)
EW = 11
SHARED = 16
SURFACE = 56

advect_rate = 0.25
mixing_rate = 0.015
salt_weight = 0.8


def lane_ids():
    return lax.broadcasted_iota(jnp.int32, (8, LANES), 1)


def merge(parts, lane):
    flat = []
    for low, width, value in parts:
        low %= LANES
        if low + width > LANES:
            flat.append((low, value))
            flat.append((0, value))
        else:
            flat.append((low, value))
    flat.sort(key=lambda part: part[0])
    result = flat[0][1]
    last = result
    for low, value in flat[1:]:
        if value is last:
            continue
        result = jnp.where(lane >= low, value, result)
        last = value
    return result


def turn(value, shift):
    shift %= LANES
    return pltpu.roll(value, shift, 1) if shift else value


class Source:
    def __init__(self, load):
        self.load = load
        self.kept = {}

    def tile(self, *key):
        if key not in self.kept:
            self.kept[key] = self.load(*key)
        return self.kept[key]

    def cells(self, position, start, width):
        parts = []
        at = start
        while at < start + width:
            number = at // LANES
            end = min(start + width, (number + 1) * LANES)
            parts.append((at, end - at, self.tile(position, number)))
            at = end
        return parts


def pack_columns(source, lane, group):
    rows = range(17 * group, min(17 * group + 17, BY))
    east = merge([c for r in rows for c in source.cells(1, BX * r + BX - REACH, REACH)], lane)
    west = merge([c for r in rows for c in source.cells(0, BX * r, REACH)], lane)
    return east, west


def strip_rows(source, lane):
    turned = {}

    def combined(r):
        if r not in turned:
            parts = source.cells(0, BX * r, BX) if r >= 0 else []
            if r + 1 < BY:
                parts += source.cells(1, BX * (r + 1), BX)
            turned[r] = turn(merge(parts, lane), BASE - BX * r)
        return turned[r]

    for r in range(-1, BY):
        combined(r)
    for row in range(BY):
        yield row, jnp.where(lane < BASE + BX, combined(row), combined(row - 1))


def message_tiles(message, block, field):
    tiles = [message[block, 2 * field], message[block, 2 * field + 1]]
    last = message[block, 8 + field // 2]
    tiles.append(turn(last, LANES - SHARED) if field % 2 else last)
    return lambda number: tiles[number]


def beside_rows(rows, west, east, lane):
    turned = {}

    def combined(r):
        if r not in turned:
            low, high = (BX * r - REACH) % LANES, BX * (r + 2) % LANES
            if not 0 <= r - 1 < BY:
                value = east((r + 2) // 17)
            elif not 0 <= r + 2 < BY:
                value = west((r - 1) // 17)
            elif low < high:
                inside = lane < high if high + REACH <= LANES else (lane >= low) & (lane < high)
                value = jnp.where(inside, west((r - 1) // 17), east((r + 2) // 17))
            else:
                inside = lane < low if low + REACH <= LANES else (lane >= high) & (lane < low)
                value = jnp.where(inside, east((r + 2) // 17), west((r - 1) // 17))
            turned[r] = turn(value, BASE - BX * r)
        return turned[r]

    for r in sorted({row + 1 for row in rows} | {row - 2 for row in rows}):
        combined(r)
    for row in rows:
        yield row, combined(row + 1), combined(row - 2)


def slot_swap(block_list):
    first = block_list[0]
    return jnp.where(first >= 0, first & 1, 1 - (block_list[1] & 1))


def over_level_blocks(work):
    def body(block, carry):
        work(block, pl.ds(pl.multiple_of(8 * block, 8), 8))
        return carry

    lax.fori_loop(0, TILES - 1, body, 0)
    work(TILES - 1, pl.ds(LEVELS - 8, 8))


def field_loader(ref, which, levels, swap):
    def load(position, number):
        slot = swap if position == 0 else 1 - swap
        if number < 14:
            return ref[slot, which, levels, number * LANES : (number + 1) * LANES]
        return turn(ref[slot, which, levels, CELLS - LANES : CELLS], CELLS % LANES)

    return load


def column_loader(wet_levels, mixing, swap):
    def load(position, number):
        slot = swap if position == 0 else 1 - swap
        low = number * LANES if number < 14 else CELLS - LANES
        both = wet_levels[:, low : low + LANES].astype(jnp.float32)
        depth = jnp.where(slot == 0, both[0:1, :], both[1:2, :])
        both = mixing[:, low : low + LANES]
        mix = jnp.where(slot == 0, both[0:1, :], both[1:2, :])
        sublane = lax.broadcasted_iota(jnp.int32, (8, LANES), 0)
        value = jnp.where(
            sublane == 0, jnp.broadcast_to(depth, (8, LANES)), jnp.broadcast_to(mix, (8, LANES))
        )
        return value if number < 14 else turn(value, CELLS % LANES)

    return load


def columns_kernel(
    block_list, wet_levels_far, mixing_far, damping_far, velocity, tracers,
    east, west, padded, wet_levels, mixing, damping, semaphores,
):
    lane = lane_ids()
    swap = slot_swap(block_list)
    sides = (east, west)
    copies = [
        pltpu.make_async_copy(far, near, semaphores.at[number])
        for number, (far, near) in enumerate(
            ((wet_levels_far, wet_levels), (mixing_far, mixing), (damping_far, damping))
        )
    ]
    for copy in copies:
        copy.start()

    def work(block, levels):
        sources = [Source(field_loader(ref, n, levels, swap)) for ref in (tracers, velocity) for n in range(2)]
        scales = (1.0, 1.0, 0.25 * advect_rate, 0.25 * advect_rate)
        lasts = [pack_columns(source, lane, 2) for source in sources]
        lasts = [[tile * scale for tile in both] for both, scale in zip(lasts, scales)]
        lasts = [[turn(tile, SHARED * (field % 2)) for tile in both] for field, both in enumerate(lasts)]
        for field, source in enumerate(sources):
            for number in range(2):
                for message, tile in zip(sides, pack_columns(source, lane, number)):
                    message[block, 2 * field + number] = tile * scales[field]
        for pair in range(2):
            for side, message in enumerate(sides):
                first = BX - REACH if side == 0 else 0
                lows = [BX * row + first for row in range(34, BY)]
                one, two = lasts[2 * pair][side], lasts[2 * pair + 1][side]
                parts = [(low, REACH, one) for low in lows] + [(low + SHARED, REACH, two) for low in lows]
                message[block, 8 + pair] = merge(parts, lane)

    over_level_blocks(work)
    for copy in copies:
        copy.wait()
    source = Source(column_loader(wet_levels, mixing, swap))
    extras = [pack_columns(source, lane, number) for number in range(3)]
    padded[...] = jnp.zeros_like(padded)
    padded[:, 0:WIDE] = damping[...]
    tiles = [padded[8 * j : 8 * j + 8, :] for j in range(5)]
    extras.append(
        (
            merge([(2 * j, 2, turn(t, 2 * j - WIDE + 2)) for j, t in enumerate(tiles)], lane),
            merge([(2 * j, 2, turn(t, 2 * j)) for j, t in enumerate(tiles)], lane),
        )
    )
    for block in range(TILES):
        for side, message in enumerate(sides):
            message[block, EW - 1] = extras[min(block, 3)][side]


def strips_kernel(block_list, wet_levels, mixing, damping, velocity, tracers, fields, columns, padded):
    lane = lane_ids()
    swap = slot_swap(block_list)
    padded[...] = jnp.zeros_like(padded)
    padded[:, 0:WIDE] = damping[...]
    for j in range(5):
        padded[8 * j : 8 * j + 8, :] = turn(padded[8 * j : 8 * j + 8, :], BASE)
    sublane = lax.broadcasted_iota(jnp.int32, (8, LANES), 0)
    for row, value in strip_rows(Source(column_loader(wet_levels, mixing, swap)), lane):
        damp = jnp.broadcast_to(padded[row : row + 1, :], (8, LANES))
        columns[row] = jnp.where(sublane == 2, damp, value)

    def work(block, levels):
        for field in range(4):
            ref = tracers if field < 2 else velocity
            for row, value in strip_rows(Source(field_loader(ref, field % 2, levels, swap)), lane):
                fields[block, field, row] = value if field < 2 else (0.25 * advect_rate) * value

    over_level_blocks(work)


def place_halos(own_fields, own_columns, from_west, from_east, low_damp, high_damp, rows, put):
    lane = lane_ids()
    sublane = lax.broadcasted_iota(jnp.int32, (8, LANES), 0)
    for j in range(5):
        low_damp[8 * j : 8 * j + 8, :] = turn(from_west[3, EW - 1], BASE - 2 - 2 * j)
        high_damp[8 * j : 8 * j + 8, :] = turn(from_east[3, EW - 1], BASE + WIDE - 2 * j)
    sides = beside_rows(rows, lambda t: from_west[t, EW - 1], lambda t: from_east[t, EW - 1], lane)
    for row, west, east in sides:
        west = jnp.where(sublane == 2, jnp.broadcast_to(low_damp[row : row + 1, :], (8, LANES)), west)
        east = jnp.where(sublane == 2, jnp.broadcast_to(high_damp[row : row + 1, :], (8, LANES)), east)
        value = jnp.where(lane < BASE, west, own_columns[row])
        put(0, 4, row, jnp.where(lane < BASE + WIDE, value, east))

    def work(block, carry):
        for field in range(4):
            sides = beside_rows(
                rows,
                message_tiles(from_west, block, field),
                message_tiles(from_east, block, field),
                lane,
            )
            for row, west, east in sides:
                value = jnp.where(lane < BASE, west, own_fields[block, field, row])
                put(block, field, row, jnp.where(lane < BASE + WIDE, value, east))
        return carry

    lax.fori_loop(0, TILES, work, 0)


def row_message_kernel(parity, own_fields, own_columns, from_west, from_east, chip, link, low_damp, high_damp):
    def write(up, down):
        def put(block, field, row, value):
            if row < REACH:
                target, number = down, row
            else:
                target, number = up, row - (BY - REACH)
            if field == 4:
                target[number, NS - 1] = value
            elif field < 2:
                target[block, FIELD_AT[field] + number] = value
            elif row < REACH - 1:
                target[block, FIELD_AT[field] + number] = value
            elif row > BY - REACH:
                target[block, FIELD_AT[field] + number - 1] = value

        rows = (*range(REACH), *range(BY - REACH, BY))
        place_halos(own_fields, own_columns, from_west, from_east, low_damp, high_damp, rows, put)

    for message in (chip, link):
        message[TILES - 1, NS - 1] = jnp.zeros((8, LANES), jnp.float32)

    @pl.when(parity[0] == 0)
    def _():
        write(chip, link)

    @pl.when(parity[0] != 0)
    def _():
        write(link, chip)


def halo_kernel(own_fields, own_columns, from_west, from_east, fields, columns, low_damp, high_damp):
    def put(block, field, row, value):
        if field == 4:
            columns[row] = value
        else:
            fields[block, field, row] = value

    place_halos(own_fields, own_columns, from_west, from_east, low_damp, high_damp, range(BY), put)


def staggered(spans, phases):
    state = {}
    length = max(high - low + 1 for low, high in spans)
    ahead = min(AHEAD, length)
    for time in range(length + ahead * (len(phases) - 1)):
        for number in reversed(range(len(phases))):
            for span, (low, high) in enumerate(spans):
                row = low + time - number * ahead
                if low <= row <= high:
                    phases[number](span, row, state)


class Band:
    def __init__(self, low, high, read, write, eastward, northward, levels, part=0):
        self.low, self.high, self.read, self.write = low, high, read, write
        self.eastward, self.northward = eastward, northward
        self.levels, self.part = levels, 2 * part


def advance(bands, shared, scratch):
    depth_east, depth_north, mix = shared
    scaled, held = scratch

    def rise(band, n, row):
        read = bands[band].read
        return jnp.where(bands[band].levels < depth_north(row), read(n, row + 1) - read(n, row), 0.0)

    def look_east(band, row, state):
        for n in range(2):
            state[band, n, row] = turn(bands[band].read(n, row), LANES - 1)

    def step_east(band, row, state):
        wet = bands[band].levels < depth_east(row)
        for n in range(2):
            here, beside = bands[band].read(n, row), state[band, n, row]
            step = jnp.where(wet, beside - here, 0.0)
            state[band, n, row] = step, turn(step, 1)
            held[bands[band].part + n, row + REACH] = beside + here

    def scale(band, row, state):
        for n in range(2):
            step, back = state.pop((band, n, row))
            drop = state.pop((band, n)) if (band, n) in state else rise(band, n, row - 1)
            state[band, n] = rise(band, n, row)
            scaled[bands[band].part + n, row + REACH] = mix(row) * ((step - back) + (state[band, n] - drop))

    staggered([(b.low - 1, b.high + 1) for b in bands], (look_east, step_east, scale))

    def north_flow(band, n, row):
        read, northward = bands[band].read, bands[band].northward
        step = scaled[bands[band].part + n, row + 1 + REACH] - scaled[bands[band].part + n, row + REACH]
        both = (northward(row) + northward(row + 1)) * (read(n, row) + read(n, row + 1)) + step
        return jnp.where(bands[band].levels < depth_north(row), both, 0.0)

    def look_east_again(band, row, state):
        state[band, "flow", row] = turn(bands[band].eastward(row), LANES - 1)
        for n in range(2):
            state[band, n, row] = turn(scaled[bands[band].part + n, row + REACH], LANES - 1)

    def east_flow(band, row, state):
        wet = bands[band].levels < depth_east(row)
        flow = bands[band].eastward(row) + state.pop((band, "flow", row))
        for n in range(2):
            at = row + REACH
            both = flow * held[bands[band].part + n, at] + (state[band, n, row] - scaled[bands[band].part + n, at])
            both = jnp.where(wet, both, 0.0)
            state[band, n, row] = both, turn(both, 1)

    def change(band, row, state):
        for n in range(2):
            east, back = state.pop((band, n, row))
            south = state.pop((band, n)) if (band, n) in state else north_flow(band, n, row - 1)
            state[band, n] = north_flow(band, n, row)
            result = bands[band].read(n, row) - ((east - back) + (state[band, n] - south))
            bands[band].write(n, row, result)

    staggered([(b.low, b.high) for b in bands], (look_east_again, east_flow, change))


def level_ids(step):
    sublane = lax.broadcasted_iota(jnp.int32, (8, LANES), 0)
    last = step == TILES - 1
    twice = last & (sublane < 8 * TILES - LEVELS)
    numbers = sublane + jnp.where(last, LEVELS - 8, 8 * step)
    return jnp.where(twice, LEVELS, numbers).astype(jnp.float32)


def spread_columns(column, rows, depth, depth_east, depth_north, mix):
    last = None
    for row in rows:
        value = column(row)
        here = jnp.broadcast_to(value[0:1, :], (8, LANES))
        depth[row + REACH] = here
        depth_east[row + REACH] = jnp.minimum(here, turn(here, LANES - 1))
        mix[row + REACH] = mixing_rate * jnp.broadcast_to(value[1:2, :], (8, LANES))
        if last is not None:
            depth_north[row + REACH - 1] = jnp.minimum(here, last)
        last = here


def contribution(levels, depth, warm, salt):
    return jnp.where(levels < depth, warm - salt_weight * salt, 0.0)


def inner_kernel(
    fields, columns, halfway, moved, forcing,
    middle, depth, depth_east, depth_north, mix, scaled, held,
):
    step = pl.program_id(0)

    @pl.when(step == 0)
    def _():
        spread_columns(lambda row: columns[row], range(BY), depth, depth_east, depth_north, mix)
        forcing[...] = jnp.zeros_like(forcing)

    levels = level_ids(step)
    shared = (
        lambda row: depth_east[row + REACH],
        lambda row: depth_north[row + REACH],
        lambda row: mix[row + REACH],
    )

    def write_middle(n, row, value):
        middle[n, row] = value
        if row < 6:
            halfway[0, n, row - 2] = value
        if row >= 34:
            halfway[0, n, row - 30] = value

    def write_moved(n, row, value):
        moved[0, n, row - 4] = value

    def eastward(row):
        return fields[0, 2, row]

    def northward(row):
        return fields[0, 3, row]

    first = Band(2, 37, lambda n, row: fields[0, n, row], write_middle, eastward, northward, levels)
    second = Band(4, 35, lambda n, row: middle[n, row], write_moved, eastward, northward, levels)
    advance([first], shared, (scaled, held))
    advance([second], shared, (scaled, held))
    for row in range(4, 36):
        forcing[row] += contribution(
            levels, depth[row + REACH], moved[0, 0, row - 4], moved[0, 1, row - 4]
        )


def surface_operator(values, couple_east, couple_north, damping):
    east = couple_east * (values - turn(values, LANES - 1))
    north = couple_north * (values - pltpu.roll(values, SURFACE - 1, 0))
    return damping * values + ((east - turn(east, 1)) + (north - pltpu.roll(north, 1, 0)))


def outer_kernel(parity, low_fields, high_fields, columns, chip, link, chip_extra, link_extra, *others):
    @pl.when(parity[0] == 0)
    def _():
        outer_rows(low_fields, high_fields, columns, link, chip, link_extra, chip_extra, *others)

    @pl.when(parity[0] != 0)
    def _():
        outer_rows(low_fields, high_fields, columns, chip, link, chip_extra, link_extra, *others)


def outer_rows(
    low_fields, high_fields, columns, up, down, up_extra, down_extra, halfway, inner_forcing,
    moved, basis, moments,
    middle, beyond, depth, depth_east, depth_north, mix, scaled, held, forcing, surface, depths, dampings,
):
    step = pl.program_id(0)

    def column(row):
        if row < 0:
            return up_extra[row + REACH, 0]
        if row >= BY:
            return down_extra[row - BY, 0]
        return columns[row]

    rows = range(-REACH, BY + REACH)

    @pl.when(step == 0)
    def _():
        spread_columns(column, rows, depth, depth_east, depth_north, mix)
        forcing[...] = jnp.zeros_like(forcing)

    shared = (
        lambda row: depth_east[row + REACH],
        lambda row: depth_north[row + REACH],
        lambda row: mix[row + REACH],
    )
    first, second = [], []
    for part in range(PARTS):
        levels = level_ids(PARTS * step + part)

        def field(number, row, part=part):
            if row < 0:
                return up[part, FIELD_AT[number] + row + (REACH if number < 2 else REACH - 1)]
            if row >= BY:
                return down[part, FIELD_AT[number] + row - BY]
            return low_fields[part, number, row] if row < 10 else high_fields[part, number, row - 30]

        def read_middle(n, row, part=part):
            if 2 <= row < 6:
                return halfway[part, n, row - 2]
            if 34 <= row < 38:
                return halfway[part, n, row - 30]
            return middle[2 * part + n, row + REACH]

        def write_middle(n, row, value, part=part):
            middle[2 * part + n, row + REACH] = value

        def write_beyond(n, row, value, part=part):
            beyond[2 * part + n, row + REACH] = value
            if 0 <= row < 4:
                moved[part, n, row] = value
            if 36 <= row < BY:
                moved[part, n, row - 32] = value

        flows = (functools.partial(field, 2), functools.partial(field, 3), levels, part)
        first += [Band(low, high, field, write_middle, *flows) for low, high in ((-5, 1), (38, 44))]
        second += [Band(low, high, read_middle, write_beyond, *flows) for low, high in ((-3, 3), (36, 42))]
    advance(first, shared, (scaled, held))
    advance(second, shared, (scaled, held))
    for row in (*range(-3, 4), *range(36, 43)):
        at = row + REACH
        for part in range(PARTS):
            forcing[at] += contribution(
                second[2 * part].levels, depth[at], beyond[2 * part, at], beyond[2 * part + 1, at]
            )

    @pl.when(step == TILES // PARTS - 1)
    def _():
        surface[...] = jnp.zeros_like(surface)
        for row in range(-3, 43):
            part = inner_forcing[row] if 4 <= row < 36 else forcing[row + REACH]
            total = jnp.sum(part, axis=0, keepdims=True)
            surface[row + 8 : row + 9, :] = total * (1.0 / math.sqrt(LEVELS))
        depths[...] = jnp.zeros_like(depths)
        dampings[...] = jnp.zeros_like(dampings)
        for row in rows:
            value = column(row)
            depths[row + 8 : row + 9, :] = value[0:1, :]
            dampings[row + 8 : row + 9, :] = value[2:3, :]
        here = depths[...]
        couple_east = jnp.minimum(here, turn(here, LANES - 1)) * (1.0 / LEVELS)
        couple_north = jnp.minimum(here, pltpu.roll(here, SURFACE - 1, 0)) * (1.0 / LEVELS)
        diagonal = dampings[...]
        powers = [surface[...]]
        for _ in range(3):
            powers.append(surface_operator(powers[-1], couple_east, couple_north, diagonal))
        row_id = lax.broadcasted_iota(jnp.int32, (SURFACE, LANES), 0)
        lane_id = lax.broadcasted_iota(jnp.int32, (SURFACE, LANES), 1)
        own = (row_id >= 8) & (row_id < 8 + BY) & (lane_id >= BASE) & (lane_id < BASE + WIDE)
        moments[...] = jnp.zeros_like(moments)
        for k in range(6):
            product = jnp.where(own, powers[k // 2] * powers[(k + 1) // 2], 0.0)
            moments[k : k + 1, :] = jnp.sum(product, axis=0, keepdims=True)
        for k in range(3):
            basis[k] = turn(powers[k], LANES - BASE)[8 : 8 + BY, :]


def to_slots(numbers, start, rows, load, block_list, out, group, width, ahead):
    lane = lane_ids()
    swap = slot_swap(block_list)
    pieces = [numbers[i : i + width] for i in range(0, len(numbers), width)]

    def rotations(block, n, piece):
        cells = [c for t in piece for c in range(t * LANES, min((t + 1) * LANES, CELLS))]
        turned = {}
        for r in sorted({c // BX - p for c in cells for p in range(2)}):
            low, high = (min(max(row, rows[0]), rows[1]) for row in (r, r + 1))
            value = jnp.where(lane < BASE + BX, load(block, n, low), load(block, n, high))
            turned[r] = turn(value, BX * r - BASE)
        return turned

    def place(block, last, n, piece, turned):
        for number in piece:
            for position in range(2):
                slot = swap if position == 0 else 1 - swap
                first, end = number * LANES, min((number + 1) * LANES, CELLS)
                parts = []
                for row in range(first // BX, (end - 1) // BX + 1):
                    low = max(row * BX, first)
                    parts.append((low, min((row + 1) * BX, end) - low, turned[row - position]))
                value = merge(parts, lane)[:, 0 : end - first]
                if last:
                    rest = value[8 * TILES - LEVELS : 8]
                    out[slot, 8 * TILES - 8 : LEVELS, n, first - start : end - start] = rest
                else:
                    out[slot, pl.ds(8 * block, 8), n, first - start : end - start] = value

    def work(blocks):
        jobs = [(block, last, n, piece) for block, last in blocks for n in range(2) for piece in pieces]
        ready = [rotations(block, n, piece) for block, _, n, piece in jobs[:ahead]]
        for index, (block, last, n, piece) in enumerate(jobs):
            if index + ahead < len(jobs):
                later = jobs[index + ahead]
                ready.append(rotations(later[0], later[2], later[3]))
            place(block, last, n, piece, ready[index])
            ready[index] = None

    def body(index, carry):
        work([(group * index + i, False) for i in range(group)])
        return carry

    lax.fori_loop(0, TILES // group - 1, body, 0)
    work([(block, block == TILES - 1) for block in range(TILES - group, TILES)])


def inner_slots_kernel(block_list, moved, out, cells, semaphore):
    to_slots(tuple(range(2, 12)), 2 * LANES, (4, 35), lambda block, n, row: moved[block, n, row - 4], block_list, cells, *INNER_PLAN)
    copy = pltpu.make_async_copy(cells, out.at[:, :, :, 2 * LANES : 12 * LANES], semaphore)
    copy.start()
    copy.wait()


def outer_slots_kernel(numbers, block_list, moved, edges, inner, out, cells, semaphore):
    def load(block, n, row):
        if 4 <= row < 36:
            return moved[block, n, row - 4]
        return edges[block, n, row if row < 4 else row - 32]

    start, end = numbers[0] * LANES, min((numbers[-1] + 1) * LANES, CELLS)
    to_slots(numbers, start, (0, BY - 1), load, block_list, cells, *OUTER_PLAN)
    copy = pltpu.make_async_copy(cells, out.at[:, :, :, start:end], semaphore)
    copy.start()
    copy.wait()


def finish_kernel(first, second, third, fourth, basis, out):
    moments = (first[...] + second[...]) + (third[...] + fourth[...])
    totals = jnp.sum(moments, axis=1, keepdims=True)
    m = [totals[k : k + 1, :] for k in range(6)]
    low10 = m[2] / m[1]
    low20 = m[3] / m[1]
    pivot1 = m[3] - low10 * m[2]
    part21 = m[4] - low20 * m[2]
    low21 = part21 / pivot1
    pivot2 = m[5] - low20 * m[3] - low21 * part21
    y1 = m[1] - low10 * m[0]
    y2 = m[2] - low20 * m[0] - low21 * y1
    z2 = y2 / pivot2
    z1 = y1 / pivot1 - low21 * z2
    z0 = m[0] / m[1] - low10 * z1 - low20 * z2
    value = z0 * basis[0] + z1 * basis[1] + z2 * basis[2]
    out[...] = value[:, 0:WIDE]


def quad(values, axis, partner):
    count = lax.axis_size(axis)
    others = [
        lax.ppermute(values, axis, [(i, partner(i, turn)) for i in range(count)])
        for turn in range(1, 4)
    ]
    return [values, *others]


def quad_sum(values, axis, partner):
    four = quad(values, axis, partner)
    return (four[0] + four[1]) + (four[2] + four[3])


def terms_over_devices(values, beside):
    values = values + lax.ppermute(values, "gy", [(i, i ^ 1) for i in range(lax.axis_size("gy"))])
    values = quad_sum(values, "gy", lambda i, turn: i ^ (2 * turn))
    values, done = lax.optimization_barrier((values, beside[0]()))
    values = quad_sum(values, "gx", lambda i, turn: i ^ turn)
    values, done = lax.optimization_barrier((values, beside[1](done)))
    return quad(values, "gx", lambda i, turn: i ^ (4 * turn)), done


def held_in_vmem(arrays):
    return [pltpu.with_memory_space_constraint(a, pltpu.VMEM) for a in arrays]


def vmem(kind):
    return pltpu.VMEM(kind.shape, kind.dtype)


def whole(shape):
    return pl.BlockSpec(shape, lambda k: (0,) * len(shape))


def per_device(block_list, wet_levels, mixing, velocity, tracers, damping):
    f32 = jnp.float32
    slots, fields_each, levels, cells = tracers.shape
    params = pltpu.CompilerParams(
        dimension_semantics=("arbitrary",), vmem_limit_bytes=20 * 1024 * 1024
    )

    def tiles(*shape):
        zeros = (0,) * (len(shape) + 2)
        return (
            pl.BlockSpec((1, *shape, 8, LANES), lambda k: (k, *zeros)),
            jax.ShapeDtypeStruct((TILES, *shape, 8, LANES), f32),
        )

    _, rows_type = tiles(NS)
    _, columns_type = tiles(EW)
    rows_extra = pl.BlockSpec((TILES, 1, 8, LANES), lambda k: (0, NS - 1, 0, 0))
    in_vmem = pl.BlockSpec(memory_space=pltpu.VMEM)
    own_specs = [pl.BlockSpec(memory_space=pltpu.SMEM)] + [in_vmem] * 5
    own = (block_list, *held_in_vmem((wet_levels, mixing, damping, velocity, tracers)))
    whole_params = pltpu.CompilerParams(vmem_limit_bytes=10 * 1024 * 1024)

    east, west = pl.pallas_call(
        columns_kernel,
        in_specs=own_specs[:1] + [pl.BlockSpec(memory_space=pl.ANY)] * 3 + [in_vmem] * 2,
        out_specs=[in_vmem] * 2,
        out_shape=[vmem(columns_type)] * 2,
        scratch_shapes=[
            pltpu.VMEM((BY, LANES), f32),
            pltpu.VMEM(wet_levels.shape, jnp.int32),
            pltpu.VMEM(mixing.shape, f32),
            pltpu.VMEM(damping.shape, f32),
            pltpu.SemaphoreType.DMA((3,)),
        ],
        compiler_params=whole_params,
        name="pack_columns",
    )(block_list, wet_levels, mixing, damping, *own[4:])
    columns_total = lax.axis_size("gx")
    from_west = lax.ppermute(east, "gx", [(i, (i + 1) % columns_total) for i in range(columns_total)])
    from_east = lax.ppermute(west, "gx", [((i + 1) % columns_total, i) for i in range(columns_total)])

    fields_block, fields_type = tiles(4, BY)
    column_shape = (BY, 8, LANES)
    column_type = jax.ShapeDtypeStruct(column_shape, f32)
    own_strips = pl.pallas_call(
        strips_kernel,
        in_specs=own_specs,
        out_specs=[in_vmem] * 2,
        out_shape=[vmem(fields_type), vmem(column_type)],
        scratch_shapes=[pltpu.VMEM((BY, LANES), f32)],
        compiler_params=whole_params,
        cost_estimate=pl.CostEstimate(flops=30_000_000, bytes_accessed=9_000_000, transcendentals=0),
        name="strips",
    )(*own)
    with_halos = held_in_vmem((*own_strips, from_west, from_east))
    parity = (lax.axis_index("gy") & 1).astype(jnp.int32).reshape(1)
    chip, link = pl.pallas_call(
        row_message_kernel,
        in_specs=[pl.BlockSpec(memory_space=pltpu.SMEM)] + [in_vmem] * 4,
        out_specs=[in_vmem] * 2,
        out_shape=[vmem(rows_type)] * 2,
        scratch_shapes=[pltpu.VMEM((BY, LANES), f32)] * 2,
        compiler_params=whole_params,
        name="row_message",
    )(parity, *with_halos)
    fields, columns = pl.pallas_call(
        halo_kernel,
        in_specs=[in_vmem] * 4,
        out_specs=[in_vmem] * 2,
        out_shape=[vmem(fields_type), vmem(column_type)],
        scratch_shapes=[pltpu.VMEM((BY, LANES), f32)] * 2,
        compiler_params=whole_params,
        cost_estimate=pl.CostEstimate(flops=30_000_000, bytes_accessed=9_000_000, transcendentals=0),
        name="halos",
    )(*with_halos)
    rows_total = lax.axis_size("gy")
    pairs = [(i, i ^ 1) for i in range(rows_total)]
    from_chip = lax.ppermute(chip, "gy", pairs)
    pairs = [pair for i in range(1, rows_total - 1, 2) for pair in ((i, i + 1), (i + 1, i))]
    from_link = lax.ppermute(link, "gy", pairs)

    row_store = pltpu.VMEM((ROWS, 8, LANES), f32)
    pair_store = pltpu.VMEM((2, ROWS, 8, LANES), f32)
    halfway_block, halfway_type = tiles(2, 8)
    moved_block, moved_type = tiles(2, 32)
    halfway, moved, forcing = pl.pallas_call(
        inner_kernel,
        grid=(TILES,),
        in_specs=[fields_block, whole(column_shape)],
        out_specs=[halfway_block, moved_block, whole(column_shape)],
        out_shape=[halfway_type, moved_type, jax.ShapeDtypeStruct(column_shape, f32)],
        scratch_shapes=[pair_store] + [row_store] * 4 + [pair_store] * 2,
        compiler_params=params,
        cost_estimate=pl.CostEstimate(flops=60_000_000, bytes_accessed=10_000_000, transcendentals=0),
        name="inner_rows",
    )(fields, columns)

    slots_type = jax.ShapeDtypeStruct((slots, levels, fields_each, cells), f32)
    inner_slots = pl.pallas_call(
        inner_slots_kernel,
        in_specs=[pl.BlockSpec(memory_space=pltpu.SMEM), in_vmem],
        out_specs=pl.BlockSpec(memory_space=pl.ANY),
        out_shape=slots_type,
        scratch_shapes=[
            pltpu.VMEM((slots, levels, fields_each, 10 * LANES), f32),
            pltpu.SemaphoreType.DMA,
        ],
        compiler_params=whole_params,
        cost_estimate=pl.CostEstimate(flops=20_000_000, bytes_accessed=6_000_000, transcendentals=0),
        name="inner_slots",
    )(block_list, moved)
    inner_slots, forcing = lax.optimization_barrier((inner_slots, forcing))

    low_block = pl.BlockSpec((PARTS, 4, 10, 8, LANES), lambda k: (k, 0, 0, 0, 0))
    high_block = pl.BlockSpec((PARTS, 4, 10, 8, LANES), lambda k: (k, 0, 3, 0, 0))
    part_rows = pl.BlockSpec((PARTS, NS, 8, LANES), lambda k: (k, 0, 0, 0))
    part_halfway = pl.BlockSpec((PARTS, 2, 8, 8, LANES), lambda k: (k, 0, 0, 0, 0))
    parts_store = pltpu.VMEM((2 * PARTS, ROWS, 8, LANES), f32)
    edges, basis, moments = pl.pallas_call(
        outer_kernel,
        grid=(TILES // PARTS,),
        in_specs=[pl.BlockSpec(memory_space=pltpu.SMEM), low_block, high_block, whole(column_shape)]
        + [part_rows, part_rows]
        + [rows_extra, rows_extra, part_halfway, whole(column_shape)],
        out_specs=[part_halfway, whole((3, BY, LANES)), whole((8, LANES))],
        out_shape=[
            halfway_type,
            jax.ShapeDtypeStruct((3, BY, LANES), f32),
            jax.ShapeDtypeStruct((8, LANES), f32),
        ],
        scratch_shapes=[parts_store] * 2
        + [row_store] * 4
        + [parts_store] * 2
        + [row_store]
        + [pltpu.VMEM((SURFACE, LANES), f32)] * 3,
        compiler_params=params,
        name="outer_rows",
    )(parity, fields, fields, columns, from_chip, from_link, from_chip, from_link, halfway, forcing)

    def outer_slots(numbers, before):
        width = min((numbers[-1] + 1) * LANES, cells) - numbers[0] * LANES
        return pl.pallas_call(
            functools.partial(outer_slots_kernel, numbers),
            in_specs=[pl.BlockSpec(memory_space=pltpu.SMEM), in_vmem, in_vmem]
            + [pl.BlockSpec(memory_space=pl.ANY)],
            out_specs=pl.BlockSpec(memory_space=pl.ANY),
            out_shape=slots_type,
            scratch_shapes=[
                pltpu.VMEM((slots, levels, fields_each, width), f32),
                pltpu.SemaphoreType.DMA,
            ],
            input_output_aliases={3: 0},
            compiler_params=whole_params,
            cost_estimate=pl.CostEstimate(flops=2_000_000, bytes_accessed=2_000_000, transcendentals=0),
            name="outer_slots",
        )(block_list, moved, edges, before)

    beside = (lambda: outer_slots((0, 1), inner_slots), lambda before: outer_slots((12, 13, 14), before))
    moments, new_tracers = terms_over_devices(moments, beside)
    new_tracers = jnp.transpose(new_tracers, (0, 2, 1, 3))
    height = pl.pallas_call(
        finish_kernel,
        in_specs=[in_vmem] * 5,
        out_specs=in_vmem,
        out_shape=jax.ShapeDtypeStruct((BY, WIDE), f32),
        name="finish",
    )(*held_in_vmem((*moments, basis)))
    return (new_tracers, height)


def solution(mesh):
    return jax.shard_map(
        per_device,
        mesh=mesh,
        in_specs=(
            P(("gx", "gy")),
            P(("gx", "gy"), None),
            P(("gx", "gy"), None),
            P(("gx", "gy"), None, None, None),
            P(("gx", "gy"), None, None, None),
            P("gy", "gx"),
        ),
        out_specs=(P(("gx", "gy"), None, None, None), P("gy", "gx")),
        check_vma=False,
    )
```
